32 devices in a mesh: px: 8 (over z, y), py: 4 (over x, core).
Axes of the slice: x: 2, y: 2, z: 4, core: 2. Of those that a mesh axis runs over, the one named last changes fastest.
Arguments:
- point_channel_values: bfloat16 [4096, 64, 128], P(('px', 'py')), may hold values from -6 to 6
- point_offsets: bfloat16 [4096, 3, 128], P(('px', 'py')), may hold values from -1 to 17
- point_counts: int32 [4096], P(('px', 'py')), may hold values from 1 to 128
- block_bricks: int32 [4096, 4], P(('px', 'py')), may hold values from 0 to 16383, as said below
- spectral_weights: bfloat16 [2, 32, 32, 32, 64, 128], P(None, None, 'px', 'py'), may hold values from -0.5 to 0.5
- skip_weights: bfloat16 [2, 64, 64], replicated, may hold values from -0.75 to 0.75
- skip_bias: float32 [2, 64], replicated, may hold values from -3 to 3
Outputs:
- decoded: bfloat16 [4096, 64, 128], P(('px', 'py'))
The draws below stay inside these ranges and needn't reach their ends.
Inputs may be any that keep to these rules, and one draw needn't show every extreme that they name: `block_bricks`: the 4 bricks of a block are distinct and lie on one device. Among the 128 blocks of one device at most 8 have their bricks on any one device, and in every draw some device receives exactly 8 blocks from every device.
All inputs are finite; a program needn't handle non-finite values.
Results may differ from the reference program's by a relative error of at most 0.0075.
Values may be sent and summed in bfloat16 or wider, within the bound.
A program may use at most 256 MiB of HBM per device.

```python
import math
import jax
import jax.numpy as jnp
from jax import lax

CH = 64
MODES = 32
NX = 128
NY = 128
NZ = 128
LAYERS = 2
BLOCK = 128
HALO = 4
BLK_DEV = 128
CAPB = 8
NBLK = 4096
BY = 8
BZ = 8
BRK_DEV = 512
N_PX = 8
N_PY = 4
DEVICES = 32


def draw_block_bricks(key, part):
    hot_key, device_key = jax.random.split(key)
    hottest = jax.random.randint(hot_key, (), 0, DEVICES)

    def per_source(source_point):
        source_key = jax.random.fold_in(device_key, source_point)
        pick_key, shuffle_key, brick_key = jax.random.split(source_key, 3)
        chosen = jax.random.permutation(pick_key, (DEVICES - 1) * CAPB)[:BLK_DEV - CAPB]
        others = chosen // CAPB
        others = others + (others >= hottest).astype(others.dtype)
        owners = jnp.concatenate([jnp.full((CAPB,), hottest, jnp.int32), others.astype(jnp.int32)])
        owners = jax.random.permutation(shuffle_key, owners)
        home_bricks = jax.random.randint(brick_key, (BLK_DEV,), 0, BRK_DEV)
        return (owners, home_bricks)
    owners, home_bricks = jax.vmap(per_source)(jnp.arange(DEVICES, dtype=jnp.int32))
    first_coord = home_bricks // (BY * BZ)
    second_coord = home_bricks // BZ % BY
    third_coord = home_bricks % BZ
    flip_first = (jnp.bitwise_xor(first_coord, 1) * BY + second_coord) * BZ + third_coord
    flip_second = (first_coord * BY + jnp.bitwise_xor(second_coord, 1)) * BZ + third_coord
    flip_third = (first_coord * BY + second_coord) * BZ + jnp.bitwise_xor(third_coord, 1)
    listed = jnp.stack([home_bricks, flip_first, flip_second, flip_third], axis=-1)
    return (owners[..., None] * BRK_DEV + listed).reshape(NBLK, HALO).astype(jnp.int32)


def draw_point_offsets(key, part):
    uniform_draw = jax.random.uniform(key, (NBLK, 3, BLOCK), jnp.float32)
    extent = jnp.array([2.0, 4.0, 16.0], jnp.float32)[None, :, None]
    return (-1.0 + uniform_draw * (extent + 2.0)).astype(jnp.bfloat16)


def touch_ends(result, stream_key, smallest, largest):
    longest = result.shape.index(max(result.shape))
    spots = []
    for shift in (0, 1):
        where = [jax.random.randint(jax.random.fold_in(stream_key, axis), (), 0, length) for axis, length in enumerate(result.shape)]
        where[longest] = (where[longest] + shift) % result.shape[longest]
        spots.append(tuple(where))
    return result.at[spots[0]].set(smallest).at[spots[1]].set(largest)


def levels(stream_key, dims, cuts, smallest, top_value):
    factor_of = 1.0
    for axis_at, shards_of in cuts:
        steps = jax.random.uniform(jax.random.fold_in(jax.random.fold_in(stream_key, 6), axis_at), (shards_of,), jnp.float32, smallest / len(cuts), top_value / len(cuts))
        factor_of = factor_of * jnp.repeat(jnp.exp(steps), dims[axis_at] // shards_of).reshape((-1,) + (1,) * (len(dims) - 1 - axis_at))
    return factor_of


def gaussian(rng, shape, scale, limit, pieces=(), kind=jnp.bfloat16):
    entries = jax.random.normal(rng, shape, jnp.float32) * scale
    if len(pieces) > 0:
        entries = levels(rng, shape, pieces, -0.22, 0.18) * entries
    return jnp.clip(entries, min=-limit, max=limit).astype(kind)


def setup_inputs(seed: int = 0) -> dict:
    key_of = jax.random.split(jax.random.key(seed), 8)
    return {
        "point_channel_values": gaussian(key_of[0], (NBLK, CH, BLOCK), 1.0, 6.0, ((0, 32),)),
        "point_offsets": draw_point_offsets(jax.random.fold_in(key_of[7], 71), 0),
        "point_counts": touch_ends(jax.random.randint(key_of[2], (NBLK,), 1, BLOCK + 1), jax.random.fold_in(key_of[2], 1), 1, BLOCK).astype(jnp.int32),
        "block_bricks": draw_block_bricks(jax.random.fold_in(key_of[7], 71), 0),
        "spectral_weights": gaussian(key_of[4], (LAYERS, MODES, MODES, MODES, CH, 2 * CH), (2 * CH) ** -0.5, 0.5, ((2, 8), (3, 4))),
        "skip_weights": gaussian(key_of[5], (LAYERS, CH, CH), CH ** -0.5, 0.75),
        "skip_bias": gaussian(key_of[6], (LAYERS, CH), 0.5, 3.0, (), jnp.float32),
    }


AMPLITUDE = 0.25
SPREAD = 4.5
DECODE_SCALE = 0.1


def cell_centers():
    cell_index = jnp.arange(128, dtype=jnp.int32)
    return jnp.stack([cell_index // 64, (cell_index // 16) % 4, cell_index % 16]).astype(jnp.float32) + 0.5


def brick_anchor(local_ids, bricks_y, bricks_z):
    clamped_weights = jnp.maximum(local_ids, 0)
    return jnp.stack([2 * (clamped_weights // (bricks_y * bricks_z)), 4 * ((clamped_weights // bricks_z) % bricks_y), 16 * (clamped_weights % bricks_z)], axis=-1).astype(jnp.float32)


def block_work(features, offsets, counts, local_ids, bricks_y, bricks_z):
    total_items, channels, points = features.shape
    group_size = math.gcd(total_items, 16)
    centers = cell_centers()

    def one_group(items):
        feature_share, offset_part, count_part, id_part = items
        validity = (jnp.arange(points, dtype=jnp.int32)[None, :] < count_part[:, None]).astype(jnp.float32)
        anchors = brick_anchor(id_part, bricks_y, bricks_z)
        relative_position = anchors - anchors[:, :1, :]
        placed = offset_part.astype(jnp.float32)[:, None, :, :] - relative_position[:, :, :, None]
        apart = placed[..., None] - centers[None, None, :, None, :]
        distance = jnp.sum(apart * apart, axis=2)
        kernel_weight_value = (AMPLITUDE * jnp.exp(-distance / SPREAD) * validity[:, None, :, None]).astype(jnp.bfloat16)
        brick_tile_grid = jnp.einsum('dqw,dewn->deqn', feature_share.astype(jnp.float32), kernel_weight_value.astype(jnp.float32)).astype(jnp.bfloat16)
        return kernel_weight_value, brick_tile_grid

    grouped = tuple(member.reshape((total_items // group_size, group_size) + member.shape[1:]) for member in (features, offsets, counts, local_ids))
    kernel_weight_value, brick_tile_grid = lax.map(one_group, grouped)
    return kernel_weight_value.reshape((total_items,) + kernel_weight_value.shape[2:]), brick_tile_grid.reshape((total_items,) + brick_tile_grid.shape[2:])


def decode_points(brick_values, kernel_weight_value):
    summed = jnp.einsum('nhcx,nhpx->ncp', brick_values.astype(jnp.float32), kernel_weight_value.astype(jnp.float32))
    return (DECODE_SCALE * summed).astype(jnp.bfloat16)


def round_half(values):
    lowered = values.astype(jnp.bfloat16)
    lowered = lax.optimization_barrier(lowered)
    return lowered.astype(values.dtype)


def round_complex(values):
    return lax.complex(round_half(jnp.real(values)), round_half(jnp.imag(values)))


def keep_index(length, kept_modes):
    half_modes = kept_modes // 2
    return jnp.concatenate([jnp.arange(half_modes, dtype=jnp.int32), jnp.arange(length - half_modes, length, dtype=jnp.int32)]).astype(jnp.int32)


def spectral_reference(grid, weights):
    third_modes = round_complex(jnp.fft.rfft(grid, axis=3, norm="ortho")[..., :MODES])
    second_modes = round_complex(jnp.take(jnp.fft.fft(third_modes, axis=2, norm="ortho"), keep_index(NY, MODES), axis=2))
    first_modes = round_complex(jnp.take(jnp.fft.fft(second_modes, axis=1, norm="ortho"), keep_index(NX, MODES), axis=1))
    real_part = jnp.real(first_modes).transpose(1, 2, 3, 0)
    imag_part = jnp.imag(first_modes).transpose(1, 2, 3, 0)

    def mix_slice(items):
        left_real, left_imag, weight_slice = items
        weight_full = weight_slice.astype(real_part.dtype)
        from_real = jnp.einsum('kzc,kzcr->kzr', left_real, weight_full, precision=lax.Precision.HIGHEST)
        from_imag = jnp.einsum('kzc,kzcr->kzr', left_imag, weight_full, precision=lax.Precision.HIGHEST)
        return from_real[..., :CH] - from_imag[..., CH:], from_real[..., CH:] + from_imag[..., :CH]

    mixed_real, mixed_imag = lax.map(mix_slice, (real_part, imag_part, weights))
    mixed = lax.complex(mixed_real, mixed_imag).transpose(3, 0, 1, 2)
    widened = jnp.zeros((CH, NX, MODES, MODES), mixed.dtype).at[:, keep_index(NX, MODES)].set(mixed)
    first_back = round_complex(jnp.fft.ifft(widened, axis=1, norm="ortho"))
    widened = jnp.zeros((CH, NX, NY, MODES), first_back.dtype).at[:, :, keep_index(NY, MODES)].set(first_back)
    second_back = round_complex(jnp.fft.ifft(widened, axis=2, norm="ortho"))
    return jnp.fft.irfft(second_back, n=NZ, axis=3, norm="ortho")


def global_grid(bricks, bricks_along_first, bricks_y, bricks_z):
    shaped = bricks.reshape(N_PX, N_PY, bricks_along_first, bricks_y, bricks_z, CH, 2, 4, 16)
    return shaped.transpose(5, 0, 2, 6, 1, 3, 7, 4, 8).reshape(CH, NX, NY, NZ)


def global_bricks(grid, bricks_along_first, bricks_y, bricks_z):
    shaped = grid.reshape(CH, N_PX, bricks_along_first, 2, N_PY, bricks_y, 4, bricks_z, 16)
    return shaped.transpose(1, 4, 2, 5, 7, 0, 3, 6, 8).reshape(N_PX * N_PY * bricks_along_first * bricks_y * bricks_z, CH, 128)


def reference(point_channel_values, point_offsets, point_counts, block_bricks, spectral_weights, skip_weights, skip_bias):
    bricks_along_first = NX // N_PX // 2
    bricks_y = NY // N_PY // 4
    bricks_z = NZ // 16
    bricks_device = bricks_along_first * bricks_y * bricks_z
    total_bricks = bricks_device * N_PX * N_PY
    block_total = point_channel_values.shape[0]
    group_size = math.gcd(block_total, 256)
    local_ids = block_bricks % bricks_device
    stacked = tuple(member.reshape((block_total // group_size, group_size) + member.shape[1:]) for member in (point_channel_values, point_offsets, point_counts, local_ids, block_bricks))

    def add_group(brick_sums, items):
        features, offsets, counts, local_part, global_part = items
        unused, brick_tile_grid = block_work(features, offsets, counts, local_part, bricks_y, bricks_z)
        flat_tiles = brick_tile_grid.reshape((-1,) + brick_tile_grid.shape[2:]).astype(jnp.float32)
        return brick_sums.at[global_part.reshape(-1)].add(flat_tiles), None

    brick_sums, unused = lax.scan(add_group, jnp.zeros((total_bricks, CH, 128), jnp.float32), stacked)
    grid = global_grid(brick_sums.astype(jnp.bfloat16), bricks_along_first, bricks_y, bricks_z)
    for depth_index in range(LAYERS):
        spectral = spectral_reference(grid.astype(jnp.float32), spectral_weights[depth_index])
        skipped = jnp.einsum('io,ixyz->oxyz', skip_weights[depth_index].astype(jnp.float32), grid.astype(jnp.float32), precision=lax.Precision.HIGHEST)
        grid = jax.nn.gelu(spectral + skipped + skip_bias[depth_index][:, None, None, None], approximate=False).astype(jnp.bfloat16)
    final_bricks = global_bricks(grid, bricks_along_first, bricks_y, bricks_z)

    def decode_group(items):
        features, offsets, counts, local_part, global_part = items
        kernel_weight_value, unused_tiles = block_work(features, offsets, counts, local_part, bricks_y, bricks_z)
        return decode_points(jnp.take(final_bricks, global_part, axis=0), kernel_weight_value)

    decoded = lax.map(decode_group, stacked)
    return decoded.reshape((block_total,) + decoded.shape[2:])
```

```python
import functools
import math

import jax
import jax.numpy as jnp
from jax import lax
from jax.experimental import pallas as pl
from jax.experimental.pallas import tpu as pltpu
from jax.sharding import PartitionSpec as P

MODES = 32
NX = 128
NY = 128
NZ = 128
LAYERS = 2

AMPLITUDE = 0.25
SPREAD = 4.5
DECODE_SCALE = 0.1
CHUNKS = 2
MOST_PARTS = 4
WAYS = 4
VMEM_LIMIT = 60 * 1024 * 1024
F32 = jnp.float32
BF16 = jnp.bfloat16


def wave_numbers(kept_modes):
    position = jnp.arange(kept_modes, dtype=jnp.int32)
    return jnp.where(position < kept_modes // 2, position, position - kept_modes)


def forward_matrix(length, frequency):
    places = jnp.arange(length, dtype=jnp.int32)
    products = jnp.remainder(places[:, None] * frequency[None, :], length)
    angles = 2.0 * math.pi / length * products.astype(F32)
    cosine = jnp.cos(angles) / math.sqrt(length)
    sine_part = jnp.sin(angles) / math.sqrt(length)
    from_real = jnp.stack([cosine, -sine_part], axis=-1)
    from_imag = jnp.stack([sine_part, cosine], axis=-1)
    return jnp.stack([from_real, from_imag], axis=1)


def unit_angles(products, length):
    return 2.0 * math.pi / length * jnp.remainder(products, length).astype(F32)


def repeat_lines(table, slabs, copies):
    rows, depth = table.shape
    span = rows // slabs
    same = jnp.eye(copies, dtype=bool)[None, :, None, :, None]
    wide = jnp.where(same, table.reshape(slabs, 1, span, 1, depth), 0.0)
    return wide.reshape(rows * copies, copies * depth)


def block_kernel(info_ref, slot, offsets, points):
    base = slot * 13
    count = info_ref[base + 12]
    lanes = lax.broadcasted_iota(jnp.int32, (1, points), 1)
    amplitude = jnp.where(lanes < count, AMPLITUDE, 0.0).astype(F32)

    def part(dim, brick, cells, scale):
        shift = ((info_ref[base + 3 * brick + dim] - info_ref[base + dim]) * scale).astype(F32)
        center = lax.broadcasted_iota(jnp.int32, (cells, points), 0).astype(F32) + 0.5
        apart = (offsets[dim : dim + 1, :] - shift) - center
        return jnp.exp(apart * apart * (-1.0 / SPREAD))

    rows = []
    for brick in range(4):
        along_x = part(0, brick, 2, 2) * amplitude
        along_y = part(1, brick, 4, 4)
        along_z = part(2, brick, 16, 16)
        for cy in range(4):
            plane = along_z * along_y[cy : cy + 1, :]
            rows.append(
                jnp.concatenate(
                    [plane * along_x[0:1, :], plane * along_x[1:2, :]], axis=1
                ).astype(BF16)
            )
    return jnp.concatenate(rows, axis=0)


def brick_place(info_ref, slot, brick, cy, depth):
    base = slot * 13 + 3 * brick
    row = (info_ref[base + 1] * 4 + cy) * depth + info_ref[base + 2] * 16
    return (
        pl.ds(pl.multiple_of(row, 16), 16),
        pl.ds(pl.multiple_of(info_ref[base] * 128, 128), 128),
    )


def encode_body(group, depth, steps, info_ref, feature_ref, offset_ref, *refs):
    out_ref, total_ref = refs
    step = pl.program_id(0)

    @pl.when(step == 0)
    def _():
        total_ref[...] = jnp.zeros_like(total_ref)

    def some(turn, carry):
        tiles = []
        for way in range(WAYS):
            member = turn * WAYS + way
            values = block_kernel(
                info_ref, step * group + member, offset_ref[member].astype(F32), offset_ref.shape[2]
            )
            feature = feature_ref[member]
            empty = jnp.zeros_like(feature)
            pair = jnp.concatenate(
                [
                    jnp.concatenate([feature, empty], axis=1),
                    jnp.concatenate([empty, feature], axis=1),
                ],
                axis=0,
            )
            tiles.append(
                lax.dot_general(values, pair, (((1,), (1,)), ((), ())), preferred_element_type=F32)
            )
        for way in range(WAYS):
            slot = step * group + turn * WAYS + way
            rounded = tiles[way].astype(BF16).astype(F32)
            places = [
                brick_place(info_ref, slot, brick, cy, depth)
                for brick in range(4)
                for cy in range(4)
            ]
            sums = [
                total_ref[place] + rounded[16 * at : 16 * at + 16, :]
                for at, place in enumerate(places)
            ]
            for place, value in zip(places, sums):
                total_ref[place] = value

        return carry

    lax.fori_loop(0, group // WAYS, some, 0)

    @pl.when(step == steps - 1)
    def _():
        out_ref[...] = total_ref[...].astype(BF16)


def encode(info, features, offsets, rows, depth, lanes):
    slots, channels, points = features.shape
    group = math.gcd(slots, 32)
    steps = slots // group
    return pl.pallas_call(
        functools.partial(encode_body, group, depth, steps),
        grid_spec=pltpu.PrefetchScalarGridSpec(
            num_scalar_prefetch=1,
            grid=(steps,),
            in_specs=[
                pl.BlockSpec((group, channels, points), lambda i, info: (i, 0, 0)),
                pl.BlockSpec((group, offsets.shape[1], points), lambda i, info: (i, 0, 0)),
            ],
            out_specs=pl.BlockSpec((rows, lanes), lambda i, info: (0, 0)),
            scratch_shapes=[pltpu.VMEM((rows, lanes), F32)],
        ),
        out_shape=jax.ShapeDtypeStruct((rows, lanes), BF16),
        compiler_params=pltpu.CompilerParams(vmem_limit_bytes=VMEM_LIMIT),
        name="encode",
    )(info, features, offsets)


def decode_body(group, depth, info_ref, *refs):
    held_ref, offset_ref, out_ref = refs
    step = pl.program_id(0)
    channels, points = out_ref.shape[1:]

    def some(turn, carry):
        results = []
        for way in range(WAYS):
            member = turn * WAYS + way
            slot = step * group + member
            values = block_kernel(info_ref, slot, offset_ref[member].astype(F32), points)
            cells = jnp.concatenate(
                [
                    held_ref[brick_place(info_ref, slot, brick, cy, depth)]
                    for brick in range(4)
                    for cy in range(4)
                ],
                axis=0,
            )
            both = lax.dot_general(
                cells, values, (((0,), (0,)), ((), ())), preferred_element_type=F32
            )
            summed = both[:channels, :points] + both[channels:, points:]
            results.append((DECODE_SCALE * summed).astype(BF16))
        for way in range(WAYS):
            out_ref[turn * WAYS + way] = results[way]
        return carry

    lax.fori_loop(0, group // WAYS, some, 0)


def decode(info, grid, offsets, channels, depth):
    slots, rows3, points = offsets.shape
    group = math.gcd(slots, 32)
    rows, width = grid.shape
    return pl.pallas_call(
        functools.partial(decode_body, group, depth),
        grid_spec=pltpu.PrefetchScalarGridSpec(
            num_scalar_prefetch=1,
            grid=(slots // group,),
            in_specs=[pl.BlockSpec((rows, width), lambda i, info: (0, 0))]
            + [pl.BlockSpec((group, rows3, points), lambda i, info: (i, 0, 0))],
            out_specs=pl.BlockSpec((group, channels, points), lambda i, info: (i, 0, 0)),
        ),
        out_shape=jax.ShapeDtypeStruct((slots, channels, points), BF16),
        compiler_params=pltpu.CompilerParams(vmem_limit_bytes=VMEM_LIMIT),
        cost_estimate=pl.CostEstimate(
            flops=4 * slots * channels * points * 512,
            bytes_accessed=2 * rows * width,
            transcendentals=slots * points * 128,
        ),
        name="decode",
    )(info, grid, offsets)


def third_body(third_ref, grid_ref, out_ref):
    kinds, parts, lines = out_ref.shape[:3]
    depth = third_ref.shape[1] // 2
    both = third_ref.shape[0]
    span = both // (2 * kinds * parts)
    turns = 16 // (2 * span)
    slabs = kinds * parts

    def some(turn, carry):
        found = []
        for way in range(turns):
            place = pl.multiple_of((turn * turns + way) * 2 * depth, depth)
            lines_in = grid_ref[pl.ds(place, 2 * depth), :]
            found.append(jnp.dot(third_ref[...], lines_in, preferred_element_type=F32))
        row = pl.multiple_of(turn * 16, 16)
        for slab in range(slabs):
            piece = [one[slab * 2 * span : (slab + 1) * 2 * span, :] for one in found]
            piece = piece[0] if turns == 1 else jnp.concatenate(piece, axis=0)
            out_ref[slab // parts, slab % parts, pl.ds(row, 16), :] = piece.astype(BF16)
        return carry

    lax.fori_loop(0, lines // 16, some, 0)


def third_modes(third_pair, grid, kinds, parts):
    rows, lanes = grid.shape
    depth = third_pair.shape[1] // 2
    span = third_pair.shape[0] // (2 * kinds * parts)
    lines = rows // depth * span
    width = math.gcd(lanes, 256)
    return pl.pallas_call(
        third_body,
        grid=(lanes // width,),
        in_specs=[
            pl.BlockSpec(third_pair.shape, lambda i: (0, 0)),
            pl.BlockSpec((rows, width), lambda i: (0, i)),
        ],
        out_specs=pl.BlockSpec((kinds, parts, lines, width), lambda i: (0, 0, 0, i)),
        out_shape=jax.ShapeDtypeStruct((kinds, parts, lines, lanes), BF16),
        compiler_params=pltpu.CompilerParams(vmem_limit_bytes=40 * 1024 * 1024),
        name="third_modes",
    )(third_pair, grid)


def partner(me, distance):
    return me + distance - 2 * distance * ((me // distance) % 2)


def spectral_body(
    layer,
    second_ref,
    forward_ref,
    backward_ref,
    third_ref,
    weight_ref,
    modes_ref,
    held_ref,
    sums_send,
    sums_recv,
    lines_send,
    lines_recv,
    back_send,
    weight_held,
    wide_in,
    wide_out,
    sums_ssem,
    sums_rsem,
    lines_ssem,
    lines_rsem,
    back_ssem,
    back_rsem,
    modes_ssem,
    modes_rsem,
    weight_sem,
):
    kinds, parts, rows, lanes = modes_ref.shape
    devices_x, slab_rows = lines_send.shape[1:3]
    pairs_x = lanes // 128
    channels = weight_held.shape[4]
    kz_part = weight_held.shape[3]
    kx_all = weight_held.shape[1]
    me_x, me_y = lax.axis_index("px"), lax.axis_index("py")
    steps = kinds.bit_length() - 1
    tile = math.gcd(lanes, 256)
    lane_tiles = lanes // tile
    batch = 8
    weight_copies = []
    for part in range(parts):
        copy = pltpu.make_async_copy(
            weight_ref.at[layer, :, :, pl.ds(part * kz_part, kz_part)],
            weight_held.at[part],
            weight_sem.at[part],
        )
        copy.start()
        weight_copies.append(copy)

    def at_x(device):
        return {"px": device}

    def at_y(distance):
        return {"py": partner(me_y, distance)}

    barrier = pltpu.get_barrier_semaphore()
    for hop in range(1, devices_x):
        pl.semaphore_signal(
            barrier,
            inc=1,
            device_id=at_x((me_x + hop) % devices_x),
            device_id_type=pl.DeviceIdType.MESH,
        )
    for step in range(steps):
        pl.semaphore_signal(
            barrier, inc=1, device_id=at_y(1 << step), device_id_type=pl.DeviceIdType.MESH
        )

    started = []

    def send(source, target, ssem, rsem, device):
        copy = pltpu.make_async_remote_copy(
            src_ref=source,
            dst_ref=target,
            send_sem=ssem,
            recv_sem=rsem,
            device_id=device,
            device_id_type=pl.DeviceIdType.MESH,
        )
        copy.start()
        started.append(copy)
        return copy

    bases = [kinds - (kinds >> step) for step in range(steps)]
    sums_copies, lines_copies, back_copies, modes_copies = {}, {}, {}, {}

    def send_sums(part, step):
        count = kinds >> (step + 1)
        at = pl.ds(bases[step], count)
        sums_copies[part, step] = send(
            sums_send.at[part, at],
            sums_recv.at[part, at],
            sums_ssem.at[part, step],
            sums_rsem.at[part, step],
            at_y(1 << step),
        )

    def second_stage(part):
        def one(turn, carry):
            columns = pl.ds(pl.multiple_of(turn * tile, tile), tile)
            for kind in range(kinds - 1, -1, -1):
                value = jnp.dot(
                    second_ref[...], third_ref[kind, part, :, columns], preferred_element_type=F32
                )
                if kind % 2:
                    sums_send[part, kind // 2, :, columns] = value.astype(BF16)
                else:
                    held_ref[part, kind // 2, :, columns] = value
            return carry

        lax.fori_loop(0, lane_tiles, one, 0)
        send_sums(part, 0)

    def sum_stage(part, step):
        sums_copies[part, step].wait_recv()

        def one(turn, carry):
            columns = pl.ds(pl.multiple_of(turn * tile, tile), tile)
            for index in range(kinds >> (step + 1)):
                kind = index << (step + 1)
                value = held_ref[part, kind // 2, :, columns] + sums_recv[
                    part, bases[step] + index, :, columns
                ].astype(F32)
                if index % 2:
                    sums_send[part, bases[step + 1] + index // 2, :, columns] = value.astype(BF16)
                elif step + 1 < steps:
                    held_ref[part, kind // 2, :, columns] = value
                else:
                    lines_send[part, :, :, columns] = value.astype(BF16).reshape(
                        devices_x, slab_rows, tile
                    )
            return carry

        lax.fori_loop(0, lane_tiles, one, 0)
        if step + 1 < steps:
            send_sums(part, step + 1)
            return
        for hop in range(1, devices_x):
            target = (me_x + hop) % devices_x
            lines_copies[part, hop] = send(
                lines_send.at[part, target],
                lines_recv.at[part, me_x],
                lines_ssem.at[part, hop],
                lines_rsem.at[part, hop],
                at_x(target),
            )
        lines_recv[part, me_x] = lines_send[part, me_x]

    half_lane = lax.broadcasted_iota(jnp.int32, (1, 128), 1) < channels

    def mix_stage(part):
        for hop in range(1, devices_x):
            lines_copies[part, hop].wait_recv()
        weight_copies[part].wait()

        def widen(source, carry):
            for pair in range(pairs_x):
                row = pl.multiple_of((source * pairs_x + pair) * slab_rows, slab_rows)
                wide_in[pl.ds(row, slab_rows), :] = lines_recv[
                    part, source, :, pair * 128 : (pair + 1) * 128
                ].astype(F32)
            return carry

        lax.fori_loop(0, devices_x, widen, 0)
        count = devices_x * pairs_x
        modes_rows = 2 * kx_all
        row_at = lax.broadcasted_iota(jnp.int32, (modes_rows, batch * channels), 0)
        lane_at = lax.broadcasted_iota(jnp.int32, (modes_rows, batch * channels), 1)
        own = (row_at // 2) % batch == lane_at // channels

        def one(pick, carry):
            ky, kz = pick // kz_part, pick % kz_part
            line = jnp.concatenate(
                [
                    wide_in[pl.ds(2 * pick, count, stride=slab_rows), :],
                    wide_in[pl.ds(2 * pick + 1, count, stride=slab_rows), :],
                ],
                axis=0,
            ).astype(BF16)
            first = jnp.dot(forward_ref[...], line, preferred_element_type=F32)
            first = jnp.where(half_lane, first[:modes_rows], first[modes_rows:])
            first = first + pltpu.roll(first, channels, 1)
            spread = jnp.where(own, jnp.concatenate([first] * (batch // 2), axis=1), 0.0)
            spread = spread.astype(BF16)
            mixed = []
            for at in range(kx_all // batch):
                weight = weight_held[part, at * batch : (at + 1) * batch, ky, kz]
                mixed.append(
                    jnp.dot(
                        spread[2 * at * batch : 2 * (at + 1) * batch],
                        weight.reshape(batch * channels, 2 * channels),
                        preferred_element_type=F32,
                    )
                )
            mixed = jnp.concatenate(mixed, axis=0).astype(BF16)
            back = jnp.dot(backward_ref[...], mixed, preferred_element_type=F32)
            size = 2 * count
            part_at = [back[at * size : (at + 1) * size] for at in range(4)]
            final = jnp.where(half_lane, part_at[0], part_at[3]) + pltpu.roll(
                jnp.where(half_lane, part_at[2], part_at[1]), channels, 1
            )
            wide_out[pl.ds(2 * pick, count, stride=slab_rows), :] = final[:count]
            wide_out[pl.ds(2 * pick + 1, count, stride=slab_rows), :] = final[count:]
            return carry

        lax.fori_loop(0, slab_rows // 2, one, 0)

        def narrow(target, carry):
            for pair in range(pairs_x):
                row = pl.multiple_of((target * pairs_x + pair) * slab_rows, slab_rows)
                back_send[part, target, :, pair * 128 : (pair + 1) * 128] = wide_out[
                    pl.ds(row, slab_rows), :
                ].astype(BF16)
            return carry

        lax.fori_loop(0, devices_x, narrow, 0)
        mine = pl.ds(pl.multiple_of(me_x * slab_rows, slab_rows), slab_rows)
        for hop in range(1, devices_x):
            target = (me_x + hop) % devices_x
            back_copies[part, hop] = send(
                back_send.at[part, target],
                modes_ref.at[0, part, mine],
                back_ssem.at[part, hop],
                back_rsem.at[part, hop],
                at_x(target),
            )
        modes_ref[0, part, mine, :] = back_send[part, me_x]

    def spread_stage(part, kind):
        if kind == 0:
            for hop in range(1, devices_x):
                back_copies[part, hop].wait_recv()
            limit = kinds
        else:
            modes_copies[part, kind].wait_recv()
            limit = kind & -kind
        distance = limit // 2
        while distance >= 1:
            modes_copies[part, kind + distance] = send(
                modes_ref.at[kind, part],
                modes_ref.at[kind + distance, part],
                modes_ssem.at[part, kind + distance],
                modes_rsem.at[part, kind + distance],
                at_y(distance),
            )
            distance //= 2

    order = []
    for part in range(parts):
        order.append((1.5 * part, second_stage, (part,)))
        for step in range(steps):
            order.append((1.5 * part + 3.0 if step == 0 else 12.0 * step + 5.0 * part, sum_stage, (part, step)))
        base = 12.0 * (steps - 1) + 5.0 * part
        order.append((base + 7.1, mix_stage, (part,)))
        order.append((base + 19.2, spread_stage, (part, 0)))
        level = kinds // 2
        while level >= 1:
            for kind in range(level, kinds, 2 * level):
                late = 6.0 * (kinds // level).bit_length()
                order.append((base + 19.3 + late, spread_stage, (part, kind)))
            level //= 2
    order.sort(key=lambda entry: entry[0])
    waited = False
    for _, stage, given in order:
        stage_first = stage is second_stage and given == (0,)
        if stage_first and not waited:
            pl.semaphore_wait(barrier, devices_x - 1 + steps)
            waited = True
        stage(*given)
    for copy in started:
        copy.wait_send()


def spectral(layer, second, first_forward, first_back, third, weights, parts):
    kinds, _, lines, lanes = third.shape
    rows = second.shape[0]
    devices_x = lax.axis_size("px")
    slab_rows = rows // devices_x
    _, kx_all, ky_dev, kz_dev, channels, wide = weights.shape
    steps = kinds.bit_length() - 1
    count = devices_x * lanes // 128 * slab_rows
    dma = pltpu.SemaphoreType.DMA
    return pl.pallas_call(
        functools.partial(spectral_body, layer),
        in_specs=[pl.BlockSpec(memory_space=pltpu.VMEM)] * 4 + [pl.BlockSpec(memory_space=pl.ANY)],
        out_specs=pl.BlockSpec(memory_space=pltpu.VMEM),
        out_shape=jax.ShapeDtypeStruct((kinds, parts, rows, lanes), BF16),
        scratch_shapes=[
            pltpu.VMEM((parts, kinds // 2, rows, lanes), F32),
            pltpu.VMEM((parts, kinds - 1, rows, lanes), BF16),
            pltpu.VMEM((parts, kinds - 1, rows, lanes), BF16),
            pltpu.VMEM((parts, devices_x, slab_rows, lanes), BF16),
            pltpu.VMEM((parts, devices_x, slab_rows, lanes), BF16),
            pltpu.VMEM((parts, devices_x, slab_rows, lanes), BF16),
            pltpu.VMEM((parts, kx_all, ky_dev, kz_dev // parts, channels, wide), BF16),
            pltpu.VMEM((count, 128), F32),
            pltpu.VMEM((count, 128), F32),
            dma((parts, steps)),
            dma((parts, steps)),
            dma((parts, devices_x)),
            dma((parts, devices_x)),
            dma((parts, devices_x)),
            dma((parts, devices_x)),
            dma((parts, kinds)),
            dma((parts, kinds)),
            dma((parts,)),
        ],
        compiler_params=pltpu.CompilerParams(
            vmem_limit_bytes=VMEM_LIMIT, collective_id=layer, has_side_effects=True
        ),
        name="spectral",
    )(second, first_forward, first_back, third, weights)


def layer_body(second_ref, third_ref, modes_ref, grid_ref, skip_ref, bias_ref, out_ref, held_ref):
    kinds, parts = modes_ref.shape[:2]
    slabs = kinds * parts
    lines = second_ref.shape[0]
    block = third_ref.shape[0]
    for slab in range(slabs):
        held_ref[slab] = jnp.dot(
            second_ref[...],
            modes_ref[slab // parts, slab % parts],
            preferred_element_type=F32,
        ).astype(BF16)

    def some(turn, carry):
        row = pl.ds(pl.multiple_of(turn * 16, 16), 16)
        line = jnp.concatenate([held_ref[slab, row, :] for slab in range(slabs)], axis=0)
        for way in range(block // 128):
            place = pl.ds(pl.multiple_of(turn * block + way * 128, 128), 128)
            spectral_part = jnp.dot(
                third_ref[way * 128 : (way + 1) * 128, :], line, preferred_element_type=F32
            )
            skipped = jnp.dot(grid_ref[place, :], skip_ref[...], preferred_element_type=F32)
            value = spectral_part + skipped + bias_ref[...]
            out_ref[place, :] = (0.5 * value * (1.0 + lax.erf(value * math.sqrt(0.5)))).astype(BF16)
        return carry

    lax.fori_loop(0, lines // 16, some, 0)


def skip_tables(skip, bias, width):
    copies = width // skip.shape[0]
    same = jnp.eye(copies, dtype=bool)[:, None, :, None]
    wide = jnp.where(same, skip[None, :, None, :], jnp.zeros((), skip.dtype))
    return wide.reshape(width, width), jnp.tile(bias, copies).reshape(1, width)


def layer_back(second, third, modes, grid, wide_skip, wide_bias):
    rows, lanes = grid.shape
    kinds, parts, mode_rows = modes.shape[:3]
    width = wide_skip.shape[0]
    lines = second.shape[0]
    return pl.pallas_call(
        layer_body,
        grid=(lanes // width,),
        in_specs=[
            pl.BlockSpec(second.shape, lambda i: (0, 0)),
            pl.BlockSpec(third.shape, lambda i: (0, 0)),
            pl.BlockSpec((kinds, parts, mode_rows, width), lambda i: (0, 0, 0, i)),
            pl.BlockSpec((rows, width), lambda i: (0, i)),
            pl.BlockSpec((width, width), lambda i: (0, 0)),
            pl.BlockSpec((1, width), lambda i: (0, 0)),
        ],
        out_specs=pl.BlockSpec((rows, width), lambda i: (0, i)),
        out_shape=jax.ShapeDtypeStruct((rows, lanes), BF16),
        scratch_shapes=[pltpu.VMEM((kinds * parts, lines, width), BF16)],
        compiler_params=pltpu.CompilerParams(vmem_limit_bytes=40 * 1024 * 1024),
        name="layer_back",
    )(second, third, modes, grid, wide_skip, wide_bias)


def slot_plan(block_bricks, bricks_device, slot_total, capacity):
    owners = block_bricks[:, 0] // bricks_device
    order_index = jnp.arange(owners.shape[0], dtype=jnp.int32)
    earlier = (owners[None, :] == owners[:, None]) & (order_index[None, :] < order_index[:, None])
    ranking = jnp.sum(earlier.astype(jnp.int32), axis=1)
    slot_index = owners * capacity + ranking
    matching = slot_index[None, :] == jnp.arange(slot_total, dtype=jnp.int32)[:, None]
    present = jnp.any(matching, axis=1)
    sources = jnp.sum(jnp.where(matching, order_index[None, :], 0), axis=1)
    return (slot_index, present, sources)


def pack_body(sources_ref, *refs):
    half = len(refs) // 2
    slots = refs[half].shape[0]

    def some(turn, carry):
        for way in range(WAYS):
            slot = turn * WAYS + way
            source = sources_ref[slot]
            for value_ref, out_ref in zip(refs[:half], refs[half:]):
                value = value_ref[jnp.maximum(source, 0)]
                out_ref[slot] = jnp.where(source >= 0, value, jnp.zeros_like(value))
        return carry

    lax.fori_loop(0, slots // WAYS, some, 0)


def pack_slots(sources, *arrays):
    vmem = pl.BlockSpec(memory_space=pltpu.VMEM)
    return pl.pallas_call(
        pack_body,
        grid_spec=pltpu.PrefetchScalarGridSpec(
            num_scalar_prefetch=1,
            grid=(1,),
            in_specs=[vmem] * len(arrays),
            out_specs=[vmem] * len(arrays),
        ),
        out_shape=[
            jax.ShapeDtypeStruct(sources.shape + value.shape[1:], value.dtype) for value in arrays
        ],
        compiler_params=pltpu.CompilerParams(vmem_limit_bytes=40 * 1024 * 1024),
        name="pack_slots",
    )(sources, *arrays)


def unpack_body(places_ref, *refs):
    out_ref = refs[-1]
    sides = len(refs) - 1
    size = refs[0].shape[0]

    def some(turn, carry):
        for way in range(WAYS):
            block = turn * WAYS + way
            place = places_ref[block]
            value = refs[0][jnp.minimum(place, size - 1)]
            for side in range(1, sides):
                other = refs[side][jnp.clip(place - side * size, 0, size - 1)]
                value = jnp.where(place >= side * size, other, value)
            out_ref[block] = value
        return carry

    lax.fori_loop(0, out_ref.shape[0] // WAYS, some, 0)


def unpack_slots(places, replies):
    vmem = pl.BlockSpec(memory_space=pltpu.VMEM)
    return pl.pallas_call(
        unpack_body,
        grid_spec=pltpu.PrefetchScalarGridSpec(
            num_scalar_prefetch=1,
            grid=(1,),
            in_specs=[vmem] * len(replies),
            out_specs=vmem,
        ),
        out_shape=jax.ShapeDtypeStruct(places.shape + replies[0].shape[1:], replies[0].dtype),
        compiler_params=pltpu.CompilerParams(vmem_limit_bytes=40 * 1024 * 1024),
        name="unpack_slots",
    )(places, *replies)


def route_back(values):
    return lax.all_to_all(values, ("px", "py"), split_axis=0, concat_axis=0, tiled=True)


def per_device(
    point_channel_values,
    point_offsets,
    point_counts,
    block_bricks,
    spectral_weights,
    skip_weights,
    skip_bias,
):
    mesh_rows = lax.axis_size("px")
    mesh_columns = lax.axis_size("py")
    device_total = mesh_rows * mesh_columns
    capacity = max(2, 2 * point_channel_values.shape[0] // device_total)
    channels, points = point_channel_values.shape[1:]
    x_dev, y_dev = NX // mesh_rows, NY // mesh_columns
    bricks_y = y_dev // 4
    bricks_z = NZ // 16
    bricks_device = x_dev // 2 * bricks_y * bricks_z
    slot_total = device_total * capacity
    local_ids = block_bricks % bricks_device
    slot_index, present, sources = slot_plan(block_bricks, bricks_device, slot_total, capacity)
    coordinates = jnp.stack(
        [local_ids // (bricks_y * bricks_z), local_ids // bricks_z % bricks_y, local_ids % bricks_z],
        axis=-1,
    ).reshape(local_ids.shape[0], -1)
    facts = jnp.concatenate([coordinates, point_counts[:, None]], axis=1).astype(BF16)
    facts = jnp.pad(facts, ((0, 0), (0, points - facts.shape[1])))
    notes = jnp.concatenate([point_offsets, facts[:, None, :]], axis=1)
    wanted = jnp.where(present, sources, -1)
    packed_notes, packed_features = pack_slots(wanted, notes, point_channel_values)
    got_notes = route_back(packed_notes)
    got_features = route_back(packed_features)
    info = got_notes[:, 3, :13].astype(jnp.int32).reshape(-1)

    kz_dev = MODES // mesh_columns
    ky_dev = MODES // mesh_rows
    parts = 1
    while ky_dev * kz_dev * 2 // (2 * parts) % 16 == 0 and kz_dev % (2 * parts) == 0 and parts < MOST_PARTS:
        parts *= 2
    me_y = lax.axis_index("py")
    index = jnp.arange(2 * MODES, dtype=jnp.int32)
    group_at = jnp.bitwise_xor(index // (2 * kz_dev), me_y)
    kz = index // 2 % kz_dev + kz_dev * group_at
    angle_z = unit_angles(kz[:, None] * jnp.arange(NZ, dtype=jnp.int32)[None, :], NZ)
    third = jnp.where((index % 2 == 0)[:, None], jnp.cos(angle_z), -jnp.sin(angle_z))
    third = third / math.sqrt(NZ)
    fold = jnp.where(kz == 0, 1.0, 2.0).astype(F32)[:, None]
    span = 2 * kz_dev // parts
    slabs = mesh_columns * parts
    third_pair = repeat_lines(third, slabs, 2).astype(BF16)
    third_back = repeat_lines(third * fold, slabs, 16 // span).T.astype(BF16)
    row = jnp.arange(MODES * span, dtype=jnp.int32)[:, None]
    column = jnp.arange(y_dev * span, dtype=jnp.int32)[None, :]
    ky_at = row // span
    ky = jnp.where(ky_at < MODES // 2, ky_at, ky_at - MODES)
    angle_y = unit_angles(ky * (me_y * y_dev + column // span), NY)
    row_part, column_part = row % 2, column % 2
    sine = jnp.where(row_part == 0, jnp.sin(angle_y), -jnp.sin(angle_y))
    second = jnp.where(row_part == column_part, jnp.cos(angle_y), sine) / math.sqrt(NY)
    second = jnp.where(row % span // 2 == column % span // 2, second, 0.0).astype(BF16)
    second_back = second.T
    first_matrix = forward_matrix(NX, wave_numbers(MODES))
    by_pair = first_matrix.reshape(NX // 2, 2, 2, MODES, 2)
    first_forward = by_pair.transpose(1, 3, 4, 2, 0).reshape(4 * MODES, NX).astype(BF16)
    turned = jnp.stack([by_pair[..., 1], -by_pair[..., 0]], axis=-1)
    first_back = jnp.stack([by_pair, turned], axis=0).transpose(2, 0, 3, 1, 4, 5)
    first_back = first_back.reshape(4 * NX, 2 * MODES).astype(BF16)
    lanes = x_dev * channels
    width = math.gcd(lanes // CHUNKS, 4 * channels)
    skips = [skip_tables(skip_weights[at], skip_bias[at], width) for at in range(LAYERS)]
    tables = (third_pair, third_back, second, second_back, first_forward, first_back, skips)
    got_features, tables = lax.optimization_barrier((got_features, tables))
    third_pair, third_back, second, second_back, first_forward, first_back, skips = tables
    grid = encode(info, got_features, got_notes, y_dev * NZ, NZ, lanes)
    for layer in range(LAYERS):
        third_found = third_modes(third_pair, grid, mesh_columns, parts)
        modes = spectral(
            layer, second, first_forward, first_back, third_found, spectral_weights, parts
        )
        grid = layer_back(second_back, third_back, modes, grid, *skips[layer])
    half = capacity // 2
    ranks = slot_index % capacity
    at_half = slot_index // capacity * half + ranks % half
    infos = info.reshape(device_total, 2, -1)
    halved_notes = got_notes.reshape((device_total, 2, half) + got_notes.shape[1:])
    replies = []
    for side in range(2):
        side_notes = halved_notes[:, side].reshape((-1,) + got_notes.shape[1:])
        reply = decode(infos[:, side].reshape(-1), grid, side_notes, channels, NZ)
        replies.append(route_back(reply))
    places = jnp.where(ranks < half, at_half, at_half + device_total * half)
    return unpack_slots(places, replies)


def solution(mesh):
    return jax.shard_map(
        per_device,
        mesh=mesh,
        in_specs=(
            P(("px", "py"), None, None),
            P(("px", "py"), None, None),
            P(("px", "py")),
            P(("px", "py"), None),
            P(None, None, "px", "py", None, None),
            P(),
            P(),
        ),
        out_specs=P(("px", "py"), None, None),
        check_vma=False,
    )
```

```python
import functools
import math

import jax
import jax.numpy as jnp
from jax import lax
from jax.experimental import pallas as pl
from jax.experimental.pallas import tpu as pltpu
from jax.sharding import PartitionSpec as P

MODES = 32
NX = 128
NY = 128
NZ = 128
LAYERS = 2

AMPLITUDE = 0.25
SPREAD = 4.5
DECODE_SCALE = 0.1
CHUNKS = 2
MOST_PARTS = 4
WAYS = 4
VMEM_LIMIT = 60 * 1024 * 1024
F32 = jnp.float32
BF16 = jnp.bfloat16


def wave_numbers(kept_modes):
    position = jnp.arange(kept_modes, dtype=jnp.int32)
    return jnp.where(position < kept_modes // 2, position, position - kept_modes)


def forward_matrix(length, frequency):
    places = jnp.arange(length, dtype=jnp.int32)
    products = jnp.remainder(places[:, None] * frequency[None, :], length)
    angles = 2.0 * math.pi / length * products.astype(F32)
    cosine = jnp.cos(angles) / math.sqrt(length)
    sine_part = jnp.sin(angles) / math.sqrt(length)
    from_real = jnp.stack([cosine, -sine_part], axis=-1)
    from_imag = jnp.stack([sine_part, cosine], axis=-1)
    return jnp.stack([from_real, from_imag], axis=1)


def unit_angles(products, length):
    return 2.0 * math.pi / length * jnp.remainder(products, length).astype(F32)


def repeat_lines(table, slabs, copies):
    rows, depth = table.shape
    span = rows // slabs
    same = jnp.eye(copies, dtype=bool)[None, :, None, :, None]
    wide = jnp.where(same, table.reshape(slabs, 1, span, 1, depth), 0.0)
    return wide.reshape(rows * copies, copies * depth)


def block_values(offsets, shift_of, count, points):
    lanes = lax.broadcasted_iota(jnp.int32, (1, points), 1).astype(F32)
    amplitude = jnp.where(lanes < count, AMPLITUDE, 0.0).astype(F32)

    def part(dim, brick, cells, scale):
        center = lax.broadcasted_iota(jnp.int32, (cells, points), 0).astype(F32) + 0.5
        apart = (offsets[dim : dim + 1, :] - shift_of(dim, brick) * scale) - center
        return jnp.exp(apart * apart * (-1.0 / SPREAD))

    rows = []
    for brick in range(4):
        along_x = part(0, brick, 2, 2.0) * amplitude
        along_y = part(1, brick, 4, 4.0)
        along_z = part(2, brick, 16, 16.0)
        for cy in range(4):
            plane = along_z * along_y[cy : cy + 1, :]
            rows.append(
                jnp.concatenate(
                    [plane * along_x[0:1, :], plane * along_x[1:2, :]], axis=1
                ).astype(BF16)
            )
    return jnp.concatenate(rows, axis=0)


def block_kernel(info_ref, slot, offsets, points):
    base = slot * 13
    return block_values(
        offsets,
        lambda dim, brick: (info_ref[base + 3 * brick + dim] - info_ref[base + dim]).astype(F32),
        info_ref[base + 12].astype(F32),
        points,
    )


def mask_at(turn, devices):
    return (turn * ((13 * devices // 32) | 1)) % devices


def crossed(value, mask, size):
    result, bit = 0, 1
    while bit < size:
        result = result + bit * ((value // bit + mask // bit) % 2)
        bit *= 2
    return result


def route_body(
    size_x,
    size_y,
    source_ref,
    note_ref,
    feature_ref,
    tile_ref,
    got_note_ref,
    feature_send,
    feature_got,
    note_send,
    tile_held,
    feature_ssem,
    feature_rsem,
    note_ssem,
    note_rsem,
    tile_sem,
):
    slots, channels, points = feature_send.shape
    devices = size_x * size_y
    capacity = slots // devices
    ways = math.gcd(WAYS, capacity)
    note_rows = note_send.shape[1]
    me = lax.axis_index("px") * size_y + lax.axis_index("py")
    barrier = pltpu.get_barrier_semaphore()

    def greet(mask, carry):
        other = crossed(me, mask, devices)
        pl.semaphore_signal(
            barrier,
            inc=1,
            device_id={"px": other // size_y, "py": other % size_y},
            device_id_type=pl.DeviceIdType.MESH,
        )
        return carry

    lax.fori_loop(1, devices, greet, 0)

    def transfers(mask):
        other = crossed(me, mask, devices)
        there = {"px": other // size_y, "py": other % size_y}
        return (
            pltpu.make_async_remote_copy(
                src_ref=note_send.at[other],
                dst_ref=got_note_ref.at[me],
                send_sem=note_ssem.at[mask],
                recv_sem=note_rsem.at[mask],
                device_id=there,
                device_id_type=pl.DeviceIdType.MESH,
            ),
            pltpu.make_async_remote_copy(
                src_ref=feature_send.at[pl.ds(other * capacity, capacity)],
                dst_ref=feature_got.at[pl.ds(me * capacity, capacity)],
                send_sem=feature_ssem.at[mask],
                recv_sem=feature_rsem.at[mask],
                device_id=there,
                device_id_type=pl.DeviceIdType.MESH,
            ),
        )

    def pack(other, notes_to, features_to):
        notes = []
        for slot in range(capacity):
            source = source_ref[other * capacity + slot]
            present = source >= 0
            source = jnp.maximum(source, 0)
            feature = feature_ref[source]
            features_to[other * capacity + slot] = jnp.where(
                present, feature, jnp.zeros_like(feature)
            )
            notes.append(jnp.where(present, note_ref[source].astype(F32), 0.0))
        if note_rows > 4 * capacity:
            notes.append(jnp.zeros((note_rows - 4 * capacity, points), F32))
        notes_to[other] = jnp.concatenate(notes, axis=0).astype(BF16)

    first = mask_at(1, devices)
    pack(crossed(me, first, devices), note_send, feature_send)
    pl.semaphore_wait(barrier, devices - 1)
    for copy in transfers(first):
        copy.start()

    def launch(turn, carry):
        mask = mask_at(turn, devices)
        pack(crossed(me, mask, devices), note_send, feature_send)
        for copy in transfers(mask):
            copy.start()
        return carry

    lax.fori_loop(2, devices, launch, 0)
    pack(me, got_note_ref, feature_got)

    def tile_copy(turn, other):
        return pltpu.make_async_copy(
            tile_held.at[turn % 2],
            tile_ref.at[pl.ds(other * capacity, capacity)],
            tile_sem.at[turn % 2],
        )

    def work(turn, other):
        notes = got_note_ref[other].astype(F32)
        for start in range(0, capacity, ways):
            tiles = []
            for slot in range(start, start + ways):
                offsets = notes[4 * slot : 4 * slot + 3, :]
                facts = notes[4 * slot + 3 : 4 * slot + 4, :]
                values = block_values(
                    offsets,
                    lambda dim, brick: facts[:, 3 * brick + dim : 3 * brick + dim + 1]
                    - facts[:, dim : dim + 1],
                    facts[:, 12:13],
                    points,
                )
                feature = feature_got[other * capacity + slot]
                empty = jnp.zeros_like(feature)
                pair = jnp.concatenate(
                    [
                        jnp.concatenate([feature, empty], axis=1),
                        jnp.concatenate([empty, feature], axis=1),
                    ],
                    axis=0,
                )
                tiles.append(
                    lax.dot_general(
                        values, pair, (((1,), (1,)), ((), ())), preferred_element_type=F32
                    ).astype(BF16)
                )
            for way in range(ways):
                tile_held[turn % 2, start + way] = tiles[way]
        tile_copy(turn, other).start()

    work(0, me)

    def step(turn, carry):
        mask = mask_at(turn, devices)
        for copy in transfers(mask):
            copy.wait_recv()

        @pl.when(turn >= 2)
        def _():
            tile_copy(turn, me).wait()

        work(turn, crossed(me, mask, devices))
        return carry

    lax.fori_loop(1, devices, step, 0)
    for turn in range(devices - 2, devices):
        tile_copy(turn, me).wait()

    def leave(mask, carry):
        for copy in transfers(mask):
            copy.wait_send()
        return carry

    lax.fori_loop(1, devices, leave, 0)


def route(sources, notes, features):
    slots = sources.shape[0]
    channels, points = features.shape[1:]
    size_x, size_y = lax.axis_size("px"), lax.axis_size("py")
    devices = size_x * size_y
    capacity = slots // devices
    note_rows = (4 * capacity + 15) // 16 * 16
    vmem = pl.BlockSpec(memory_space=pltpu.VMEM)
    dma = pltpu.SemaphoreType.DMA
    return pl.pallas_call(
        functools.partial(route_body, size_x, size_y),
        in_specs=[pl.BlockSpec(memory_space=pltpu.SMEM), vmem, vmem],
        out_specs=[pl.BlockSpec(memory_space=pl.ANY), vmem],
        out_shape=[
            jax.ShapeDtypeStruct((slots, 256, 2 * channels), BF16),
            jax.ShapeDtypeStruct((devices, note_rows, points), BF16),
        ],
        scratch_shapes=[
            pltpu.VMEM((slots, channels, points), BF16),
            pltpu.VMEM((slots, channels, points), BF16),
            pltpu.VMEM((devices, note_rows, points), BF16),
            pltpu.VMEM((2, capacity, 256, 2 * channels), BF16),
            dma((devices,)),
            dma((devices,)),
            dma((devices,)),
            dma((devices,)),
            dma((2,)),
        ],
        compiler_params=pltpu.CompilerParams(
            vmem_limit_bytes=VMEM_LIMIT, collective_id=LAYERS + 1, has_side_effects=True
        ),
        name="route",
    )(sources, notes, features)


def find_third(third_ref, lines_of, out_ref, columns):
    kinds, parts, lines = out_ref.shape[:3]
    both = third_ref.shape[0]
    span = both // (2 * kinds * parts)
    turns = 16 // (2 * span)

    def some(turn, carry):
        found = [
            jnp.dot(third_ref[...], lines_of(turn * turns + way), preferred_element_type=F32)
            for way in range(turns)
        ]
        row = pl.multiple_of(turn * 16, 16)
        for slab in range(kinds * parts):
            piece = [one[slab * 2 * span : (slab + 1) * 2 * span, :] for one in found]
            piece = piece[0] if turns == 1 else jnp.concatenate(piece, axis=0)
            out_ref[slab // parts, slab % parts, pl.ds(row, 16), columns] = piece.astype(BF16)
        return carry

    lax.fori_loop(0, lines // 16, some, 0, unroll=2)


def gather_body(group, steps, lift, base_ref, tile_ref, third_ref, out_ref, modes_ref, total_ref):
    step = pl.program_id(0)
    lanes = out_ref.shape[1]
    depth = third_ref.shape[1] // 2
    tiles = lanes // 128

    @pl.when(step == 0)
    def _():
        total_ref[...] = jnp.zeros_like(total_ref)

    def some(turn, carry):
        for way in range(WAYS):
            member = turn * WAYS + way
            slot = step * group + member
            bases = [base_ref[slot * 4 + brick] for brick in range(4)]
            places = [base + cy * lift for base in bases for cy in range(4)]
            sums = [
                total_ref[place] + tile_ref[member, 16 * at : 16 * at + 16, :].astype(F32)
                for at, place in enumerate(places)
            ]
            for place, value in zip(places, sums):
                total_ref[place] = value
        return carry

    lax.fori_loop(0, group // WAYS, some, 0)

    @pl.when(step == steps - 1)
    def _():
        width = math.gcd(lanes, 256)
        pieces = width // 128

        def tile(turn, carry):
            columns = pl.ds(pl.multiple_of(turn * width, width), width)

            def lines_of(pair):
                place = pl.ds(pl.multiple_of(pair * 2 * depth, 2 * depth), 2 * depth)
                rows = []
                for at in range(2 * depth // 16):
                    here = (pair * (2 * depth // 16) + at) * tiles + turn * pieces
                    rows.append(
                        jnp.concatenate([total_ref[here + to] for to in range(pieces)], axis=1)
                    )
                value = jnp.concatenate(rows, axis=0).astype(BF16)
                out_ref[place, columns] = value
                return value

            find_third(third_ref, lines_of, modes_ref, columns)
            return carry

        lax.fori_loop(0, lanes // width, tile, 0)


def gather_grid(bases, tiles, third_pair, rows, lanes, kinds, parts, lift):
    slots = tiles.shape[0]
    group = math.gcd(slots, 16)
    depth = third_pair.shape[1] // 2
    lines = rows // depth * third_pair.shape[0] // (2 * kinds * parts)
    return pl.pallas_call(
        functools.partial(gather_body, group, slots // group, lift),
        grid_spec=pltpu.PrefetchScalarGridSpec(
            num_scalar_prefetch=1,
            grid=(slots // group,),
            in_specs=[
                pl.BlockSpec((group,) + tiles.shape[1:], lambda i, info: (i, 0, 0)),
                pl.BlockSpec(third_pair.shape, lambda i, info: (0, 0)),
            ],
            out_specs=[
                pl.BlockSpec((rows, lanes), lambda i, info: (0, 0)),
                pl.BlockSpec((kinds, parts, lines, lanes), lambda i, info: (0, 0, 0, 0)),
            ],
            scratch_shapes=[pltpu.VMEM((rows * lanes // 2048, 16, 128), F32)],
        ),
        out_shape=[
            jax.ShapeDtypeStruct((rows, lanes), BF16),
            jax.ShapeDtypeStruct((kinds, parts, lines, lanes), BF16),
        ],
        compiler_params=pltpu.CompilerParams(vmem_limit_bytes=VMEM_LIMIT),
        name="gather_grid",
    )(bases, tiles, third_pair)


def decode_body(size_x, size_y, lift, info_ref, base_ref, held_ref, offset_ref, got_ref, reply_ref, ssem, rsem, own_sem):
    slots, channels, points = got_ref.shape
    devices = size_x * size_y
    capacity = slots // devices
    ways = math.gcd(WAYS, capacity)
    me_x, me_y = lax.axis_index("px"), lax.axis_index("py")
    me = me_x * size_y + me_y
    barrier = pltpu.get_barrier_semaphore()

    def greet(mask, carry):
        other = crossed(me, mask, devices)
        pl.semaphore_signal(
            barrier,
            inc=1,
            device_id={"px": other // size_y, "py": other % size_y},
            device_id_type=pl.DeviceIdType.MESH,
        )
        return carry

    lax.fori_loop(1, devices, greet, 0)

    def transfer(mask):
        other = crossed(me, mask, devices)
        return pltpu.make_async_remote_copy(
            src_ref=reply_ref.at[pl.ds(other * capacity, capacity)],
            dst_ref=got_ref.at[pl.ds(me * capacity, capacity)],
            send_sem=ssem.at[mask],
            recv_sem=rsem.at[mask],
            device_id={"px": other // size_y, "py": other % size_y},
            device_id_type=pl.DeviceIdType.MESH,
        )

    def fill(other):
        def some(turn, carry):
            results = []
            for way in range(ways):
                slot = other * capacity + turn * ways + way
                values = block_kernel(info_ref, slot, offset_ref[slot].astype(F32), points)
                cells = jnp.concatenate(
                    [
                        held_ref[base_ref[slot * 4 + brick] + cy * lift]
                        for brick in range(4)
                        for cy in range(4)
                    ],
                    axis=0,
                )
                both = lax.dot_general(
                    cells, values, (((0,), (0,)), ((), ())), preferred_element_type=F32
                )
                summed = both[:channels, :points] + both[channels:, points:]
                results.append((DECODE_SCALE * summed).astype(BF16))
            for way in range(ways):
                reply_ref[other * capacity + turn * ways + way] = results[way]
            return carry

        lax.fori_loop(0, capacity // ways, some, 0)

    first = mask_at(1, devices)
    fill(crossed(me, first, devices))
    pl.semaphore_wait(barrier, devices - 1)
    transfer(first).start()

    def step(turn, carry):
        mask = mask_at(turn, devices)
        fill(crossed(me, mask, devices))
        transfer(mask).start()
        return carry

    lax.fori_loop(2, devices, step, 0)
    fill(me)
    mine = pl.ds(me * capacity, capacity)
    own = pltpu.make_async_copy(reply_ref.at[mine], got_ref.at[mine], own_sem)
    own.start()
    own.wait()

    def finish(mask, carry):
        transfer(mask).wait_recv()
        return carry

    lax.fori_loop(1, devices, finish, 0)

    def leave(mask, carry):
        transfer(mask).wait_send()
        return carry

    lax.fori_loop(1, devices, leave, 0)


def decode(info, bases, grid, offsets, channels, lift):
    slots, _, points = offsets.shape
    size_x, size_y = lax.axis_size("px"), lax.axis_size("py")
    devices = size_x * size_y
    vmem = pl.BlockSpec(memory_space=pltpu.VMEM)
    return pl.pallas_call(
        functools.partial(decode_body, size_x, size_y, lift),
        in_specs=[pl.BlockSpec(memory_space=pltpu.SMEM)] * 2 + [vmem, vmem],
        out_specs=vmem,
        out_shape=jax.ShapeDtypeStruct((slots, channels, points), BF16),
        scratch_shapes=[
            pltpu.VMEM((slots, channels, points), BF16),
            pltpu.SemaphoreType.DMA((devices,)),
            pltpu.SemaphoreType.DMA((devices,)),
            pltpu.SemaphoreType.DMA,
        ],
        compiler_params=pltpu.CompilerParams(
            vmem_limit_bytes=VMEM_LIMIT, collective_id=LAYERS, has_side_effects=True
        ),
        name="decode",
    )(info, bases, grid, offsets)


def partner(me, distance):
    return me + distance - 2 * distance * ((me // distance) % 2)


def spectral_body(
    layer,
    second_ref,
    forward_ref,
    backward_ref,
    third_ref,
    weight_ref,
    modes_ref,
    held_ref,
    sums_send,
    sums_recv,
    lines_send,
    lines_recv,
    back_send,
    weight_held,
    wide_in,
    wide_out,
    sums_ssem,
    sums_rsem,
    lines_ssem,
    lines_rsem,
    back_ssem,
    back_rsem,
    modes_ssem,
    modes_rsem,
    weight_sem,
):
    kinds, parts, rows, lanes = modes_ref.shape
    devices_x, slab_rows = lines_send.shape[1:3]
    pairs_x = lanes // 128
    channels = weight_held.shape[4]
    kz_part = weight_held.shape[3]
    kx_all = weight_held.shape[1]
    me_x, me_y = lax.axis_index("px"), lax.axis_index("py")
    steps = kinds.bit_length() - 1
    tile = math.gcd(lanes, 256)
    lane_tiles = lanes // tile
    batch = 8
    weight_copies = []
    for part in range(parts):
        copy = pltpu.make_async_copy(
            weight_ref.at[layer, :, :, pl.ds(part * kz_part, kz_part)],
            weight_held.at[part],
            weight_sem.at[part],
        )
        copy.start()
        weight_copies.append(copy)

    def at_x(device):
        return {"px": device}

    def at_y(distance):
        return {"py": partner(me_y, distance)}

    barrier = pltpu.get_barrier_semaphore()
    for hop in range(1, devices_x):
        pl.semaphore_signal(
            barrier,
            inc=1,
            device_id=at_x((me_x + hop) % devices_x),
            device_id_type=pl.DeviceIdType.MESH,
        )
    for step in range(steps):
        pl.semaphore_signal(
            barrier, inc=1, device_id=at_y(1 << step), device_id_type=pl.DeviceIdType.MESH
        )

    started = []

    def send(source, target, ssem, rsem, device):
        copy = pltpu.make_async_remote_copy(
            src_ref=source,
            dst_ref=target,
            send_sem=ssem,
            recv_sem=rsem,
            device_id=device,
            device_id_type=pl.DeviceIdType.MESH,
        )
        copy.start()
        started.append(copy)
        return copy

    bases = [kinds - (kinds >> step) for step in range(steps)]
    sums_copies, lines_copies, back_copies, modes_copies = {}, {}, {}, {}

    def send_sums(part, step):
        count = kinds >> (step + 1)
        at = pl.ds(bases[step], count)
        sums_copies[part, step] = send(
            sums_send.at[part, at],
            sums_recv.at[part, at],
            sums_ssem.at[part, step],
            sums_rsem.at[part, step],
            at_y(1 << step),
        )

    def second_stage(part):
        def one(turn, carry):
            columns = pl.ds(pl.multiple_of(turn * tile, tile), tile)
            for kind in range(kinds - 1, -1, -1):
                value = jnp.dot(
                    second_ref[...], third_ref[kind, part, :, columns], preferred_element_type=F32
                )
                if kind % 2:
                    sums_send[part, kind // 2, :, columns] = value.astype(BF16)
                else:
                    held_ref[part, kind // 2, :, columns] = value
            return carry

        lax.fori_loop(0, lane_tiles, one, 0)
        send_sums(part, 0)

    def sum_stage(part, step):
        sums_copies[part, step].wait_recv()

        def one(turn, carry):
            columns = pl.ds(pl.multiple_of(turn * tile, tile), tile)
            for index in range(kinds >> (step + 1)):
                kind = index << (step + 1)
                value = held_ref[part, kind // 2, :, columns] + sums_recv[
                    part, bases[step] + index, :, columns
                ].astype(F32)
                if index % 2:
                    sums_send[part, bases[step + 1] + index // 2, :, columns] = value.astype(BF16)
                elif step + 1 < steps:
                    held_ref[part, kind // 2, :, columns] = value
                else:
                    lines_send[part, :, :, columns] = value.astype(BF16).reshape(
                        devices_x, slab_rows, tile
                    )
            return carry

        lax.fori_loop(0, lane_tiles, one, 0)
        if step + 1 < steps:
            send_sums(part, step + 1)
            return
        for hop in range(1, devices_x):
            target = (me_x + hop) % devices_x
            lines_copies[part, hop] = send(
                lines_send.at[part, target],
                lines_recv.at[part, me_x],
                lines_ssem.at[part, hop],
                lines_rsem.at[part, hop],
                at_x(target),
            )
        lines_recv[part, me_x] = lines_send[part, me_x]

    half_lane = lax.broadcasted_iota(jnp.int32, (1, 128), 1) < channels

    def mix_stage(part):
        for hop in range(1, devices_x):
            lines_copies[part, hop].wait_recv()
        weight_copies[part].wait()

        def widen(source, carry):
            for pair in range(pairs_x):
                row = pl.multiple_of((source * pairs_x + pair) * slab_rows, slab_rows)
                wide_in[pl.ds(row, slab_rows), :] = lines_recv[
                    part, source, :, pair * 128 : (pair + 1) * 128
                ].astype(F32)
            return carry

        lax.fori_loop(0, devices_x, widen, 0)
        count = devices_x * pairs_x
        modes_rows = 2 * kx_all
        row_at = lax.broadcasted_iota(jnp.int32, (modes_rows, batch * channels), 0)
        lane_at = lax.broadcasted_iota(jnp.int32, (modes_rows, batch * channels), 1)
        own = (row_at // 2) % batch == lane_at // channels

        def one(pick, carry):
            ky, kz = pick // kz_part, pick % kz_part
            line = jnp.concatenate(
                [
                    wide_in[pl.ds(2 * pick, count, stride=slab_rows), :],
                    wide_in[pl.ds(2 * pick + 1, count, stride=slab_rows), :],
                ],
                axis=0,
            ).astype(BF16)
            first = jnp.dot(forward_ref[...], line, preferred_element_type=F32)
            first = jnp.where(half_lane, first[:modes_rows], first[modes_rows:])
            first = first + pltpu.roll(first, channels, 1)
            spread = jnp.where(own, jnp.concatenate([first] * (batch // 2), axis=1), 0.0)
            spread = spread.astype(BF16)
            mixed = []
            for at in range(kx_all // batch):
                weight = weight_held[part, at * batch : (at + 1) * batch, ky, kz]
                mixed.append(
                    jnp.dot(
                        spread[2 * at * batch : 2 * (at + 1) * batch],
                        weight.reshape(batch * channels, 2 * channels),
                        preferred_element_type=F32,
                    )
                )
            mixed = jnp.concatenate(mixed, axis=0).astype(BF16)
            back = jnp.dot(backward_ref[...], mixed, preferred_element_type=F32)
            size = 2 * count
            part_at = [back[at * size : (at + 1) * size] for at in range(4)]
            final = jnp.where(half_lane, part_at[0], part_at[3]) + pltpu.roll(
                jnp.where(half_lane, part_at[2], part_at[1]), channels, 1
            )
            wide_out[pl.ds(2 * pick, count, stride=slab_rows), :] = final[:count]
            wide_out[pl.ds(2 * pick + 1, count, stride=slab_rows), :] = final[count:]
            return carry

        lax.fori_loop(0, slab_rows // 2, one, 0)

        def narrow(target, carry):
            for pair in range(pairs_x):
                row = pl.multiple_of((target * pairs_x + pair) * slab_rows, slab_rows)
                back_send[part, target, :, pair * 128 : (pair + 1) * 128] = wide_out[
                    pl.ds(row, slab_rows), :
                ].astype(BF16)
            return carry

        lax.fori_loop(0, devices_x, narrow, 0)
        mine = pl.ds(pl.multiple_of(me_x * slab_rows, slab_rows), slab_rows)
        for hop in range(1, devices_x):
            target = (me_x + hop) % devices_x
            back_copies[part, hop] = send(
                back_send.at[part, target],
                modes_ref.at[0, part, mine],
                back_ssem.at[part, hop],
                back_rsem.at[part, hop],
                at_x(target),
            )
        modes_ref[0, part, mine, :] = back_send[part, me_x]

    def spread_stage(part, kind):
        if kind == 0:
            for hop in range(1, devices_x):
                back_copies[part, hop].wait_recv()
            limit = kinds
        else:
            modes_copies[part, kind].wait_recv()
            limit = kind & -kind
        distance = limit // 2
        while distance >= 1:
            modes_copies[part, kind + distance] = send(
                modes_ref.at[kind, part],
                modes_ref.at[kind + distance, part],
                modes_ssem.at[part, kind + distance],
                modes_rsem.at[part, kind + distance],
                at_y(distance),
            )
            distance //= 2

    order = []
    for part in range(parts):
        order.append((1.5 * part, second_stage, (part,)))
        for step in range(steps):
            order.append((1.5 * part + 3.0 if step == 0 else 12.0 * step + 5.0 * part, sum_stage, (part, step)))
        base = 12.0 * (steps - 1) + 5.0 * part
        order.append((base + 7.1, mix_stage, (part,)))
        order.append((base + 19.2, spread_stage, (part, 0)))
        level = kinds // 2
        while level >= 1:
            for kind in range(level, kinds, 2 * level):
                late = 6.0 * (kinds // level).bit_length()
                order.append((base + 19.3 + late, spread_stage, (part, kind)))
            level //= 2
    order.sort(key=lambda entry: entry[0])
    waited = False
    for _, stage, given in order:
        stage_first = stage is second_stage and given == (0,)
        if stage_first and not waited:
            pl.semaphore_wait(barrier, devices_x - 1 + steps)
            waited = True
        stage(*given)
    for copy in started:
        copy.wait_send()


def spectral(layer, second, first_forward, first_back, third, weights, parts):
    kinds, _, lines, lanes = third.shape
    rows = second.shape[0]
    devices_x = lax.axis_size("px")
    slab_rows = rows // devices_x
    _, kx_all, ky_dev, kz_dev, channels, wide = weights.shape
    steps = kinds.bit_length() - 1
    count = devices_x * lanes // 128 * slab_rows
    dma = pltpu.SemaphoreType.DMA
    return pl.pallas_call(
        functools.partial(spectral_body, layer),
        in_specs=[pl.BlockSpec(memory_space=pltpu.VMEM)] * 4 + [pl.BlockSpec(memory_space=pl.ANY)],
        out_specs=pl.BlockSpec(memory_space=pltpu.VMEM),
        out_shape=jax.ShapeDtypeStruct((kinds, parts, rows, lanes), BF16),
        scratch_shapes=[
            pltpu.VMEM((parts, kinds // 2, rows, lanes), F32),
            pltpu.VMEM((parts, kinds - 1, rows, lanes), BF16),
            pltpu.VMEM((parts, kinds - 1, rows, lanes), BF16),
            pltpu.VMEM((parts, devices_x, slab_rows, lanes), BF16),
            pltpu.VMEM((parts, devices_x, slab_rows, lanes), BF16),
            pltpu.VMEM((parts, devices_x, slab_rows, lanes), BF16),
            pltpu.VMEM((parts, kx_all, ky_dev, kz_dev // parts, channels, wide), BF16),
            pltpu.VMEM((count, 128), F32),
            pltpu.VMEM((count, 128), F32),
            dma((parts, steps)),
            dma((parts, steps)),
            dma((parts, devices_x)),
            dma((parts, devices_x)),
            dma((parts, devices_x)),
            dma((parts, devices_x)),
            dma((parts, kinds)),
            dma((parts, kinds)),
            dma((parts,)),
        ],
        compiler_params=pltpu.CompilerParams(
            vmem_limit_bytes=VMEM_LIMIT, collective_id=layer, has_side_effects=True
        ),
        name="spectral",
    )(second, first_forward, first_back, third, weights)


def layer_body(
    second_ref, third_ref, pair_ref, modes_ref, grid_ref, skip_ref, bias_ref, out_ref, *refs
):
    held_ref = refs[-1]
    tiled = len(out_ref.shape) == 4
    kinds, parts = modes_ref.shape[:2]
    slabs = kinds * parts
    lines = second_ref.shape[0]
    block = third_ref.shape[0]
    for slab in range(slabs):
        held_ref[slab] = jnp.dot(
            second_ref[...],
            modes_ref[slab // parts, slab % parts],
            preferred_element_type=F32,
        ).astype(BF16)

    def some(turn, carry):
        row = pl.ds(pl.multiple_of(turn * 16, 16), 16)
        line = jnp.concatenate([held_ref[slab, row, :] for slab in range(slabs)], axis=0)
        for way in range(block // 128):
            place = pl.ds(pl.multiple_of(turn * block + way * 128, 128), 128)
            spectral_part = jnp.dot(
                third_ref[way * 128 : (way + 1) * 128, :], line, preferred_element_type=F32
            )
            skipped = jnp.dot(grid_ref[place, :], skip_ref[...], preferred_element_type=F32)
            value = spectral_part + skipped + bias_ref[...]
            value = (0.5 * value * (1.0 + lax.erf(value * math.sqrt(0.5)))).astype(BF16)
            if tiled:
                row_tiles = pl.ds(turn * (block // 16) + way * 8, 8)
                for at in range(out_ref.shape[1]):
                    piece = value[:, at * 128 : (at + 1) * 128]
                    out_ref[row_tiles, at] = piece.reshape(8, 16, 128)
            else:
                out_ref[place, :] = value
        return carry

    lax.fori_loop(0, lines // 16, some, 0)
    if not tiled:
        pair = pair_ref.shape[1]

        def lines_of(at):
            return out_ref[pl.ds(pl.multiple_of(at * pair, pair), pair), :]

        find_third(pair_ref, lines_of, refs[0], slice(None))


def skip_tables(skip, bias, width):
    copies = width // skip.shape[0]
    same = jnp.eye(copies, dtype=bool)[:, None, :, None]
    wide = jnp.where(same, skip[None, :, None, :], jnp.zeros((), skip.dtype))
    return wide.reshape(width, width), jnp.tile(bias, copies).reshape(1, width)


def layer_back(second, third, third_pair, modes, grid, wide_skip, wide_bias, last):
    rows, lanes = grid.shape
    kinds, parts, mode_rows = modes.shape[:3]
    width = wide_skip.shape[0]
    lines = second.shape[0]
    out_specs = [
        pl.BlockSpec((rows, width), lambda i: (0, i)),
        pl.BlockSpec((kinds, parts, lines, width), lambda i: (0, 0, 0, i)),
    ]
    out_shape = [
        jax.ShapeDtypeStruct((rows, lanes), BF16),
        jax.ShapeDtypeStruct((kinds, parts, lines, lanes), BF16),
    ]
    if last:
        out_specs = [
            pl.BlockSpec((rows // 16, width // 128, 16, 128), lambda i: (0, i, 0, 0)),
        ]
        out_shape = [jax.ShapeDtypeStruct((rows // 16, lanes // 128, 16, 128), BF16)]
    return pl.pallas_call(
        layer_body,
        grid=(lanes // width,),
        in_specs=[
            pl.BlockSpec(second.shape, lambda i: (0, 0)),
            pl.BlockSpec(third.shape, lambda i: (0, 0)),
            pl.BlockSpec(third_pair.shape, lambda i: (0, 0)),
            pl.BlockSpec((kinds, parts, mode_rows, width), lambda i: (0, 0, 0, i)),
            pl.BlockSpec((rows, width), lambda i: (0, i)),
            pl.BlockSpec((width, width), lambda i: (0, 0)),
            pl.BlockSpec((1, width), lambda i: (0, 0)),
        ],
        out_specs=out_specs,
        out_shape=out_shape,
        scratch_shapes=[pltpu.VMEM((kinds * parts, lines, width), BF16)],
        compiler_params=pltpu.CompilerParams(vmem_limit_bytes=40 * 1024 * 1024),
        name="layer_back",
    )(second, third, third_pair, modes, grid, wide_skip, wide_bias)


def slot_plan(block_bricks, bricks_device, slot_total, capacity):
    owners = block_bricks[:, 0] // bricks_device
    order_index = jnp.arange(owners.shape[0], dtype=jnp.int32)
    earlier = (owners[None, :] == owners[:, None]) & (order_index[None, :] < order_index[:, None])
    ranking = jnp.sum(earlier.astype(jnp.int32), axis=1)
    slot_index = owners * capacity + ranking
    matching = slot_index[None, :] == jnp.arange(slot_total, dtype=jnp.int32)[:, None]
    present = jnp.any(matching, axis=1)
    sources = jnp.sum(jnp.where(matching, order_index[None, :], 0), axis=1)
    return (slot_index, present, sources)


def unpack_body(places_ref, reply_ref, out_ref):
    def some(turn, carry):
        for way in range(WAYS):
            block = turn * WAYS + way
            out_ref[block] = reply_ref[places_ref[block]]
        return carry

    lax.fori_loop(0, out_ref.shape[0] // WAYS, some, 0)


def unpack_slots(places, reply):
    vmem = pl.BlockSpec(memory_space=pltpu.VMEM)
    return pl.pallas_call(
        unpack_body,
        grid_spec=pltpu.PrefetchScalarGridSpec(
            num_scalar_prefetch=1, grid=(1,), in_specs=[vmem], out_specs=vmem
        ),
        out_shape=jax.ShapeDtypeStruct(places.shape + reply.shape[1:], reply.dtype),
        compiler_params=pltpu.CompilerParams(vmem_limit_bytes=40 * 1024 * 1024),
        name="unpack_slots",
    )(places, reply)


def per_device(
    point_channel_values,
    point_offsets,
    point_counts,
    block_bricks,
    spectral_weights,
    skip_weights,
    skip_bias,
):
    mesh_rows = lax.axis_size("px")
    mesh_columns = lax.axis_size("py")
    device_total = mesh_rows * mesh_columns
    capacity = max(2, 2 * point_channel_values.shape[0] // device_total)
    channels, points = point_channel_values.shape[1:]
    x_dev, y_dev = NX // mesh_rows, NY // mesh_columns
    bricks_y = y_dev // 4
    bricks_z = NZ // 16
    bricks_device = x_dev // 2 * bricks_y * bricks_z
    slot_total = device_total * capacity
    local_ids = block_bricks % bricks_device
    slot_index, present, sources = slot_plan(block_bricks, bricks_device, slot_total, capacity)
    coordinates = jnp.stack(
        [local_ids // (bricks_y * bricks_z), local_ids // bricks_z % bricks_y, local_ids % bricks_z],
        axis=-1,
    ).reshape(local_ids.shape[0], -1)
    facts = jnp.concatenate([coordinates, point_counts[:, None]], axis=1).astype(BF16)
    facts = jnp.pad(facts, ((0, 0), (0, points - facts.shape[1])))
    notes = jnp.concatenate([point_offsets, facts[:, None, :]], axis=1)
    wanted = jnp.where(present, sources, -1)
    tiles, got_notes = route(wanted, notes, point_channel_values)
    got_notes = got_notes[:, : 4 * capacity].reshape((slot_total,) + notes.shape[1:])
    info = got_notes[:, 3, :13].astype(jnp.int32)
    tiles_x, tiles_z = x_dev * channels // 128, NZ // 16
    lift = tiles_z * tiles_x
    spots = info[:, :12].reshape(slot_total, 4, 3)
    bases = (spots[..., 1] * 4 * tiles_z + spots[..., 2]) * tiles_x + spots[..., 0]
    info, bases = info.reshape(-1), bases.reshape(-1)

    kz_dev = MODES // mesh_columns
    ky_dev = MODES // mesh_rows
    parts = 1
    while ky_dev * kz_dev * 2 // (2 * parts) % 16 == 0 and kz_dev % (2 * parts) == 0 and parts < MOST_PARTS:
        parts *= 2
    me_y = lax.axis_index("py")
    index = jnp.arange(2 * MODES, dtype=jnp.int32)
    group_at = jnp.bitwise_xor(index // (2 * kz_dev), me_y)
    kz = index // 2 % kz_dev + kz_dev * group_at
    angle_z = unit_angles(kz[:, None] * jnp.arange(NZ, dtype=jnp.int32)[None, :], NZ)
    third = jnp.where((index % 2 == 0)[:, None], jnp.cos(angle_z), -jnp.sin(angle_z))
    third = third / math.sqrt(NZ)
    fold = jnp.where(kz == 0, 1.0, 2.0).astype(F32)[:, None]
    span = 2 * kz_dev // parts
    slabs = mesh_columns * parts
    third_pair = repeat_lines(third, slabs, 2).astype(BF16)
    third_back = repeat_lines(third * fold, slabs, 16 // span).T.astype(BF16)
    row = jnp.arange(MODES * span, dtype=jnp.int32)[:, None]
    column = jnp.arange(y_dev * span, dtype=jnp.int32)[None, :]
    ky_at = row // span
    ky = jnp.where(ky_at < MODES // 2, ky_at, ky_at - MODES)
    angle_y = unit_angles(ky * (me_y * y_dev + column // span), NY)
    row_part, column_part = row % 2, column % 2
    sine = jnp.where(row_part == 0, jnp.sin(angle_y), -jnp.sin(angle_y))
    second = jnp.where(row_part == column_part, jnp.cos(angle_y), sine) / math.sqrt(NY)
    second = jnp.where(row % span // 2 == column % span // 2, second, 0.0).astype(BF16)
    second_back = second.T
    first_matrix = forward_matrix(NX, wave_numbers(MODES))
    by_pair = first_matrix.reshape(NX // 2, 2, 2, MODES, 2)
    first_forward = by_pair.transpose(1, 3, 4, 2, 0).reshape(4 * MODES, NX).astype(BF16)
    turned = jnp.stack([by_pair[..., 1], -by_pair[..., 0]], axis=-1)
    first_back = jnp.stack([by_pair, turned], axis=0).transpose(2, 0, 3, 1, 4, 5)
    first_back = first_back.reshape(4 * NX, 2 * MODES).astype(BF16)
    lanes = x_dev * channels
    width = math.gcd(lanes // CHUNKS, 4 * channels)
    skips = [skip_tables(skip_weights[at], skip_bias[at], width) for at in range(LAYERS)]
    tables = (third_pair, third_back, second, second_back, first_forward, first_back, skips)
    tiles, tables = lax.optimization_barrier((tiles, tables))
    third_pair, third_back, second, second_back, first_forward, first_back, skips = tables
    grid, third_found = gather_grid(
        bases, tiles, third_pair, y_dev * NZ, lanes, mesh_columns, parts, lift
    )
    for layer in range(LAYERS):
        modes = spectral(
            layer, second, first_forward, first_back, third_found, spectral_weights, parts
        )
        last = layer == LAYERS - 1
        found = layer_back(
            second_back, third_back, third_pair, modes, grid, *skips[layer], last
        )
        grid, third_found = found[0], found[-1]
    grid = grid.reshape(-1, 16, 128)
    reply = decode(info, bases, grid, got_notes, channels, lift)
    return unpack_slots(slot_index, reply)


def solution(mesh):
    return jax.shard_map(
        per_device,
        mesh=mesh,
        in_specs=(
            P(("px", "py"), None, None),
            P(("px", "py"), None, None),
            P(("px", "py")),
            P(("px", "py"), None),
            P(None, None, "px", "py", None, None),
            P(),
            P(),
        ),
        out_specs=P(("px", "py"), None, None),
        check_vma=False,
    )
```

```python
import functools
import math

import jax
import jax.numpy as jnp
import ml_dtypes
import numpy as np
from jax import lax
from jax.experimental import pallas as pl
from jax.experimental.pallas import tpu as pltpu
from jax.sharding import PartitionSpec as P

MODES = 32
NX = 128
NY = 128
NZ = 128
LAYERS = 2

AMPLITUDE = 0.25
SPREAD = 4.5
DECODE_SCALE = 0.1
CHUNKS = 2
MOST_PARTS = 4
WAYS = 4
VMEM_LIMIT = 60 * 1024 * 1024
F32 = jnp.float32
BF16 = jnp.bfloat16


def wave_numbers(kept_modes):
    position = np.arange(kept_modes)
    return np.where(position < kept_modes // 2, position, position - kept_modes)


def forward_matrix(length, frequency):
    angles = 2.0 * math.pi / length * (np.arange(length)[:, None] * frequency[None, :] % length)
    cosine = np.cos(angles) / math.sqrt(length)
    sine_part = np.sin(angles) / math.sqrt(length)
    from_real = np.stack([cosine, -sine_part], axis=-1)
    from_imag = np.stack([sine_part, cosine], axis=-1)
    return np.stack([from_real, from_imag], axis=1)


def unit_angles(products, length):
    return 2.0 * math.pi / length * (products % length)


def repeat_lines(table, slabs, copies):
    rows, depth = table.shape
    span = rows // slabs
    same = np.eye(copies, dtype=bool)[None, :, None, :, None]
    wide = np.where(same, table.reshape(slabs, 1, span, 1, depth), 0.0)
    return wide.reshape(rows * copies, copies * depth)


def constant(table):
    return jnp.asarray(np.asarray(table).astype(ml_dtypes.bfloat16))


def third_tables(kinds, parts, me_y):
    kz_dev = MODES // kinds
    index = np.arange(2 * MODES)
    kz = index // 2 % kz_dev + kz_dev * (index // (2 * kz_dev) ^ me_y)
    angle = unit_angles(kz[:, None] * np.arange(NZ)[None, :], NZ)
    third = np.where((index % 2 == 0)[:, None], np.cos(angle), -np.sin(angle)) / math.sqrt(NZ)
    fold = np.where(kz == 0, 1.0, 2.0)[:, None]
    span = 2 * kz_dev // parts
    return (
        repeat_lines(third, kinds * parts, 2),
        repeat_lines(third * fold, kinds * parts, 16 // span).T,
    )


def second_table(kinds, parts, me_y):
    span = 2 * MODES // kinds // parts
    y_dev = NY // kinds
    row = np.arange(MODES * span)[:, None]
    column = np.arange(y_dev * span)[None, :]
    ky = wave_numbers(MODES)[row // span]
    angle = unit_angles(ky * (me_y * y_dev + column // span), NY)
    sine = np.where(row % 2 == 0, np.sin(angle), -np.sin(angle))
    second = np.where(row % 2 == column % 2, np.cos(angle), sine) / math.sqrt(NY)
    return np.where(row % span // 2 == column % span // 2, second, 0.0)


def all_tables(kinds, parts):
    third = [third_tables(kinds, parts, me_y) for me_y in range(kinds)]
    second = np.stack([second_table(kinds, parts, me_y) for me_y in range(kinds)])
    by_pair = forward_matrix(NX, wave_numbers(MODES)).reshape(NX // 2, 2, 2, MODES, 2)
    first_forward = by_pair.transpose(1, 3, 4, 2, 0).reshape(4 * MODES, NX)
    turned = np.stack([by_pair[..., 1], -by_pair[..., 0]], axis=-1)
    first_back = np.stack([by_pair, turned], axis=0).transpose(2, 0, 3, 1, 4, 5)
    return [
        constant(table)
        for table in (
            np.stack([one[0] for one in third]),
            np.stack([one[1] for one in third]),
            second,
            second.transpose(0, 2, 1),
            first_forward,
            first_back.reshape(4 * NX, 2 * MODES),
        )
    ]


def gelu(value):
    return 0.5 * value * (1.0 + lax.erf(value * math.sqrt(0.5)))


def block_values(offsets, shift_of, count, points):
    lanes = lax.broadcasted_iota(jnp.int32, (1, points), 1).astype(F32)
    amplitude = jnp.where(lanes < count, AMPLITUDE, 0.0).astype(F32)

    def part(dim, brick, cells, scale):
        center = lax.broadcasted_iota(jnp.int32, (cells, points), 0).astype(F32) + 0.5
        apart = (offsets[dim : dim + 1, :] - shift_of(dim, brick) * scale) - center
        return jnp.exp(apart * apart * (-1.0 / SPREAD))

    rows = []
    for brick in range(4):
        along_x = part(0, brick, 2, 2.0) * amplitude
        along_y = part(1, brick, 4, 4.0)
        along_z = part(2, brick, 16, 16.0)
        for cy in range(4):
            plane = along_z * along_y[cy : cy + 1, :]
            rows.append(
                jnp.concatenate(
                    [plane * along_x[0:1, :], plane * along_x[1:2, :]], axis=1
                ).astype(BF16)
            )
    return jnp.concatenate(rows, axis=0)


def note_values(notes, slot, points):
    facts = notes[4 * slot + 3 : 4 * slot + 4, :]
    return block_values(
        notes[4 * slot : 4 * slot + 3, :],
        lambda dim, brick: facts[:, 3 * brick + dim : 3 * brick + dim + 1]
        - facts[:, dim : dim + 1],
        facts[:, 12:13],
        points,
    )


def bits(size):
    return size.bit_length() - 1


def plan_body(bricks_y, bricks_z, capacity, brick_ref, count_ref, wanted_ref, place_ref, fact_ref):
    blocks = brick_ref.shape[0]
    slots = wanted_ref.shape[1]
    bricks_device = bricks_y[1]
    bricks_y = bricks_y[0]
    brick = brick_ref[...]
    down = lax.broadcasted_iota(jnp.int32, (blocks, blocks), 0)
    across = lax.broadcasted_iota(jnp.int32, (blocks, blocks), 1)
    owner_column = lax.shift_right_logical(brick[:, 0:1], jnp.int32(bits(bricks_device)))
    diagonal = down == across
    owner_row = jnp.sum(jnp.where(diagonal, owner_column, 0), axis=0, keepdims=True)
    same = owner_column == owner_row
    rank_row = jnp.sum(jnp.where(same & (down < across), 1, 0), axis=0, keepdims=True)
    rank_column = jnp.sum(jnp.where(same & (across < down), 1, 0), axis=1, keepdims=True)
    place_ref[...] = owner_row * capacity + rank_row
    slot = owner_column * capacity + rank_column
    slot_at = lax.broadcasted_iota(jnp.int32, (blocks, slots), 1)
    block_at = lax.broadcasted_iota(jnp.int32, (blocks, slots), 0) + 1
    wanted_ref[...] = jnp.sum(jnp.where(slot == slot_at, block_at, 0), axis=0, keepdims=True) - 1
    local = brick & (bricks_device - 1)
    parts = (
        lax.shift_right_logical(local, jnp.int32(bits(bricks_y * bricks_z))),
        lax.shift_right_logical(local, jnp.int32(bits(bricks_z))) & (bricks_y - 1),
        local & (bricks_z - 1),
    )
    count = jnp.sum(jnp.where(diagonal, count_ref[...], 0), axis=1, keepdims=True)
    lane = lax.broadcasted_iota(jnp.int32, (blocks, fact_ref.shape[2]), 1)
    facts = jnp.where(lane == 12, count, 0)
    for at in range(4):
        for dim in range(3):
            facts = jnp.where(lane == 3 * at + dim, parts[dim][:, at : at + 1], facts)
    fact_ref[...] = facts.astype(F32).reshape(fact_ref.shape)


def make_plan(bricks, counts, bricks_device, bricks_y, bricks_z, capacity, slots, points):
    blocks = bricks.shape[0]
    vmem = pl.BlockSpec(memory_space=pltpu.VMEM)
    return pl.pallas_call(
        functools.partial(plan_body, (bricks_y, bricks_device), bricks_z, capacity),
        in_specs=[vmem] * 2,
        out_specs=[vmem] * 3,
        out_shape=[
            jax.ShapeDtypeStruct((1, slots), jnp.int32),
            jax.ShapeDtypeStruct((1, blocks), jnp.int32),
            jax.ShapeDtypeStruct((blocks, 1, points), F32),
        ],
        name="make_plan",
    )(bricks, counts.reshape(1, blocks))


def spot_body(tiles_x, tiles_z, note_ref, base_ref, wide_ref):
    wide_ref[...] = note_ref[...].reshape(wide_ref.shape).astype(F32)
    facts = wide_ref[pl.ds(3, wide_ref.shape[0] // 4, stride=4), :].T
    rows = []
    for at in range(4):
        cell_x, cell_y, cell_z = (facts[3 * at + dim : 3 * at + dim + 1, :] for dim in range(3))
        rows.append((cell_y * (4 * tiles_z) + cell_z) * tiles_x + cell_x)
    base_ref[...] = jnp.concatenate(rows, axis=0).astype(jnp.int32)


def find_spots(notes, tiles_x, tiles_z):
    rows = notes.shape[0] * notes.shape[1]
    vmem = pl.BlockSpec(memory_space=pltpu.VMEM)
    return pl.pallas_call(
        functools.partial(spot_body, tiles_x, tiles_z),
        in_specs=[vmem],
        out_specs=vmem,
        out_shape=jax.ShapeDtypeStruct((4, rows // 4), jnp.int32),
        scratch_shapes=[pltpu.VMEM((rows, notes.shape[2]), F32)],
        name="find_spots",
    )(notes)


def mask_at(turn, devices):
    return (turn * ((13 * devices // 32) | 1)) % devices


def crossed(value, mask, size):
    result, bit = 0, 1
    while bit < size:
        result = result + bit * ((value // bit + mask // bit) % 2)
        bit *= 2
    return result


def route_body(
    size_x,
    size_y,
    source_ref,
    offset_ref,
    fact_ref,
    feature_ref,
    tile_ref,
    got_note_ref,
    feature_send,
    feature_got,
    note_send,
    tile_held,
    feature_ssem,
    feature_rsem,
    note_ssem,
    note_rsem,
    tile_sem,
):
    slots, channels, points = feature_send.shape
    devices = size_x * size_y
    capacity = slots // devices
    ways = math.gcd(WAYS, capacity)
    note_rows = note_send.shape[1]
    me = lax.axis_index("px") * size_y + lax.axis_index("py")
    barrier = pltpu.get_barrier_semaphore()

    def greet(mask, carry):
        other = crossed(me, mask, devices)
        pl.semaphore_signal(
            barrier,
            inc=1,
            device_id={"px": other // size_y, "py": other % size_y},
            device_id_type=pl.DeviceIdType.MESH,
        )
        return carry

    lax.fori_loop(1, devices, greet, 0)

    def transfers(mask):
        other = crossed(me, mask, devices)
        there = {"px": other // size_y, "py": other % size_y}
        return (
            pltpu.make_async_remote_copy(
                src_ref=note_send.at[other],
                dst_ref=got_note_ref.at[me],
                send_sem=note_ssem.at[mask],
                recv_sem=note_rsem.at[mask],
                device_id=there,
                device_id_type=pl.DeviceIdType.MESH,
            ),
            pltpu.make_async_remote_copy(
                src_ref=feature_send.at[pl.ds(other * capacity, capacity)],
                dst_ref=feature_got.at[pl.ds(me * capacity, capacity)],
                send_sem=feature_ssem.at[mask],
                recv_sem=feature_rsem.at[mask],
                device_id=there,
                device_id_type=pl.DeviceIdType.MESH,
            ),
        )

    def pack(other, notes_to, features_to):
        notes = []
        for slot in range(capacity):
            source = source_ref[0, other * capacity + slot]
            present = source >= 0
            source = jnp.maximum(source, 0)
            feature = feature_ref[source]
            features_to[other * capacity + slot] = jnp.where(
                present, feature, jnp.zeros_like(feature)
            )
            note = jnp.concatenate([offset_ref[source].astype(F32), fact_ref[source]], axis=0)
            notes.append(jnp.where(present, note, 0.0))
        if note_rows > 4 * capacity:
            notes.append(jnp.zeros((note_rows - 4 * capacity, points), F32))
        notes_to[other] = jnp.concatenate(notes, axis=0).astype(BF16)

    first = mask_at(1, devices)
    pack(crossed(me, first, devices), note_send, feature_send)
    pl.semaphore_wait(barrier, devices - 1)
    for copy in transfers(first):
        copy.start()

    def launch(turn, carry):
        mask = mask_at(turn, devices)
        pack(crossed(me, mask, devices), note_send, feature_send)
        for copy in transfers(mask):
            copy.start()
        return carry

    lax.fori_loop(2, devices, launch, 0)
    pack(me, got_note_ref, feature_got)

    def tile_copy(turn, other):
        return pltpu.make_async_copy(
            tile_held.at[turn % 2],
            tile_ref.at[pl.ds(other * capacity, capacity)],
            tile_sem.at[turn % 2],
        )

    def work(turn, other):
        notes = got_note_ref[other].astype(F32)
        for start in range(0, capacity, ways):
            tiles = []
            for slot in range(start, start + ways):
                values = note_values(notes, slot, points)
                feature = feature_got[other * capacity + slot]
                empty = jnp.zeros_like(feature)
                pair = jnp.concatenate(
                    [
                        jnp.concatenate([feature, empty], axis=1),
                        jnp.concatenate([empty, feature], axis=1),
                    ],
                    axis=0,
                )
                tiles.append(
                    lax.dot_general(
                        values, pair, (((1,), (1,)), ((), ())), preferred_element_type=F32
                    ).astype(BF16)
                )
            for way in range(ways):
                tile_held[turn % 2, start + way] = tiles[way]
        tile_copy(turn, other).start()

    work(0, me)

    def step(turn, carry):
        mask = mask_at(turn, devices)
        for copy in transfers(mask):
            copy.wait_recv()

        @pl.when(turn >= 2)
        def _():
            tile_copy(turn, me).wait()

        work(turn, crossed(me, mask, devices))
        return carry

    lax.fori_loop(1, devices, step, 0)
    for turn in range(devices - 2, devices):
        tile_copy(turn, me).wait()

    def leave(mask, carry):
        for copy in transfers(mask):
            copy.wait_send()
        return carry

    lax.fori_loop(1, devices, leave, 0)


def route(sources, offsets, facts, features):
    slots = sources.shape[1]
    channels, points = features.shape[1:]
    size_x, size_y = lax.axis_size("px"), lax.axis_size("py")
    devices = size_x * size_y
    capacity = slots // devices
    note_rows = (4 * capacity + 15) // 16 * 16
    vmem = pl.BlockSpec(memory_space=pltpu.VMEM)
    dma = pltpu.SemaphoreType.DMA
    return pl.pallas_call(
        functools.partial(route_body, size_x, size_y),
        in_specs=[pl.BlockSpec(memory_space=pltpu.SMEM), vmem, vmem, vmem],
        out_specs=[pl.BlockSpec(memory_space=pl.ANY), vmem],
        out_shape=[
            jax.ShapeDtypeStruct((slots, 256, 2 * channels), BF16),
            jax.ShapeDtypeStruct((devices, note_rows, points), BF16),
        ],
        scratch_shapes=[
            pltpu.VMEM((slots, channels, points), BF16),
            pltpu.VMEM((slots, channels, points), BF16),
            pltpu.VMEM((devices, note_rows, points), BF16),
            pltpu.VMEM((2, capacity, 256, 2 * channels), BF16),
            dma((devices,)),
            dma((devices,)),
            dma((devices,)),
            dma((devices,)),
            dma((2,)),
        ],
        compiler_params=pltpu.CompilerParams(
            vmem_limit_bytes=VMEM_LIMIT, collective_id=LAYERS + 1, has_side_effects=True
        ),
        name="route",
    )(sources, offsets, facts, features)


def find_third(third_ref, lines_of, out_ref, columns):
    kinds, parts, lines = out_ref.shape[:3]
    both = third_ref.shape[0]
    span = both // (2 * kinds * parts)
    turns = 16 // (2 * span)

    def some(turn, carry):
        found = [
            jnp.dot(third_ref[...], lines_of(turn * turns + way), preferred_element_type=F32)
            for way in range(turns)
        ]
        row = pl.multiple_of(turn * 16, 16)
        for slab in range(kinds * parts):
            piece = [one[slab * 2 * span : (slab + 1) * 2 * span, :] for one in found]
            piece = piece[0] if turns == 1 else jnp.concatenate(piece, axis=0)
            out_ref[slab // parts, slab % parts, pl.ds(row, 16), columns] = piece.astype(BF16)
        return carry

    lax.fori_loop(0, lines // 16, some, 0, unroll=2)


def gather_body(
    group, steps, lift, capacity, base_ref, me_ref, tile_ref, third_ref, out_ref, modes_ref, total_ref
):
    step = pl.program_id(0)
    lanes = out_ref.shape[1]
    depth = third_ref.shape[2] // 2
    tiles = lanes // 128

    @pl.when(step == 0)
    def _():
        total_ref[...] = jnp.zeros_like(total_ref)

    def some(turn, carry):
        for way in range(WAYS):
            member = turn * WAYS + way
            slot = step * group + member
            room = base_ref.shape[1] * capacity // (steps * group)
            spot = slot if room == capacity else slot // capacity * room + slot % capacity
            bases = [base_ref[brick, spot] for brick in range(4)]
            places = [base + cy * lift for base in bases for cy in range(4)]
            sums = [
                total_ref[place] + tile_ref[member, 16 * at : 16 * at + 16, :].astype(F32)
                for at, place in enumerate(places)
            ]
            for place, value in zip(places, sums):
                total_ref[place] = value
        return carry

    lax.fori_loop(0, group // WAYS, some, 0)

    @pl.when(step == steps - 1)
    def _():
        width = math.gcd(lanes, 256)
        pieces = width // 128

        def tile(turn, carry):
            columns = pl.ds(pl.multiple_of(turn * width, width), width)

            def lines_of(pair):
                place = pl.ds(pl.multiple_of(pair * 2 * depth, 2 * depth), 2 * depth)
                rows = []
                for at in range(2 * depth // 16):
                    here = (pair * (2 * depth // 16) + at) * tiles + turn * pieces
                    rows.append(
                        jnp.concatenate([total_ref[here + to] for to in range(pieces)], axis=1)
                    )
                value = jnp.concatenate(rows, axis=0).astype(BF16)
                out_ref[place, columns] = value
                return value

            find_third(third_ref.at[0], lines_of, modes_ref, columns)
            return carry

        lax.fori_loop(0, lanes // width, tile, 0)


def gather_grid(bases, me, tiles, third_pair, rows, lanes, kinds, parts, lift, capacity):
    slots = tiles.shape[0]
    group = math.gcd(slots, 16)
    depth = third_pair.shape[2] // 2
    lines = rows // depth * third_pair.shape[1] // (2 * kinds * parts)
    return pl.pallas_call(
        functools.partial(gather_body, group, slots // group, lift, capacity),
        grid_spec=pltpu.PrefetchScalarGridSpec(
            num_scalar_prefetch=2,
            grid=(slots // group,),
            in_specs=[
                pl.BlockSpec((group,) + tiles.shape[1:], lambda i, base, me: (i, 0, 0)),
                pl.BlockSpec((1,) + third_pair.shape[1:], lambda i, base, me: (me[0], 0, 0)),
            ],
            out_specs=[
                pl.BlockSpec((rows, lanes), lambda i, base, me: (0, 0)),
                pl.BlockSpec((kinds, parts, lines, lanes), lambda i, base, me: (0, 0, 0, 0)),
            ],
            scratch_shapes=[pltpu.VMEM((rows * lanes // 2048, 16, 128), F32)],
        ),
        out_shape=[
            jax.ShapeDtypeStruct((rows, lanes), BF16),
            jax.ShapeDtypeStruct((kinds, parts, lines, lanes), BF16),
        ],
        compiler_params=pltpu.CompilerParams(vmem_limit_bytes=46 * 1024 * 1024),
        name="gather_grid",
    )(bases, me, tiles, third_pair)


def decode_body(size_x, size_y, lift, base_ref, held_ref, note_ref, got_ref, reply_ref, ssem, rsem, own_sem):
    slots, channels, points = got_ref.shape
    devices = size_x * size_y
    capacity = slots // devices
    ways = math.gcd(WAYS, capacity)
    me_x, me_y = lax.axis_index("px"), lax.axis_index("py")
    me = me_x * size_y + me_y
    barrier = pltpu.get_barrier_semaphore()

    def greet(mask, carry):
        other = crossed(me, mask, devices)
        pl.semaphore_signal(
            barrier,
            inc=1,
            device_id={"px": other // size_y, "py": other % size_y},
            device_id_type=pl.DeviceIdType.MESH,
        )
        return carry

    lax.fori_loop(1, devices, greet, 0)

    def transfer(mask):
        other = crossed(me, mask, devices)
        return pltpu.make_async_remote_copy(
            src_ref=reply_ref.at[pl.ds(other * capacity, capacity)],
            dst_ref=got_ref.at[pl.ds(me * capacity, capacity)],
            send_sem=ssem.at[mask],
            recv_sem=rsem.at[mask],
            device_id={"px": other // size_y, "py": other % size_y},
            device_id_type=pl.DeviceIdType.MESH,
        )

    room = base_ref.shape[1] // devices

    def fill(other):
        notes = note_ref[other].astype(F32)
        for start in range(0, capacity, ways):
            results = []
            for slot in range(start, start + ways):
                values = note_values(notes, slot, points)
                bases = [base_ref[brick, other * room + slot] for brick in range(4)]
                cells = jnp.concatenate(
                    [held_ref[base + cy * lift] for base in bases for cy in range(4)], axis=0
                )
                both = lax.dot_general(
                    cells, values, (((0,), (0,)), ((), ())), preferred_element_type=F32
                )
                summed = both[:channels, :points] + both[channels:, points:]
                results.append((DECODE_SCALE * summed).astype(BF16))
            for way in range(ways):
                reply_ref[other * capacity + start + way] = results[way]

    first = mask_at(1, devices)
    fill(crossed(me, first, devices))
    pl.semaphore_wait(barrier, devices - 1)
    transfer(first).start()

    def step(turn, carry):
        mask = mask_at(turn, devices)
        fill(crossed(me, mask, devices))
        transfer(mask).start()
        return carry

    lax.fori_loop(2, devices, step, 0)
    fill(me)
    mine = pl.ds(me * capacity, capacity)
    own = pltpu.make_async_copy(reply_ref.at[mine], got_ref.at[mine], own_sem)
    own.start()
    own.wait()

    def finish(mask, carry):
        transfer(mask).wait_recv()
        return carry

    lax.fori_loop(1, devices, finish, 0)

    def leave(mask, carry):
        transfer(mask).wait_send()
        return carry

    lax.fori_loop(1, devices, leave, 0)


def decode(bases, grid, notes, slots, channels, lift):
    points = notes.shape[2]
    size_x, size_y = lax.axis_size("px"), lax.axis_size("py")
    devices = size_x * size_y
    vmem = pl.BlockSpec(memory_space=pltpu.VMEM)
    return pl.pallas_call(
        functools.partial(decode_body, size_x, size_y, lift),
        in_specs=[pl.BlockSpec(memory_space=pltpu.SMEM), vmem, vmem],
        out_specs=vmem,
        out_shape=jax.ShapeDtypeStruct((slots, channels, points), BF16),
        scratch_shapes=[
            pltpu.VMEM((slots, channels, points), BF16),
            pltpu.SemaphoreType.DMA((devices,)),
            pltpu.SemaphoreType.DMA((devices,)),
            pltpu.SemaphoreType.DMA,
        ],
        compiler_params=pltpu.CompilerParams(
            vmem_limit_bytes=24 * 1024 * 1024, collective_id=LAYERS, has_side_effects=True
        ),
        name="decode",
    )(bases, grid, notes)


def partner(me, distance):
    return me + distance - 2 * distance * ((me // distance) % 2)


def spectral_body(
    layer,
    second_ref,
    forward_ref,
    backward_ref,
    third_ref,
    weight_ref,
    modes_ref,
    held_ref,
    sums_send,
    sums_recv,
    lines_send,
    lines_recv,
    back_send,
    weight_held,
    wide_in,
    wide_out,
    sums_ssem,
    sums_rsem,
    lines_ssem,
    lines_rsem,
    back_ssem,
    back_rsem,
    modes_ssem,
    modes_rsem,
    weight_sem,
):
    kinds, parts, rows, lanes = modes_ref.shape
    devices_x, slab_rows = lines_send.shape[1:3]
    pairs_x = lanes // 128
    channels = weight_held.shape[4]
    kz_part = weight_held.shape[3]
    kx_all = weight_held.shape[1]
    me_x, me_y = lax.axis_index("px"), lax.axis_index("py")
    steps = kinds.bit_length() - 1
    tile = math.gcd(lanes, 256)
    lane_tiles = lanes // tile
    batch = 8
    weight_copies = []
    for part in range(parts):
        copy = pltpu.make_async_copy(
            weight_ref.at[layer, :, :, pl.ds(part * kz_part, kz_part)],
            weight_held.at[part],
            weight_sem.at[part],
        )
        copy.start()
        weight_copies.append(copy)

    def at_x(device):
        return {"px": device}

    def at_y(distance):
        return {"py": partner(me_y, distance)}

    barrier = pltpu.get_barrier_semaphore()
    for hop in range(1, devices_x):
        pl.semaphore_signal(
            barrier,
            inc=1,
            device_id=at_x((me_x + hop) % devices_x),
            device_id_type=pl.DeviceIdType.MESH,
        )
    for step in range(steps):
        pl.semaphore_signal(
            barrier, inc=1, device_id=at_y(1 << step), device_id_type=pl.DeviceIdType.MESH
        )

    started = []

    def send(source, target, ssem, rsem, device):
        copy = pltpu.make_async_remote_copy(
            src_ref=source,
            dst_ref=target,
            send_sem=ssem,
            recv_sem=rsem,
            device_id=device,
            device_id_type=pl.DeviceIdType.MESH,
        )
        copy.start()
        started.append(copy)
        return copy

    bases = [kinds - (kinds >> step) for step in range(steps)]
    sums_copies, lines_copies, back_copies, modes_copies = {}, {}, {}, {}

    def send_sums(part, step):
        count = kinds >> (step + 1)
        at = pl.ds(bases[step], count)
        sums_copies[part, step] = send(
            sums_send.at[part, at],
            sums_recv.at[part, at],
            sums_ssem.at[part, step],
            sums_rsem.at[part, step],
            at_y(1 << step),
        )

    def second_stage(part):
        def one(turn, carry):
            columns = pl.ds(pl.multiple_of(turn * tile, tile), tile)
            for kind in range(kinds - 1, -1, -1):
                value = jnp.dot(
                    second_ref[me_y], third_ref[kind, part, :, columns], preferred_element_type=F32
                )
                if kind % 2:
                    sums_send[part, kind // 2, :, columns] = value.astype(BF16)
                else:
                    held_ref[part, kind // 2, :, columns] = value
            return carry

        lax.fori_loop(0, lane_tiles, one, 0)
        send_sums(part, 0)

    def sum_stage(part, step):
        sums_copies[part, step].wait_recv()

        def one(turn, carry):
            columns = pl.ds(pl.multiple_of(turn * tile, tile), tile)
            for index in range(kinds >> (step + 1)):
                kind = index << (step + 1)
                value = held_ref[part, kind // 2, :, columns] + sums_recv[
                    part, bases[step] + index, :, columns
                ].astype(F32)
                if index % 2:
                    sums_send[part, bases[step + 1] + index // 2, :, columns] = value.astype(BF16)
                elif step + 1 < steps:
                    held_ref[part, kind // 2, :, columns] = value
                else:
                    lines_send[part, :, :, columns] = value.astype(BF16).reshape(
                        devices_x, slab_rows, tile
                    )
            return carry

        lax.fori_loop(0, lane_tiles, one, 0)
        if step + 1 < steps:
            send_sums(part, step + 1)
            return
        for hop in range(1, devices_x):
            target = (me_x + hop) % devices_x
            lines_copies[part, hop] = send(
                lines_send.at[part, target],
                lines_recv.at[part, me_x],
                lines_ssem.at[part, hop],
                lines_rsem.at[part, hop],
                at_x(target),
            )
        lines_recv[part, me_x] = lines_send[part, me_x]

    half_lane = lax.broadcasted_iota(jnp.int32, (1, 128), 1) < channels

    def mix_stage(part):
        for hop in range(1, devices_x):
            lines_copies[part, hop].wait_recv()
        weight_copies[part].wait()

        def widen(source, carry):
            for pair in range(pairs_x):
                row = pl.multiple_of((source * pairs_x + pair) * slab_rows, slab_rows)
                wide_in[pl.ds(row, slab_rows), :] = lines_recv[
                    part, source, :, pair * 128 : (pair + 1) * 128
                ].astype(F32)
            return carry

        lax.fori_loop(0, devices_x, widen, 0)
        count = devices_x * pairs_x
        modes_rows = 2 * kx_all
        row_at = lax.broadcasted_iota(jnp.int32, (modes_rows, batch * channels), 0)
        lane_at = lax.broadcasted_iota(jnp.int32, (modes_rows, batch * channels), 1)
        own = (row_at // 2) % batch == lane_at // channels

        def one(pick, carry):
            ky, kz = pick // kz_part, pick % kz_part
            line = jnp.concatenate(
                [
                    wide_in[pl.ds(2 * pick, count, stride=slab_rows), :],
                    wide_in[pl.ds(2 * pick + 1, count, stride=slab_rows), :],
                ],
                axis=0,
            ).astype(BF16)
            first = jnp.dot(forward_ref[...], line, preferred_element_type=F32)
            first = jnp.where(half_lane, first[:modes_rows], first[modes_rows:])
            first = first + pltpu.roll(first, channels, 1)
            spread = jnp.where(own, jnp.concatenate([first] * (batch // 2), axis=1), 0.0)
            spread = spread.astype(BF16)
            mixed = []
            for at in range(kx_all // batch):
                weight = weight_held[part, at * batch : (at + 1) * batch, ky, kz]
                mixed.append(
                    jnp.dot(
                        spread[2 * at * batch : 2 * (at + 1) * batch],
                        weight.reshape(batch * channels, 2 * channels),
                        preferred_element_type=F32,
                    )
                )
            mixed = jnp.concatenate(mixed, axis=0).astype(BF16)
            back = jnp.dot(backward_ref[...], mixed, preferred_element_type=F32)
            size = 2 * count
            part_at = [back[at * size : (at + 1) * size] for at in range(4)]
            final = jnp.where(half_lane, part_at[0], part_at[3]) + pltpu.roll(
                jnp.where(half_lane, part_at[2], part_at[1]), channels, 1
            )
            wide_out[pl.ds(2 * pick, count, stride=slab_rows), :] = final[:count]
            wide_out[pl.ds(2 * pick + 1, count, stride=slab_rows), :] = final[count:]
            return carry

        lax.fori_loop(0, slab_rows // 2, one, 0)

        def narrow(target, carry):
            for pair in range(pairs_x):
                row = pl.multiple_of((target * pairs_x + pair) * slab_rows, slab_rows)
                back_send[part, target, :, pair * 128 : (pair + 1) * 128] = wide_out[
                    pl.ds(row, slab_rows), :
                ].astype(BF16)
            return carry

        lax.fori_loop(0, devices_x, narrow, 0)
        mine = pl.ds(pl.multiple_of(me_x * slab_rows, slab_rows), slab_rows)
        for hop in range(1, devices_x):
            target = (me_x + hop) % devices_x
            back_copies[part, hop] = send(
                back_send.at[part, target],
                modes_ref.at[0, part, mine],
                back_ssem.at[part, hop],
                back_rsem.at[part, hop],
                at_x(target),
            )
        modes_ref[0, part, mine, :] = back_send[part, me_x]

    def spread_stage(part, kind):
        if kind == 0:
            for hop in range(1, devices_x):
                back_copies[part, hop].wait_recv()
            limit = kinds
        else:
            modes_copies[part, kind].wait_recv()
            limit = kind & -kind
        distance = limit // 2
        while distance >= 1:
            modes_copies[part, kind + distance] = send(
                modes_ref.at[kind, part],
                modes_ref.at[kind + distance, part],
                modes_ssem.at[part, kind + distance],
                modes_rsem.at[part, kind + distance],
                at_y(distance),
            )
            distance //= 2

    order = []
    for part in range(parts):
        order.append((1.5 * part, second_stage, (part,)))
        for step in range(steps):
            order.append((1.5 * part + 3.0 if step == 0 else 12.0 * step + 5.0 * part, sum_stage, (part, step)))
        base = 12.0 * (steps - 1) + 5.0 * part
        order.append((base + 7.1, mix_stage, (part,)))
        order.append((base + 19.2, spread_stage, (part, 0)))
        level = kinds // 2
        while level >= 1:
            for kind in range(level, kinds, 2 * level):
                late = 6.0 * (kinds // level).bit_length()
                order.append((base + 19.3 + late, spread_stage, (part, kind)))
            level //= 2
    order.sort(key=lambda entry: entry[0])
    waited = False
    for _, stage, given in order:
        stage_first = stage is second_stage and given == (0,)
        if stage_first and not waited:
            pl.semaphore_wait(barrier, devices_x - 1 + steps)
            waited = True
        stage(*given)
    for copy in started:
        copy.wait_send()


def spectral(layer, second, first_forward, first_back, third, weights, parts):
    kinds, _, lines, lanes = third.shape
    rows = second.shape[1]
    devices_x = lax.axis_size("px")
    slab_rows = rows // devices_x
    _, kx_all, ky_dev, kz_dev, channels, wide = weights.shape
    steps = kinds.bit_length() - 1
    count = devices_x * lanes // 128 * slab_rows
    dma = pltpu.SemaphoreType.DMA
    return pl.pallas_call(
        functools.partial(spectral_body, layer),
        in_specs=[pl.BlockSpec(memory_space=pltpu.VMEM)] * 4 + [pl.BlockSpec(memory_space=pl.ANY)],
        out_specs=pl.BlockSpec(memory_space=pltpu.VMEM),
        out_shape=jax.ShapeDtypeStruct((kinds, parts, rows, lanes), BF16),
        scratch_shapes=[
            pltpu.VMEM((parts, kinds // 2, rows, lanes), F32),
            pltpu.VMEM((parts, kinds - 1, rows, lanes), BF16),
            pltpu.VMEM((parts, kinds - 1, rows, lanes), BF16),
            pltpu.VMEM((parts, devices_x, slab_rows, lanes), BF16),
            pltpu.VMEM((parts, devices_x, slab_rows, lanes), BF16),
            pltpu.VMEM((parts, devices_x, slab_rows, lanes), BF16),
            pltpu.VMEM((parts, kx_all, ky_dev, kz_dev // parts, channels, wide), BF16),
            pltpu.VMEM((count, 128), F32),
            pltpu.VMEM((count, 128), F32),
            dma((parts, steps)),
            dma((parts, steps)),
            dma((parts, devices_x)),
            dma((parts, devices_x)),
            dma((parts, devices_x)),
            dma((parts, devices_x)),
            dma((parts, kinds)),
            dma((parts, kinds)),
            dma((parts,)),
        ],
        compiler_params=pltpu.CompilerParams(
            vmem_limit_bytes=35 * 1024 * 1024, collective_id=layer, has_side_effects=True
        ),
        name="spectral",
    )(second, first_forward, first_back, third, weights)


def layer_body(
    layer,
    me_ref,
    second_ref,
    third_ref,
    pair_ref,
    modes_ref,
    grid_ref,
    skip_ref,
    bias_ref,
    out_ref,
    *refs,
):
    held_ref, wide_ref = refs[-2:]
    tiled = len(out_ref.shape) == 4
    kinds, parts = modes_ref.shape[:2]
    slabs = kinds * parts
    lines = second_ref.shape[1]
    block = third_ref.shape[1]
    copies = wide_ref.shape[0] // skip_ref.shape[1]
    bias = jnp.concatenate([bias_ref[layer : layer + 1, :]] * copies, axis=1)

    @pl.when(pl.program_id(0) == 0)
    def _():
        skip = jnp.concatenate([skip_ref[layer].astype(F32)] * copies, axis=1)
        skip = jnp.concatenate([skip] * copies, axis=0)
        at_row = lax.broadcasted_iota(jnp.int32, wide_ref.shape, 0) // skip_ref.shape[1]
        at_lane = lax.broadcasted_iota(jnp.int32, wide_ref.shape, 1) // skip_ref.shape[1]
        wide_ref[...] = jnp.where(at_row == at_lane, skip, 0.0).astype(BF16)

    for slab in range(slabs):
        held_ref[slab] = jnp.dot(
            second_ref[0],
            modes_ref[slab // parts, slab % parts],
            preferred_element_type=F32,
        ).astype(BF16)

    def some(turn, carry):
        row = pl.ds(pl.multiple_of(turn * 16, 16), 16)
        line = jnp.concatenate([held_ref[slab, row, :] for slab in range(slabs)], axis=0)
        for way in range(block // 128):
            place = pl.ds(pl.multiple_of(turn * block + way * 128, 128), 128)
            spectral_part = jnp.dot(
                third_ref[0, way * 128 : (way + 1) * 128, :], line, preferred_element_type=F32
            )
            skipped = jnp.dot(grid_ref[place, :], wide_ref[...], preferred_element_type=F32)
            value = gelu(spectral_part + skipped + bias).astype(BF16)
            if tiled:
                row_tiles = pl.ds(turn * (block // 16) + way * 8, 8)
                for at in range(out_ref.shape[1]):
                    piece = value[:, at * 128 : (at + 1) * 128]
                    out_ref[row_tiles, at] = piece.reshape(8, 16, 128)
            else:
                out_ref[place, :] = value
        return carry

    lax.fori_loop(0, lines // 16, some, 0)
    if not tiled:
        pair = pair_ref.shape[2]

        def lines_of(at):
            return out_ref[pl.ds(pl.multiple_of(at * pair, pair), pair), :]

        find_third(pair_ref.at[0], lines_of, refs[0], slice(None))


def layer_back(layer, me, second, third, third_pair, modes, grid, skips, biases):
    rows, lanes = grid.shape
    kinds, parts, mode_rows = modes.shape[:3]
    width = math.gcd(lanes, 4 * skips.shape[1])
    lines = second.shape[1]

    def mine(table):
        return pl.BlockSpec((1,) + table.shape[1:], lambda i, me: (me[0], 0, 0))

    if layer == LAYERS - 1:
        out_specs = [
            pl.BlockSpec((rows // 16, width // 128, 16, 128), lambda i, me: (0, i, 0, 0)),
        ]
        out_shape = [jax.ShapeDtypeStruct((rows // 16, lanes // 128, 16, 128), BF16)]
    else:
        out_specs = [
            pl.BlockSpec((rows, width), lambda i, me: (0, i)),
            pl.BlockSpec((kinds, parts, lines, width), lambda i, me: (0, 0, 0, i)),
        ]
        out_shape = [
            jax.ShapeDtypeStruct((rows, lanes), BF16),
            jax.ShapeDtypeStruct((kinds, parts, lines, lanes), BF16),
        ]
    return pl.pallas_call(
        functools.partial(layer_body, layer),
        grid_spec=pltpu.PrefetchScalarGridSpec(
            num_scalar_prefetch=1,
            grid=(lanes // width,),
            in_specs=[
                mine(second),
                mine(third),
                mine(third_pair),
                pl.BlockSpec((kinds, parts, mode_rows, width), lambda i, me: (0, 0, 0, i)),
                pl.BlockSpec((rows, width), lambda i, me: (0, i)),
                pl.BlockSpec(skips.shape, lambda i, me: (0, 0, 0)),
                pl.BlockSpec(biases.shape, lambda i, me: (0, 0)),
            ],
            out_specs=out_specs,
            scratch_shapes=[
                pltpu.VMEM((kinds * parts, lines, width), BF16),
                pltpu.VMEM((width, width), BF16),
            ],
        ),
        out_shape=out_shape,
        compiler_params=pltpu.CompilerParams(vmem_limit_bytes=32 * 1024 * 1024),
        name="layer_back",
    )(me, second, third, third_pair, modes, grid, skips, biases)


def unpack_body(places_ref, reply_ref, out_ref):
    def some(turn, carry):
        for way in range(WAYS):
            block = turn * WAYS + way
            out_ref[block] = reply_ref[places_ref[0, block]]
        return carry

    lax.fori_loop(0, out_ref.shape[0] // WAYS, some, 0)


def unpack_slots(places, reply):
    vmem = pl.BlockSpec(memory_space=pltpu.VMEM)
    return pl.pallas_call(
        unpack_body,
        grid_spec=pltpu.PrefetchScalarGridSpec(
            num_scalar_prefetch=1, grid=(1,), in_specs=[vmem], out_specs=vmem
        ),
        out_shape=jax.ShapeDtypeStruct(places.shape[1:] + reply.shape[1:], reply.dtype),
        compiler_params=pltpu.CompilerParams(vmem_limit_bytes=40 * 1024 * 1024),
        name="unpack_slots",
    )(places, reply)


def per_device(
    point_channel_values,
    point_offsets,
    point_counts,
    block_bricks,
    spectral_weights,
    skip_weights,
    skip_bias,
):
    mesh_rows = lax.axis_size("px")
    mesh_columns = lax.axis_size("py")
    device_total = mesh_rows * mesh_columns
    capacity = max(2, 2 * point_channel_values.shape[0] // device_total)
    channels, points = point_channel_values.shape[1:]
    x_dev, y_dev = NX // mesh_rows, NY // mesh_columns
    bricks_y = y_dev // 4
    bricks_z = NZ // 16
    bricks_device = x_dev // 2 * bricks_y * bricks_z
    slot_total = device_total * capacity
    wanted, places, facts = make_plan(
        block_bricks, point_counts, bricks_device, bricks_y, bricks_z, capacity, slot_total, points
    )
    tiles, got_notes = route(wanted, point_offsets, facts, point_channel_values)
    lanes = x_dev * channels
    tiles_x, tiles_z = lanes // 128, NZ // 16
    lift = tiles_z * tiles_x
    bases = find_spots(got_notes, tiles_x, tiles_z)

    kz_dev = MODES // mesh_columns
    ky_dev = MODES // mesh_rows
    parts = 1
    while ky_dev * kz_dev * 2 // (2 * parts) % 16 == 0 and kz_dev % (2 * parts) == 0 and parts < MOST_PARTS:
        parts *= 2
    third_pair, third_back, second, second_back, first_forward, first_back = all_tables(
        mesh_columns, parts
    )
    me = lax.axis_index("py").astype(jnp.int32).reshape(1)
    grid, third_found = gather_grid(
        bases, me, tiles, third_pair, y_dev * NZ, lanes, mesh_columns, parts, lift, capacity
    )
    for layer in range(LAYERS):
        modes = spectral(
            layer, second, first_forward, first_back, third_found, spectral_weights, parts
        )
        found = layer_back(
            layer,
            me,
            second_back,
            third_back,
            third_pair,
            modes,
            grid,
            skip_weights,
            skip_bias,
        )
        grid, third_found = found[0], found[-1]
    grid = grid.reshape(-1, 16, 128)
    reply = decode(bases, grid, got_notes, slot_total, channels, lift)
    return unpack_slots(places, reply)


def solution(mesh):
    return jax.shard_map(
        per_device,
        mesh=mesh,
        in_specs=(
            P(("px", "py"), None, None),
            P(("px", "py"), None, None),
            P(("px", "py")),
            P(("px", "py"), None),
            P(None, None, "px", "py", None, None),
            P(),
            P(),
        ),
        out_specs=P(("px", "py"), None, None),
        check_vma=False,
    )
```

```python
import functools
import math

import jax
import jax.numpy as jnp
import ml_dtypes
import numpy as np
from jax import lax
from jax.experimental import pallas as pl
from jax.experimental.pallas import tpu as pltpu
from jax.sharding import PartitionSpec as P

MODES = 32
NX = 128
NY = 128
NZ = 128
LAYERS = 2

AMPLITUDE = 0.25
SPREAD = 4.5
DECODE_SCALE = 0.1
CHUNKS = 2
MOST_PARTS = 4
WAYS = 4
VMEM_LIMIT = 60 * 1024 * 1024
F32 = jnp.float32
BF16 = jnp.bfloat16


def wave_numbers(kept_modes):
    position = np.arange(kept_modes)
    return np.where(position < kept_modes // 2, position, position - kept_modes)


def forward_matrix(length, frequency):
    angles = 2.0 * math.pi / length * (np.arange(length)[:, None] * frequency[None, :] % length)
    cosine = np.cos(angles) / math.sqrt(length)
    sine_part = np.sin(angles) / math.sqrt(length)
    from_real = np.stack([cosine, -sine_part], axis=-1)
    from_imag = np.stack([sine_part, cosine], axis=-1)
    return np.stack([from_real, from_imag], axis=1)


def unit_angles(products, length):
    return 2.0 * math.pi / length * (products % length)


def repeat_lines(table, slabs, copies):
    rows, depth = table.shape
    span = rows // slabs
    same = np.eye(copies, dtype=bool)[None, :, None, :, None]
    wide = np.where(same, table.reshape(slabs, 1, span, 1, depth), 0.0)
    return wide.reshape(rows * copies, copies * depth)


def constant(table):
    return jnp.asarray(np.asarray(table).astype(ml_dtypes.bfloat16))


def third_tables(kinds, parts, me_y):
    kz_dev = MODES // kinds
    index = np.arange(2 * MODES)
    kz = index // 2 % kz_dev + kz_dev * (index // (2 * kz_dev) ^ me_y)
    angle = unit_angles(kz[:, None] * np.arange(NZ)[None, :], NZ)
    third = np.where((index % 2 == 0)[:, None], np.cos(angle), -np.sin(angle)) / math.sqrt(NZ)
    fold = np.where(kz == 0, 1.0, 2.0)[:, None]
    span = 2 * kz_dev // parts
    return (
        repeat_lines(third, kinds * parts, 2),
        repeat_lines(third * fold, kinds * parts, 16 // span).T,
    )


def second_table(kinds, parts, me_y):
    span = 2 * MODES // kinds // parts
    y_dev = NY // kinds
    row = np.arange(MODES * span)[:, None]
    column = np.arange(y_dev * span)[None, :]
    ky = wave_numbers(MODES)[row // span]
    angle = unit_angles(ky * (me_y * y_dev + column // span), NY)
    sine = np.where(row % 2 == 0, np.sin(angle), -np.sin(angle))
    second = np.where(row % 2 == column % 2, np.cos(angle), sine) / math.sqrt(NY)
    return np.where(row % span // 2 == column % span // 2, second, 0.0)


def all_tables(kinds, parts):
    third = [third_tables(kinds, parts, me_y) for me_y in range(kinds)]
    second = np.stack([second_table(kinds, parts, me_y) for me_y in range(kinds)])
    by_pair = forward_matrix(NX, wave_numbers(MODES)).reshape(NX // 2, 2, 2, MODES, 2)
    first_forward = by_pair.transpose(1, 3, 4, 2, 0).reshape(4 * MODES, NX)
    turned = np.stack([by_pair[..., 1], -by_pair[..., 0]], axis=-1)
    first_back = np.stack([by_pair, turned], axis=0).transpose(2, 0, 3, 1, 4, 5)
    return [
        constant(table)
        for table in (
            np.stack([one[0] for one in third]),
            np.stack([one[1] for one in third]),
            second,
            second.transpose(0, 2, 1),
            first_forward,
            first_back.reshape(4 * NX, 2 * MODES),
        )
    ]


def gelu(value):
    return 0.5 * value * (1.0 + lax.erf(value * math.sqrt(0.5)))


def block_values(offsets, shift_of, count, points):
    lanes = lax.broadcasted_iota(jnp.int32, (1, points), 1).astype(F32)
    amplitude = jnp.where(lanes < count, AMPLITUDE, 0.0).astype(F32)

    def part(dim, brick, cells, scale):
        center = lax.broadcasted_iota(jnp.int32, (cells, points), 0).astype(F32) + 0.5
        apart = (offsets[dim : dim + 1, :] - shift_of(dim, brick) * scale) - center
        return jnp.exp(apart * apart * (-1.0 / SPREAD))

    rows = []
    for brick in range(4):
        along_x = part(0, brick, 2, 2.0) * amplitude
        along_y = part(1, brick, 4, 4.0)
        along_z = part(2, brick, 16, 16.0)
        for cy in range(4):
            plane = along_z * along_y[cy : cy + 1, :]
            rows.append(
                jnp.concatenate(
                    [plane * along_x[0:1, :], plane * along_x[1:2, :]], axis=1
                ).astype(BF16)
            )
    return jnp.concatenate(rows, axis=0)


def note_values(notes, slot, points):
    facts = notes[4 * slot + 3 : 4 * slot + 4, :]
    return block_values(
        notes[4 * slot : 4 * slot + 3, :],
        lambda dim, brick: facts[:, 3 * brick + dim : 3 * brick + dim + 1]
        - facts[:, dim : dim + 1],
        facts[:, 12:13],
        points,
    )


def bits(size):
    return size.bit_length() - 1


def plan_body(bricks_y, bricks_z, capacity, brick_ref, count_ref, wanted_ref, place_ref, fact_ref):
    blocks = brick_ref.shape[0]
    slots = wanted_ref.shape[1]
    bricks_device = bricks_y[1]
    bricks_y = bricks_y[0]
    brick = brick_ref[...]
    down = lax.broadcasted_iota(jnp.int32, (blocks, blocks), 0)
    across = lax.broadcasted_iota(jnp.int32, (blocks, blocks), 1)
    owner_column = lax.shift_right_logical(brick[:, 0:1], jnp.int32(bits(bricks_device)))
    diagonal = down == across
    owner_row = jnp.sum(jnp.where(diagonal, owner_column, 0), axis=0, keepdims=True)
    same = owner_column == owner_row
    rank_row = jnp.sum(jnp.where(same & (down < across), 1, 0), axis=0, keepdims=True)
    rank_column = jnp.sum(jnp.where(same & (across < down), 1, 0), axis=1, keepdims=True)
    place_ref[...] = owner_row * capacity + rank_row
    slot = owner_column * capacity + rank_column
    slot_at = lax.broadcasted_iota(jnp.int32, (blocks, slots), 1)
    block_at = lax.broadcasted_iota(jnp.int32, (blocks, slots), 0) + 1
    wanted_ref[...] = jnp.sum(jnp.where(slot == slot_at, block_at, 0), axis=0, keepdims=True) - 1
    local = brick & (bricks_device - 1)
    parts = (
        lax.shift_right_logical(local, jnp.int32(bits(bricks_y * bricks_z))),
        lax.shift_right_logical(local, jnp.int32(bits(bricks_z))) & (bricks_y - 1),
        local & (bricks_z - 1),
    )
    count = jnp.sum(jnp.where(diagonal, count_ref[...], 0), axis=1, keepdims=True)
    lane = lax.broadcasted_iota(jnp.int32, (blocks, fact_ref.shape[2]), 1)
    facts = jnp.where(lane == 12, count, 0)
    for at in range(4):
        for dim in range(3):
            facts = jnp.where(lane == 3 * at + dim, parts[dim][:, at : at + 1], facts)
    fact_ref[...] = facts.astype(F32).reshape(fact_ref.shape)


def make_plan(bricks, counts, bricks_device, bricks_y, bricks_z, capacity, slots, points):
    blocks = bricks.shape[0]
    vmem = pl.BlockSpec(memory_space=pltpu.VMEM)
    return pl.pallas_call(
        functools.partial(plan_body, (bricks_y, bricks_device), bricks_z, capacity),
        in_specs=[vmem] * 2,
        out_specs=[vmem] * 3,
        out_shape=[
            jax.ShapeDtypeStruct((1, slots), jnp.int32),
            jax.ShapeDtypeStruct((1, blocks), jnp.int32),
            jax.ShapeDtypeStruct((blocks, 1, points), F32),
        ],
        name="make_plan",
    )(bricks, counts.reshape(1, blocks))


def spot_body(tiles_x, tiles_z, note_ref, base_ref, wide_ref):
    wide_ref[...] = note_ref[...].reshape(wide_ref.shape).astype(F32)
    facts = wide_ref[pl.ds(3, wide_ref.shape[0] // 4, stride=4), :].T
    rows = []
    for at in range(4):
        cell_x, cell_y, cell_z = (facts[3 * at + dim : 3 * at + dim + 1, :] for dim in range(3))
        rows.append((cell_y * (4 * tiles_z) + cell_z) * tiles_x + cell_x)
    base_ref[...] = jnp.concatenate(rows, axis=0).astype(jnp.int32)


def find_spots(notes, tiles_x, tiles_z):
    rows = notes.shape[0] * notes.shape[1]
    vmem = pl.BlockSpec(memory_space=pltpu.VMEM)
    return pl.pallas_call(
        functools.partial(spot_body, tiles_x, tiles_z),
        in_specs=[vmem],
        out_specs=vmem,
        out_shape=jax.ShapeDtypeStruct((4, rows // 4), jnp.int32),
        scratch_shapes=[pltpu.VMEM((rows, notes.shape[2]), F32)],
        name="find_spots",
    )(notes)


def near_at(index, devices):
    return (7 * index) % (devices // 2)


def far_at(index, devices):
    return devices // 2 + (7 * index + devices // 3) % (devices // 2)


def mask_at(turn, devices):
    index, far = turn // 2, turn % 2
    return far * far_at(index, devices) + (1 - far) * near_at(index, devices)


def crossed(value, mask, size):
    result, bit = 0, 1
    while bit < size:
        result = result + bit * ((value // bit + mask // bit) % 2)
        bit *= 2
    return result


def route_body(
    size_x,
    size_y,
    source_ref,
    offset_ref,
    fact_ref,
    feature_ref,
    tile_ref,
    got_note_ref,
    feature_send,
    feature_got,
    note_send,
    tile_held,
    feature_ssem,
    feature_rsem,
    note_ssem,
    note_rsem,
    tile_sem,
):
    slots, channels, points = feature_send.shape
    devices = size_x * size_y
    capacity = slots // devices
    ways = math.gcd(WAYS, capacity)
    note_rows = note_send.shape[1]
    me = lax.axis_index("px") * size_y + lax.axis_index("py")
    barrier = pltpu.get_barrier_semaphore()

    def greet(mask, carry):
        other = crossed(me, mask, devices)
        pl.semaphore_signal(
            barrier,
            inc=1,
            device_id={"px": other // size_y, "py": other % size_y},
            device_id_type=pl.DeviceIdType.MESH,
        )
        return carry

    lax.fori_loop(1, devices, greet, 0)

    def transfers(mask):
        other = crossed(me, mask, devices)
        there = {"px": other // size_y, "py": other % size_y}
        return (
            pltpu.make_async_remote_copy(
                src_ref=note_send.at[other],
                dst_ref=got_note_ref.at[me],
                send_sem=note_ssem.at[mask],
                recv_sem=note_rsem.at[mask],
                device_id=there,
                device_id_type=pl.DeviceIdType.MESH,
            ),
            pltpu.make_async_remote_copy(
                src_ref=feature_send.at[pl.ds(other * capacity, capacity)],
                dst_ref=feature_got.at[pl.ds(me * capacity, capacity)],
                send_sem=feature_ssem.at[mask],
                recv_sem=feature_rsem.at[mask],
                device_id=there,
                device_id_type=pl.DeviceIdType.MESH,
            ),
        )

    def pack(other, notes_to, features_to):
        notes = []
        for slot in range(capacity):
            source = source_ref[0, other * capacity + slot]
            present = source >= 0
            source = jnp.maximum(source, 0)
            feature = feature_ref[source]
            features_to[other * capacity + slot] = jnp.where(
                present, feature, jnp.zeros_like(feature)
            )
            note = jnp.concatenate([offset_ref[source].astype(F32), fact_ref[source]], axis=0)
            notes.append(jnp.where(present, note, 0.0))
        if note_rows > 4 * capacity:
            notes.append(jnp.zeros((note_rows - 4 * capacity, points), F32))
        notes_to[other] = jnp.concatenate(notes, axis=0).astype(BF16)

    first = mask_at(1, devices)
    pack(crossed(me, first, devices), note_send, feature_send)
    pl.semaphore_wait(barrier, devices - 1)
    for copy in transfers(first):
        copy.start()

    def launch(turn, carry):
        mask = mask_at(turn, devices)
        pack(crossed(me, mask, devices), note_send, feature_send)
        for copy in transfers(mask):
            copy.start()
        return carry

    lax.fori_loop(2, devices, launch, 0)
    pack(me, got_note_ref, feature_got)

    def tile_copy(turn, other):
        return pltpu.make_async_copy(
            tile_held.at[turn % 2],
            tile_ref.at[pl.ds(other * capacity, capacity)],
            tile_sem.at[turn % 2],
        )

    def work(turn, other):
        notes = got_note_ref[other].astype(F32)
        for start in range(0, capacity, ways):
            tiles = []
            for slot in range(start, start + ways):
                values = note_values(notes, slot, points)
                feature = feature_got[other * capacity + slot]
                empty = jnp.zeros_like(feature)
                pair = jnp.concatenate(
                    [
                        jnp.concatenate([feature, empty], axis=1),
                        jnp.concatenate([empty, feature], axis=1),
                    ],
                    axis=0,
                )
                tiles.append(
                    lax.dot_general(
                        values, pair, (((1,), (1,)), ((), ())), preferred_element_type=F32
                    ).astype(BF16)
                )
            for way in range(ways):
                tile_held[turn % 2, start + way] = tiles[way]
        tile_copy(turn, other).start()

    work(0, me)

    def step(mask_of, turn, carry):
        mask = mask_of(turn % (devices // 2), devices)
        for copy in transfers(mask):
            copy.wait_recv()

        @pl.when(turn >= 2)
        def _():
            tile_copy(turn, me).wait()

        work(turn, crossed(me, mask, devices))
        return carry

    lax.fori_loop(1, devices // 2, functools.partial(step, near_at), 0)
    lax.fori_loop(devices // 2, devices, functools.partial(step, far_at), 0)
    for turn in range(devices - 2, devices):
        tile_copy(turn, me).wait()

    def leave(mask, carry):
        for copy in transfers(mask):
            copy.wait_send()
        return carry

    lax.fori_loop(1, devices, leave, 0)


def route(sources, offsets, facts, features):
    slots = sources.shape[1]
    channels, points = features.shape[1:]
    size_x, size_y = lax.axis_size("px"), lax.axis_size("py")
    devices = size_x * size_y
    capacity = slots // devices
    note_rows = (4 * capacity + 15) // 16 * 16
    vmem = pl.BlockSpec(memory_space=pltpu.VMEM)
    dma = pltpu.SemaphoreType.DMA
    return pl.pallas_call(
        functools.partial(route_body, size_x, size_y),
        in_specs=[pl.BlockSpec(memory_space=pltpu.SMEM), vmem, vmem, vmem],
        out_specs=[pl.BlockSpec(memory_space=pl.ANY), vmem],
        out_shape=[
            jax.ShapeDtypeStruct((slots, 256, 2 * channels), BF16),
            jax.ShapeDtypeStruct((devices, note_rows, points), BF16),
        ],
        scratch_shapes=[
            pltpu.VMEM((slots, channels, points), BF16),
            pltpu.VMEM((slots, channels, points), BF16),
            pltpu.VMEM((devices, note_rows, points), BF16),
            pltpu.VMEM((2, capacity, 256, 2 * channels), BF16),
            dma((devices,)),
            dma((devices,)),
            dma((devices,)),
            dma((devices,)),
            dma((2,)),
        ],
        compiler_params=pltpu.CompilerParams(
            vmem_limit_bytes=VMEM_LIMIT, collective_id=LAYERS + 1, has_side_effects=True
        ),
        name="route",
    )(sources, offsets, facts, features)


def find_third(third_ref, lines_of, out_ref, columns):
    kinds, parts, lines = out_ref.shape[:3]
    both = third_ref.shape[0]
    span = both // (2 * kinds * parts)
    turns = 16 // (2 * span)

    def some(turn, carry):
        found = [
            jnp.dot(third_ref[...], lines_of(turn * turns + way), preferred_element_type=F32)
            for way in range(turns)
        ]
        row = pl.multiple_of(turn * 16, 16)
        for slab in range(kinds * parts):
            piece = [one[slab * 2 * span : (slab + 1) * 2 * span, :] for one in found]
            piece = piece[0] if turns == 1 else jnp.concatenate(piece, axis=0)
            out_ref[slab // parts, slab % parts, pl.ds(row, 16), columns] = piece.astype(BF16)
        return carry

    lax.fori_loop(0, lines // 16, some, 0, unroll=4)


def gather_body(
    group, steps, lift, capacity, base_ref, me_ref, tile_ref, third_ref, out_ref, modes_ref, total_ref
):
    step = pl.program_id(0)
    lanes = out_ref.shape[1]
    depth = third_ref.shape[2] // 2
    tiles = lanes // 128

    @pl.when(step == 0)
    def _():
        total_ref[...] = jnp.zeros_like(total_ref)

    def some(turn, carry):
        for way in range(WAYS):
            member = turn * WAYS + way
            slot = step * group + member
            room = base_ref.shape[1] * capacity // (steps * group)
            spot = slot if room == capacity else slot // capacity * room + slot % capacity
            bases = [base_ref[brick, spot] for brick in range(4)]
            places = [base + cy * lift for base in bases for cy in range(4)]
            sums = [
                total_ref[place] + tile_ref[member, 16 * at : 16 * at + 16, :].astype(F32)
                for at, place in enumerate(places)
            ]
            for place, value in zip(places, sums):
                total_ref[place] = value
        return carry

    lax.fori_loop(0, group // WAYS, some, 0)

    @pl.when(step == steps - 1)
    def _():
        width = math.gcd(lanes, 256)
        pieces = width // 128

        def tile(turn, carry):
            columns = pl.ds(pl.multiple_of(turn * width, width), width)

            def lines_of(pair):
                place = pl.ds(pl.multiple_of(pair * 2 * depth, 2 * depth), 2 * depth)
                rows = []
                for at in range(2 * depth // 16):
                    here = (pair * (2 * depth // 16) + at) * tiles + turn * pieces
                    rows.append(
                        jnp.concatenate([total_ref[here + to] for to in range(pieces)], axis=1)
                    )
                value = jnp.concatenate(rows, axis=0).astype(BF16)
                out_ref[place, columns] = value
                return value

            find_third(third_ref.at[0], lines_of, modes_ref, columns)
            return carry

        lax.fori_loop(0, lanes // width, tile, 0)


def gather_grid(bases, me, tiles, third_pair, rows, lanes, kinds, parts, lift, capacity):
    slots = tiles.shape[0]
    group = math.gcd(slots, 16)
    depth = third_pair.shape[2] // 2
    lines = rows // depth * third_pair.shape[1] // (2 * kinds * parts)
    return pl.pallas_call(
        functools.partial(gather_body, group, slots // group, lift, capacity),
        grid_spec=pltpu.PrefetchScalarGridSpec(
            num_scalar_prefetch=2,
            grid=(slots // group,),
            in_specs=[
                pl.BlockSpec((group,) + tiles.shape[1:], lambda i, base, me: (i, 0, 0)),
                pl.BlockSpec((1,) + third_pair.shape[1:], lambda i, base, me: (me[0], 0, 0)),
            ],
            out_specs=[
                pl.BlockSpec((rows, lanes), lambda i, base, me: (0, 0)),
                pl.BlockSpec((kinds, parts, lines, lanes), lambda i, base, me: (0, 0, 0, 0)),
            ],
            scratch_shapes=[pltpu.VMEM((rows * lanes // 2048, 16, 128), F32)],
        ),
        out_shape=[
            jax.ShapeDtypeStruct((rows, lanes), BF16),
            jax.ShapeDtypeStruct((kinds, parts, lines, lanes), BF16),
        ],
        compiler_params=pltpu.CompilerParams(vmem_limit_bytes=46 * 1024 * 1024),
        name="gather_grid",
    )(bases, me, tiles, third_pair)


def decode_body(size_x, size_y, lift, base_ref, held_ref, note_ref, got_ref, reply_ref, ssem, rsem, own_sem):
    slots, channels, points = got_ref.shape
    devices = size_x * size_y
    capacity = slots // devices
    ways = math.gcd(WAYS, capacity)
    me_x, me_y = lax.axis_index("px"), lax.axis_index("py")
    me = me_x * size_y + me_y
    barrier = pltpu.get_barrier_semaphore()

    def greet(mask, carry):
        other = crossed(me, mask, devices)
        pl.semaphore_signal(
            barrier,
            inc=1,
            device_id={"px": other // size_y, "py": other % size_y},
            device_id_type=pl.DeviceIdType.MESH,
        )
        return carry

    lax.fori_loop(1, devices, greet, 0)

    def transfer(mask):
        other = crossed(me, mask, devices)
        return pltpu.make_async_remote_copy(
            src_ref=reply_ref.at[pl.ds(other * capacity, capacity)],
            dst_ref=got_ref.at[pl.ds(me * capacity, capacity)],
            send_sem=ssem.at[mask],
            recv_sem=rsem.at[mask],
            device_id={"px": other // size_y, "py": other % size_y},
            device_id_type=pl.DeviceIdType.MESH,
        )

    room = base_ref.shape[1] // devices

    def fill(other):
        notes = note_ref[other].astype(F32)
        for start in range(0, capacity, ways):
            results = []
            for slot in range(start, start + ways):
                values = note_values(notes, slot, points)
                bases = [base_ref[brick, other * room + slot] for brick in range(4)]
                cells = jnp.concatenate(
                    [held_ref[base + cy * lift] for base in bases for cy in range(4)], axis=0
                )
                both = lax.dot_general(
                    cells, values, (((0,), (0,)), ((), ())), preferred_element_type=F32
                )
                summed = both[:channels, :points] + both[channels:, points:]
                results.append((DECODE_SCALE * summed).astype(BF16))
            for way in range(ways):
                reply_ref[other * capacity + start + way] = results[way]

    first = mask_at(1, devices)
    fill(crossed(me, first, devices))
    pl.semaphore_wait(barrier, devices - 1)
    transfer(first).start()

    def step(turn, carry):
        mask = mask_at(turn, devices)
        fill(crossed(me, mask, devices))
        transfer(mask).start()
        return carry

    lax.fori_loop(2, devices, step, 0)
    fill(me)
    mine = pl.ds(me * capacity, capacity)
    own = pltpu.make_async_copy(reply_ref.at[mine], got_ref.at[mine], own_sem)
    own.start()
    own.wait()

    def finish(mask, carry):
        transfer(mask).wait_recv()
        return carry

    lax.fori_loop(1, devices, finish, 0)

    def leave(mask, carry):
        transfer(mask).wait_send()
        return carry

    lax.fori_loop(1, devices, leave, 0)


def decode(bases, grid, notes, slots, channels, lift):
    points = notes.shape[2]
    size_x, size_y = lax.axis_size("px"), lax.axis_size("py")
    devices = size_x * size_y
    vmem = pl.BlockSpec(memory_space=pltpu.VMEM)
    return pl.pallas_call(
        functools.partial(decode_body, size_x, size_y, lift),
        in_specs=[pl.BlockSpec(memory_space=pltpu.SMEM), vmem, vmem],
        out_specs=vmem,
        out_shape=jax.ShapeDtypeStruct((slots, channels, points), BF16),
        scratch_shapes=[
            pltpu.VMEM((slots, channels, points), BF16),
            pltpu.SemaphoreType.DMA((devices,)),
            pltpu.SemaphoreType.DMA((devices,)),
            pltpu.SemaphoreType.DMA,
        ],
        compiler_params=pltpu.CompilerParams(
            vmem_limit_bytes=24 * 1024 * 1024, collective_id=LAYERS, has_side_effects=True
        ),
        name="decode",
    )(bases, grid, notes)


def partner(me, distance):
    return me + distance - 2 * distance * ((me // distance) % 2)


def spectral_body(
    layer,
    second_ref,
    forward_ref,
    backward_ref,
    third_ref,
    weight_ref,
    modes_ref,
    held_ref,
    sums_send,
    sums_recv,
    lines_send,
    lines_recv,
    back_send,
    weight_held,
    wide_in,
    wide_out,
    sums_ssem,
    sums_rsem,
    lines_ssem,
    lines_rsem,
    back_ssem,
    back_rsem,
    modes_ssem,
    modes_rsem,
    weight_sem,
):
    kinds, parts, rows, lanes = modes_ref.shape
    devices_x, slab_rows = lines_send.shape[1:3]
    pairs_x = lanes // 128
    channels = weight_held.shape[4]
    kz_part = weight_held.shape[3]
    kx_all = weight_held.shape[1]
    me_x, me_y = lax.axis_index("px"), lax.axis_index("py")
    steps = kinds.bit_length() - 1
    tile = math.gcd(lanes, 256)
    lane_tiles = lanes // tile
    batch = 8
    weight_copies = []
    for part in range(parts):
        copy = pltpu.make_async_copy(
            weight_ref.at[layer, :, :, pl.ds(part * kz_part, kz_part)],
            weight_held.at[part],
            weight_sem.at[part],
        )
        copy.start()
        weight_copies.append(copy)

    def at_x(device):
        return {"px": device}

    def at_y(distance):
        return {"py": partner(me_y, distance)}

    barrier = pltpu.get_barrier_semaphore()
    for hop in range(1, devices_x):
        pl.semaphore_signal(
            barrier,
            inc=1,
            device_id=at_x((me_x + hop) % devices_x),
            device_id_type=pl.DeviceIdType.MESH,
        )
    for step in range(steps):
        pl.semaphore_signal(
            barrier, inc=1, device_id=at_y(1 << step), device_id_type=pl.DeviceIdType.MESH
        )

    started = []

    def send(source, target, ssem, rsem, device):
        copy = pltpu.make_async_remote_copy(
            src_ref=source,
            dst_ref=target,
            send_sem=ssem,
            recv_sem=rsem,
            device_id=device,
            device_id_type=pl.DeviceIdType.MESH,
        )
        copy.start()
        started.append(copy)
        return copy

    bases = [kinds - (kinds >> step) for step in range(steps)]
    sums_copies, lines_copies, back_copies, modes_copies = {}, {}, {}, {}

    def send_sums(part, step):
        count = kinds >> (step + 1)
        at = pl.ds(bases[step], count)
        sums_copies[part, step] = send(
            sums_send.at[part, at],
            sums_recv.at[part, at],
            sums_ssem.at[part, step],
            sums_rsem.at[part, step],
            at_y(1 << step),
        )

    def second_stage(part):
        def one(turn, carry):
            columns = pl.ds(pl.multiple_of(turn * tile, tile), tile)
            for kind in range(kinds - 1, -1, -1):
                value = jnp.dot(
                    second_ref[me_y], third_ref[kind, part, :, columns], preferred_element_type=F32
                )
                if kind % 2:
                    sums_send[part, kind // 2, :, columns] = value.astype(BF16)
                else:
                    held_ref[part, kind // 2, :, columns] = value
            return carry

        lax.fori_loop(0, lane_tiles, one, 0)
        send_sums(part, 0)

    def sum_stage(part, step):
        sums_copies[part, step].wait_recv()

        def one(turn, carry):
            columns = pl.ds(pl.multiple_of(turn * tile, tile), tile)
            for index in range(kinds >> (step + 1)):
                kind = index << (step + 1)
                value = held_ref[part, kind // 2, :, columns] + sums_recv[
                    part, bases[step] + index, :, columns
                ].astype(F32)
                if index % 2:
                    sums_send[part, bases[step + 1] + index // 2, :, columns] = value.astype(BF16)
                elif step + 1 < steps:
                    held_ref[part, kind // 2, :, columns] = value
                else:
                    lines_send[part, :, :, columns] = value.astype(BF16).reshape(
                        devices_x, slab_rows, tile
                    )
            return carry

        lax.fori_loop(0, lane_tiles, one, 0)
        if step + 1 < steps:
            send_sums(part, step + 1)
            return
        for hop in range(1, devices_x):
            target = (me_x + hop) % devices_x
            lines_copies[part, hop] = send(
                lines_send.at[part, target],
                lines_recv.at[part, me_x],
                lines_ssem.at[part, hop],
                lines_rsem.at[part, hop],
                at_x(target),
            )
        lines_recv[part, me_x] = lines_send[part, me_x]

    half_lane = lax.broadcasted_iota(jnp.int32, (1, 128), 1) < channels

    def mix_stage(part):
        for hop in range(1, devices_x):
            lines_copies[part, hop].wait_recv()
        weight_copies[part].wait()

        def widen(source, carry):
            for pair in range(pairs_x):
                row = pl.multiple_of((source * pairs_x + pair) * slab_rows, slab_rows)
                wide_in[pl.ds(row, slab_rows), :] = lines_recv[
                    part, source, :, pair * 128 : (pair + 1) * 128
                ].astype(F32)
            return carry

        lax.fori_loop(0, devices_x, widen, 0)
        count = devices_x * pairs_x
        modes_rows = 2 * kx_all
        row_at = lax.broadcasted_iota(jnp.int32, (modes_rows, batch * channels), 0)
        lane_at = lax.broadcasted_iota(jnp.int32, (modes_rows, batch * channels), 1)
        own = (row_at // 2) % batch == lane_at // channels

        def one(pick, carry):
            ky, kz = pick // kz_part, pick % kz_part
            line = jnp.concatenate(
                [
                    wide_in[pl.ds(2 * pick, count, stride=slab_rows), :],
                    wide_in[pl.ds(2 * pick + 1, count, stride=slab_rows), :],
                ],
                axis=0,
            ).astype(BF16)
            first = jnp.dot(forward_ref[...], line, preferred_element_type=F32)
            first = jnp.where(half_lane, first[:modes_rows], first[modes_rows:])
            first = first + pltpu.roll(first, channels, 1)
            spread = jnp.where(own, jnp.concatenate([first] * (batch // 2), axis=1), 0.0)
            spread = spread.astype(BF16)
            mixed = []
            for at in range(kx_all // batch):
                weight = weight_held[part, at * batch : (at + 1) * batch, ky, kz]
                mixed.append(
                    jnp.dot(
                        spread[2 * at * batch : 2 * (at + 1) * batch],
                        weight.reshape(batch * channels, 2 * channels),
                        preferred_element_type=F32,
                    )
                )
            mixed = jnp.concatenate(mixed, axis=0).astype(BF16)
            back = jnp.dot(backward_ref[...], mixed, preferred_element_type=F32)
            size = 2 * count
            part_at = [back[at * size : (at + 1) * size] for at in range(4)]
            final = jnp.where(half_lane, part_at[0], part_at[3]) + pltpu.roll(
                jnp.where(half_lane, part_at[2], part_at[1]), channels, 1
            )
            wide_out[pl.ds(2 * pick, count, stride=slab_rows), :] = final[:count]
            wide_out[pl.ds(2 * pick + 1, count, stride=slab_rows), :] = final[count:]
            return carry

        lax.fori_loop(0, slab_rows // 2, one, 0)

        def narrow(target, carry):
            for pair in range(pairs_x):
                row = pl.multiple_of((target * pairs_x + pair) * slab_rows, slab_rows)
                back_send[part, target, :, pair * 128 : (pair + 1) * 128] = wide_out[
                    pl.ds(row, slab_rows), :
                ].astype(BF16)
            return carry

        lax.fori_loop(0, devices_x, narrow, 0)
        mine = pl.ds(pl.multiple_of(me_x * slab_rows, slab_rows), slab_rows)
        for hop in range(1, devices_x):
            target = (me_x + hop) % devices_x
            back_copies[part, hop] = send(
                back_send.at[part, target],
                modes_ref.at[0, part, mine],
                back_ssem.at[part, hop],
                back_rsem.at[part, hop],
                at_x(target),
            )
        modes_ref[0, part, mine, :] = back_send[part, me_x]

    def spread_stage(part, kind):
        if kind == 0:
            for hop in range(1, devices_x):
                back_copies[part, hop].wait_recv()
            limit = kinds
        else:
            modes_copies[part, kind].wait_recv()
            limit = kind & -kind
        distance = limit // 2
        while distance >= 1:
            modes_copies[part, kind + distance] = send(
                modes_ref.at[kind, part],
                modes_ref.at[kind + distance, part],
                modes_ssem.at[part, kind + distance],
                modes_rsem.at[part, kind + distance],
                at_y(distance),
            )
            distance //= 2

    order = []
    for part in range(parts):
        order.append((1.5 * part, second_stage, (part,)))
        for step in range(steps):
            order.append((1.5 * part + 6.0 if step == 0 else 12.0 * step + 5.0 * part, sum_stage, (part, step)))
        base = 12.0 * (steps - 1) + 5.0 * part
        order.append((base + 7.1, mix_stage, (part,)))
        order.append((base + 13.0, spread_stage, (part, 0)))
        level = kinds // 2
        while level >= 1:
            for kind in range(level, kinds, 2 * level):
                late = 6.0 * (kinds // level).bit_length()
                order.append((base + 13.1 + late, spread_stage, (part, kind)))
            level //= 2
    order.sort(key=lambda entry: entry[0])
    waited = False
    for _, stage, given in order:
        stage_first = stage is second_stage and given == (0,)
        if stage_first and not waited:
            pl.semaphore_wait(barrier, devices_x - 1 + steps)
            waited = True
        stage(*given)
    for copy in started:
        copy.wait_send()


def spectral(layer, second, first_forward, first_back, third, weights, parts):
    kinds, _, lines, lanes = third.shape
    rows = second.shape[1]
    devices_x = lax.axis_size("px")
    slab_rows = rows // devices_x
    _, kx_all, ky_dev, kz_dev, channels, wide = weights.shape
    steps = kinds.bit_length() - 1
    count = devices_x * lanes // 128 * slab_rows
    dma = pltpu.SemaphoreType.DMA
    return pl.pallas_call(
        functools.partial(spectral_body, layer),
        in_specs=[pl.BlockSpec(memory_space=pltpu.VMEM)] * 4 + [pl.BlockSpec(memory_space=pl.ANY)],
        out_specs=pl.BlockSpec(memory_space=pltpu.VMEM),
        out_shape=jax.ShapeDtypeStruct((kinds, parts, rows, lanes), BF16),
        scratch_shapes=[
            pltpu.VMEM((parts, kinds // 2, rows, lanes), F32),
            pltpu.VMEM((parts, kinds - 1, rows, lanes), BF16),
            pltpu.VMEM((parts, kinds - 1, rows, lanes), BF16),
            pltpu.VMEM((parts, devices_x, slab_rows, lanes), BF16),
            pltpu.VMEM((parts, devices_x, slab_rows, lanes), BF16),
            pltpu.VMEM((parts, devices_x, slab_rows, lanes), BF16),
            pltpu.VMEM((parts, kx_all, ky_dev, kz_dev // parts, channels, wide), BF16),
            pltpu.VMEM((count, 128), F32),
            pltpu.VMEM((count, 128), F32),
            dma((parts, steps)),
            dma((parts, steps)),
            dma((parts, devices_x)),
            dma((parts, devices_x)),
            dma((parts, devices_x)),
            dma((parts, devices_x)),
            dma((parts, kinds)),
            dma((parts, kinds)),
            dma((parts,)),
        ],
        compiler_params=pltpu.CompilerParams(
            vmem_limit_bytes=35 * 1024 * 1024, collective_id=layer, has_side_effects=True
        ),
        name="spectral",
    )(second, first_forward, first_back, third, weights)


def layer_body(
    layer,
    me_ref,
    second_ref,
    third_ref,
    pair_ref,
    modes_ref,
    grid_ref,
    skip_ref,
    bias_ref,
    out_ref,
    *refs,
):
    held_ref, wide_ref = refs[-2:]
    tiled = len(out_ref.shape) == 4
    kinds, parts = modes_ref.shape[:2]
    slabs = kinds * parts
    lines = second_ref.shape[1]
    block = third_ref.shape[1]
    copies = wide_ref.shape[0] // skip_ref.shape[1]
    bias = jnp.concatenate([bias_ref[layer : layer + 1, :]] * copies, axis=1)

    @pl.when(pl.program_id(0) == 0)
    def _():
        skip = jnp.concatenate([skip_ref[layer].astype(F32)] * copies, axis=1)
        skip = jnp.concatenate([skip] * copies, axis=0)
        at_row = lax.broadcasted_iota(jnp.int32, wide_ref.shape, 0) // skip_ref.shape[1]
        at_lane = lax.broadcasted_iota(jnp.int32, wide_ref.shape, 1) // skip_ref.shape[1]
        wide_ref[...] = jnp.where(at_row == at_lane, skip, 0.0).astype(BF16)

    for slab in range(slabs):
        held_ref[slab] = jnp.dot(
            second_ref[0],
            modes_ref[slab // parts, slab % parts],
            preferred_element_type=F32,
        ).astype(BF16)

    def some(turn, carry):
        row = pl.ds(pl.multiple_of(turn * 16, 16), 16)
        line = jnp.concatenate([held_ref[slab, row, :] for slab in range(slabs)], axis=0)
        for way in range(block // 128):
            place = pl.ds(pl.multiple_of(turn * block + way * 128, 128), 128)
            spectral_part = jnp.dot(
                third_ref[0, way * 128 : (way + 1) * 128, :], line, preferred_element_type=F32
            )
            skipped = jnp.dot(grid_ref[place, :], wide_ref[...], preferred_element_type=F32)
            value = gelu(spectral_part + skipped + bias).astype(BF16)
            if tiled:
                row_tiles = pl.ds(turn * (block // 16) + way * 8, 8)
                for at in range(out_ref.shape[1]):
                    piece = value[:, at * 128 : (at + 1) * 128]
                    out_ref[row_tiles, at] = piece.reshape(8, 16, 128)
            else:
                out_ref[place, :] = value
        return carry

    lax.fori_loop(0, lines // 16, some, 0, unroll=2)
    if not tiled:
        pair = pair_ref.shape[2]

        def lines_of(at):
            return out_ref[pl.ds(pl.multiple_of(at * pair, pair), pair), :]

        find_third(pair_ref.at[0], lines_of, refs[0], slice(None))


def layer_back(layer, me, second, third, third_pair, modes, grid, skips, biases):
    rows, lanes = grid.shape
    kinds, parts, mode_rows = modes.shape[:3]
    width = math.gcd(lanes, 4 * skips.shape[1])
    lines = second.shape[1]

    def mine(table):
        return pl.BlockSpec((1,) + table.shape[1:], lambda i, me: (me[0], 0, 0))

    if layer == LAYERS - 1:
        out_specs = [
            pl.BlockSpec((rows // 16, width // 128, 16, 128), lambda i, me: (0, i, 0, 0)),
        ]
        out_shape = [jax.ShapeDtypeStruct((rows // 16, lanes // 128, 16, 128), BF16)]
    else:
        out_specs = [
            pl.BlockSpec((rows, width), lambda i, me: (0, i)),
            pl.BlockSpec((kinds, parts, lines, width), lambda i, me: (0, 0, 0, i)),
        ]
        out_shape = [
            jax.ShapeDtypeStruct((rows, lanes), BF16),
            jax.ShapeDtypeStruct((kinds, parts, lines, lanes), BF16),
        ]
    return pl.pallas_call(
        functools.partial(layer_body, layer),
        grid_spec=pltpu.PrefetchScalarGridSpec(
            num_scalar_prefetch=1,
            grid=(lanes // width,),
            in_specs=[
                mine(second),
                mine(third),
                mine(third_pair),
                pl.BlockSpec((kinds, parts, mode_rows, width), lambda i, me: (0, 0, 0, i)),
                pl.BlockSpec((rows, width), lambda i, me: (0, i)),
                pl.BlockSpec(skips.shape, lambda i, me: (0, 0, 0)),
                pl.BlockSpec(biases.shape, lambda i, me: (0, 0)),
            ],
            out_specs=out_specs,
            scratch_shapes=[
                pltpu.VMEM((kinds * parts, lines, width), BF16),
                pltpu.VMEM((width, width), BF16),
            ],
        ),
        out_shape=out_shape,
        compiler_params=pltpu.CompilerParams(vmem_limit_bytes=32 * 1024 * 1024),
        name="layer_back",
    )(me, second, third, third_pair, modes, grid, skips, biases)


def unpack_body(places_ref, reply_ref, out_ref):
    def some(turn, carry):
        for way in range(WAYS):
            block = turn * WAYS + way
            out_ref[block] = reply_ref[places_ref[0, block]]
        return carry

    lax.fori_loop(0, out_ref.shape[0] // WAYS, some, 0)


def unpack_slots(places, reply):
    vmem = pl.BlockSpec(memory_space=pltpu.VMEM)
    return pl.pallas_call(
        unpack_body,
        grid_spec=pltpu.PrefetchScalarGridSpec(
            num_scalar_prefetch=1, grid=(1,), in_specs=[vmem], out_specs=vmem
        ),
        out_shape=jax.ShapeDtypeStruct(places.shape[1:] + reply.shape[1:], reply.dtype),
        compiler_params=pltpu.CompilerParams(vmem_limit_bytes=40 * 1024 * 1024),
        name="unpack_slots",
    )(places, reply)


def per_device(
    point_channel_values,
    point_offsets,
    point_counts,
    block_bricks,
    spectral_weights,
    skip_weights,
    skip_bias,
):
    mesh_rows = lax.axis_size("px")
    mesh_columns = lax.axis_size("py")
    device_total = mesh_rows * mesh_columns
    capacity = max(2, 2 * point_channel_values.shape[0] // device_total)
    channels, points = point_channel_values.shape[1:]
    x_dev, y_dev = NX // mesh_rows, NY // mesh_columns
    bricks_y = y_dev // 4
    bricks_z = NZ // 16
    bricks_device = x_dev // 2 * bricks_y * bricks_z
    slot_total = device_total * capacity
    wanted, places, facts = make_plan(
        block_bricks, point_counts, bricks_device, bricks_y, bricks_z, capacity, slot_total, points
    )
    tiles, got_notes = route(wanted, point_offsets, facts, point_channel_values)
    lanes = x_dev * channels
    tiles_x, tiles_z = lanes // 128, NZ // 16
    lift = tiles_z * tiles_x
    bases = find_spots(got_notes, tiles_x, tiles_z)

    kz_dev = MODES // mesh_columns
    ky_dev = MODES // mesh_rows
    parts = 1
    while ky_dev * kz_dev * 2 // (2 * parts) % 16 == 0 and kz_dev % (2 * parts) == 0 and parts < MOST_PARTS:
        parts *= 2
    third_pair, third_back, second, second_back, first_forward, first_back = all_tables(
        mesh_columns, parts
    )
    me = lax.axis_index("py").astype(jnp.int32).reshape(1)
    grid, third_found = gather_grid(
        bases, me, tiles, third_pair, y_dev * NZ, lanes, mesh_columns, parts, lift, capacity
    )
    for layer in range(LAYERS):
        modes = spectral(
            layer, second, first_forward, first_back, third_found, spectral_weights, parts
        )
        found = layer_back(
            layer,
            me,
            second_back,
            third_back,
            third_pair,
            modes,
            grid,
            skip_weights,
            skip_bias,
        )
        grid, third_found = found[0], found[-1]
    grid = grid.reshape(-1, 16, 128)
    reply = decode(bases, grid, got_notes, slot_total, channels, lift)
    return unpack_slots(places, reply)


def solution(mesh):
    return jax.shard_map(
        per_device,
        mesh=mesh,
        in_specs=(
            P(("px", "py"), None, None),
            P(("px", "py"), None, None),
            P(("px", "py")),
            P(("px", "py"), None),
            P(None, None, "px", "py", None, None),
            P(),
            P(),
        ),
        out_specs=P(("px", "py"), None, None),
        check_vma=False,
    )
```

```python
import functools
import math

import jax
import jax.numpy as jnp
import ml_dtypes
import numpy as np
from jax import lax
from jax.experimental import pallas as pl
from jax.experimental.pallas import tpu as pltpu
from jax.sharding import PartitionSpec as P

MODES = 32
NX = 128
NY = 128
NZ = 128
LAYERS = 2

AMPLITUDE = 0.25
SPREAD = 4.5
DECODE_SCALE = 0.1
CHUNKS = 2
MOST_PARTS = 4
WAYS = 4
VMEM_LIMIT = 60 * 1024 * 1024
F32 = jnp.float32
BF16 = jnp.bfloat16


def wave_numbers(kept_modes):
    position = np.arange(kept_modes)
    return np.where(position < kept_modes // 2, position, position - kept_modes)


def forward_matrix(length, frequency):
    angles = 2.0 * math.pi / length * (np.arange(length)[:, None] * frequency[None, :] % length)
    cosine = np.cos(angles) / math.sqrt(length)
    sine_part = np.sin(angles) / math.sqrt(length)
    from_real = np.stack([cosine, -sine_part], axis=-1)
    from_imag = np.stack([sine_part, cosine], axis=-1)
    return np.stack([from_real, from_imag], axis=1)


def unit_angles(products, length):
    return 2.0 * math.pi / length * (products % length)


def repeat_lines(table, slabs, copies):
    rows, depth = table.shape
    span = rows // slabs
    same = np.eye(copies, dtype=bool)[None, :, None, :, None]
    wide = np.where(same, table.reshape(slabs, 1, span, 1, depth), 0.0)
    return wide.reshape(rows * copies, copies * depth)


def constant(table):
    return jnp.asarray(np.asarray(table).astype(ml_dtypes.bfloat16))


def third_tables(kinds, parts, me_y):
    kz_dev = MODES // kinds
    index = np.arange(2 * MODES)
    kz = index // 2 % kz_dev + kz_dev * (index // (2 * kz_dev) ^ me_y)
    angle = unit_angles(kz[:, None] * np.arange(NZ)[None, :], NZ)
    third = np.where((index % 2 == 0)[:, None], np.cos(angle), -np.sin(angle)) / math.sqrt(NZ)
    fold = np.where(kz == 0, 1.0, 2.0)[:, None]
    span = 2 * kz_dev // parts
    return (
        repeat_lines(third, kinds * parts, 2),
        repeat_lines(third * fold, kinds * parts, 16 // span).T,
    )


def second_table(kinds, parts, me_y):
    span = 2 * MODES // kinds // parts
    y_dev = NY // kinds
    row = np.arange(MODES * span)[:, None]
    column = np.arange(y_dev * span)[None, :]
    ky = wave_numbers(MODES)[row // span]
    angle = unit_angles(ky * (me_y * y_dev + column // span), NY)
    sine = np.where(row % 2 == 0, np.sin(angle), -np.sin(angle))
    second = np.where(row % 2 == column % 2, np.cos(angle), sine) / math.sqrt(NY)
    return np.where(row % span // 2 == column % span // 2, second, 0.0)


def all_tables(kinds, parts):
    third = [third_tables(kinds, parts, me_y) for me_y in range(kinds)]
    second = np.stack([second_table(kinds, parts, me_y) for me_y in range(kinds)])
    by_pair = forward_matrix(NX, wave_numbers(MODES)).reshape(NX // 2, 2, 2, MODES, 2)
    first_forward = by_pair.transpose(1, 3, 4, 2, 0).reshape(4 * MODES, NX)
    turned = np.stack([by_pair[..., 1], -by_pair[..., 0]], axis=-1)
    first_back = np.stack([by_pair, turned], axis=0).transpose(2, 0, 3, 1, 4, 5)
    return [
        constant(table)
        for table in (
            np.stack([one[0] for one in third]),
            np.stack([one[1] for one in third]),
            second,
            second.transpose(0, 2, 1),
            first_forward,
            first_back.reshape(4 * NX, 2 * MODES),
        )
    ]


def gelu(value):
    return 0.5 * value * (1.0 + lax.erf(value * math.sqrt(0.5)))


def block_values(offsets, shift_of, count, points):
    lanes = lax.broadcasted_iota(jnp.int32, (1, points), 1).astype(F32)
    amplitude = jnp.where(lanes < count, AMPLITUDE, 0.0).astype(F32)

    def part(dim, brick, cells, scale):
        center = lax.broadcasted_iota(jnp.int32, (cells, points), 0).astype(F32) + 0.5
        apart = (offsets[dim : dim + 1, :] - shift_of(dim, brick) * scale) - center
        return jnp.exp(apart * apart * (-1.0 / SPREAD))

    rows = []
    for brick in range(4):
        along_x = part(0, brick, 2, 2.0) * amplitude
        along_y = part(1, brick, 4, 4.0)
        along_z = part(2, brick, 16, 16.0)
        for cy in range(4):
            plane = along_z * along_y[cy : cy + 1, :]
            rows.append(
                jnp.concatenate(
                    [plane * along_x[0:1, :], plane * along_x[1:2, :]], axis=1
                ).astype(BF16)
            )
    return jnp.concatenate(rows, axis=0)


def note_values(notes, slot, points):
    facts = notes[4 * slot + 3 : 4 * slot + 4, :]
    return block_values(
        notes[4 * slot : 4 * slot + 3, :],
        lambda dim, brick: facts[:, 3 * brick + dim : 3 * brick + dim + 1]
        - facts[:, dim : dim + 1],
        facts[:, 12:13],
        points,
    )


def bits(size):
    return size.bit_length() - 1


def plan_body(bricks_y, bricks_z, capacity, brick_ref, count_ref, wanted_ref, place_ref, fact_ref):
    blocks = brick_ref.shape[0]
    slots = wanted_ref.shape[1]
    bricks_device = bricks_y[1]
    bricks_y = bricks_y[0]
    brick = brick_ref[...]
    down = lax.broadcasted_iota(jnp.int32, (blocks, blocks), 0)
    across = lax.broadcasted_iota(jnp.int32, (blocks, blocks), 1)
    owner_column = lax.shift_right_logical(brick[:, 0:1], jnp.int32(bits(bricks_device)))
    diagonal = down == across
    owner_row = jnp.sum(jnp.where(diagonal, owner_column, 0), axis=0, keepdims=True)
    same = owner_column == owner_row
    rank_row = jnp.sum(jnp.where(same & (down < across), 1, 0), axis=0, keepdims=True)
    rank_column = jnp.sum(jnp.where(same & (across < down), 1, 0), axis=1, keepdims=True)
    place_ref[...] = owner_row * capacity + rank_row
    slot = owner_column * capacity + rank_column
    slot_at = lax.broadcasted_iota(jnp.int32, (blocks, slots), 1)
    block_at = lax.broadcasted_iota(jnp.int32, (blocks, slots), 0) + 1
    wanted_ref[...] = jnp.sum(jnp.where(slot == slot_at, block_at, 0), axis=0, keepdims=True) - 1
    local = brick & (bricks_device - 1)
    parts = (
        lax.shift_right_logical(local, jnp.int32(bits(bricks_y * bricks_z))),
        lax.shift_right_logical(local, jnp.int32(bits(bricks_z))) & (bricks_y - 1),
        local & (bricks_z - 1),
    )
    count = jnp.sum(jnp.where(diagonal, count_ref[...], 0), axis=1, keepdims=True)
    lane = lax.broadcasted_iota(jnp.int32, (blocks, fact_ref.shape[2]), 1)
    facts = jnp.where(lane == 12, count, 0)
    for at in range(4):
        for dim in range(3):
            facts = jnp.where(lane == 3 * at + dim, parts[dim][:, at : at + 1], facts)
    fact_ref[...] = facts.astype(F32).reshape(fact_ref.shape)


def make_plan(bricks, counts, bricks_device, bricks_y, bricks_z, capacity, slots, points):
    blocks = bricks.shape[0]
    vmem = pl.BlockSpec(memory_space=pltpu.VMEM)
    return pl.pallas_call(
        functools.partial(plan_body, (bricks_y, bricks_device), bricks_z, capacity),
        in_specs=[vmem] * 2,
        out_specs=[vmem] * 3,
        out_shape=[
            jax.ShapeDtypeStruct((1, slots), jnp.int32),
            jax.ShapeDtypeStruct((1, blocks), jnp.int32),
            jax.ShapeDtypeStruct((blocks, 1, points), F32),
        ],
        name="make_plan",
    )(bricks, counts.reshape(1, blocks))


def spot_body(tiles_x, tiles_z, note_ref, base_ref, wide_ref):
    wide_ref[...] = note_ref[...].reshape(wide_ref.shape).astype(F32)
    facts = wide_ref[pl.ds(3, wide_ref.shape[0] // 4, stride=4), :].T
    rows = []
    for at in range(4):
        cell_x, cell_y, cell_z = (facts[3 * at + dim : 3 * at + dim + 1, :] for dim in range(3))
        rows.append((cell_y * (4 * tiles_z) + cell_z) * tiles_x + cell_x)
    base_ref[...] = jnp.concatenate(rows, axis=0).astype(jnp.int32)


def find_spots(notes, tiles_x, tiles_z):
    rows = notes.shape[0] * notes.shape[1]
    vmem = pl.BlockSpec(memory_space=pltpu.VMEM)
    return pl.pallas_call(
        functools.partial(spot_body, tiles_x, tiles_z),
        in_specs=[vmem],
        out_specs=vmem,
        out_shape=jax.ShapeDtypeStruct((4, rows // 4), jnp.int32),
        scratch_shapes=[pltpu.VMEM((rows, notes.shape[2]), F32)],
        name="find_spots",
    )(notes)


def near_at(index, devices):
    return (7 * index) % (devices // 2)


def far_at(index, devices):
    return devices // 2 + (7 * index + devices // 3) % (devices // 2)


def mask_at(turn, devices):
    index, far = turn // 2, turn % 2
    return far * far_at(index, devices) + (1 - far) * near_at(index, devices)


def crossed(value, mask, size):
    result, bit = 0, 1
    while bit < size:
        result = result + bit * ((value // bit + mask // bit) % 2)
        bit *= 2
    return result


def route_body(
    size_x,
    size_y,
    source_ref,
    offset_ref,
    fact_ref,
    feature_ref,
    tile_ref,
    got_note_ref,
    feature_send,
    feature_got,
    note_send,
    tile_held,
    feature_ssem,
    feature_rsem,
    note_ssem,
    note_rsem,
    tile_sem,
):
    slots, channels, points = feature_send.shape
    devices = size_x * size_y
    capacity = slots // devices
    ways = math.gcd(WAYS, capacity)
    note_rows = note_send.shape[1]
    me = lax.axis_index("px") * size_y + lax.axis_index("py")
    barrier = pltpu.get_barrier_semaphore()

    def greet(mask, carry):
        other = crossed(me, mask, devices)
        pl.semaphore_signal(
            barrier,
            inc=1,
            device_id={"px": other // size_y, "py": other % size_y},
            device_id_type=pl.DeviceIdType.MESH,
        )
        return carry

    lax.fori_loop(1, devices, greet, 0)

    def transfers(mask):
        other = crossed(me, mask, devices)
        there = {"px": other // size_y, "py": other % size_y}
        return (
            pltpu.make_async_remote_copy(
                src_ref=note_send.at[other],
                dst_ref=got_note_ref.at[me],
                send_sem=note_ssem.at[mask],
                recv_sem=note_rsem.at[mask],
                device_id=there,
                device_id_type=pl.DeviceIdType.MESH,
            ),
            pltpu.make_async_remote_copy(
                src_ref=feature_send.at[pl.ds(other * capacity, capacity)],
                dst_ref=feature_got.at[pl.ds(me * capacity, capacity)],
                send_sem=feature_ssem.at[mask],
                recv_sem=feature_rsem.at[mask],
                device_id=there,
                device_id_type=pl.DeviceIdType.MESH,
            ),
        )

    def pack(other, notes_to, features_to):
        notes = []
        for slot in range(capacity):
            source = source_ref[0, other * capacity + slot]
            present = source >= 0
            source = jnp.maximum(source, 0)
            feature = feature_ref[source]
            features_to[other * capacity + slot] = jnp.where(
                present, feature, jnp.zeros_like(feature)
            )
            note = jnp.concatenate([offset_ref[source].astype(F32), fact_ref[source]], axis=0)
            notes.append(jnp.where(present, note, 0.0))
        if note_rows > 4 * capacity:
            notes.append(jnp.zeros((note_rows - 4 * capacity, points), F32))
        notes_to[other] = jnp.concatenate(notes, axis=0).astype(BF16)

    first = mask_at(1, devices)
    pack(crossed(me, first, devices), note_send, feature_send)
    pl.semaphore_wait(barrier, devices - 1)
    for copy in transfers(first):
        copy.start()

    def launch(turn, carry):
        mask = mask_at(turn, devices)
        pack(crossed(me, mask, devices), note_send, feature_send)
        for copy in transfers(mask):
            copy.start()
        return carry

    lax.fori_loop(2, devices, launch, 0)
    pack(me, got_note_ref, feature_got)

    def tile_copy(turn, other):
        return pltpu.make_async_copy(
            tile_held.at[turn % 2],
            tile_ref.at[pl.ds(other * capacity, capacity)],
            tile_sem.at[turn % 2],
        )

    def work(turn, other):
        notes = got_note_ref[other].astype(F32)
        for start in range(0, capacity, ways):
            tiles = []
            for slot in range(start, start + ways):
                values = note_values(notes, slot, points)
                feature = feature_got[other * capacity + slot]
                empty = jnp.zeros_like(feature)
                pair = jnp.concatenate(
                    [
                        jnp.concatenate([feature, empty], axis=1),
                        jnp.concatenate([empty, feature], axis=1),
                    ],
                    axis=0,
                )
                tiles.append(
                    lax.dot_general(
                        values, pair, (((1,), (1,)), ((), ())), preferred_element_type=F32
                    ).astype(BF16)
                )
            for way in range(ways):
                tile_held[turn % 2, start + way] = tiles[way]
        tile_copy(turn, other).start()

    work(0, me)

    def step(mask_of, turn, carry):
        mask = mask_of(turn % (devices // 2), devices)
        for copy in transfers(mask):
            copy.wait_recv()

        @pl.when(turn >= 2)
        def _():
            tile_copy(turn, me).wait()

        work(turn, crossed(me, mask, devices))
        return carry

    lax.fori_loop(1, devices // 2, functools.partial(step, near_at), 0)
    lax.fori_loop(devices // 2, devices, functools.partial(step, far_at), 0)
    for turn in range(devices - 2, devices):
        tile_copy(turn, me).wait()

    def leave(mask, carry):
        for copy in transfers(mask):
            copy.wait_send()
        return carry

    lax.fori_loop(1, devices, leave, 0)


def route(sources, offsets, facts, features):
    slots = sources.shape[1]
    channels, points = features.shape[1:]
    size_x, size_y = lax.axis_size("px"), lax.axis_size("py")
    devices = size_x * size_y
    capacity = slots // devices
    note_rows = (4 * capacity + 15) // 16 * 16
    vmem = pl.BlockSpec(memory_space=pltpu.VMEM)
    dma = pltpu.SemaphoreType.DMA
    return pl.pallas_call(
        functools.partial(route_body, size_x, size_y),
        in_specs=[pl.BlockSpec(memory_space=pltpu.SMEM), vmem, vmem, vmem],
        out_specs=[pl.BlockSpec(memory_space=pl.ANY), vmem],
        out_shape=[
            jax.ShapeDtypeStruct((slots, 256, 2 * channels), BF16),
            jax.ShapeDtypeStruct((devices, note_rows, points), BF16),
        ],
        scratch_shapes=[
            pltpu.VMEM((slots, channels, points), BF16),
            pltpu.VMEM((slots, channels, points), BF16),
            pltpu.VMEM((devices, note_rows, points), BF16),
            pltpu.VMEM((2, capacity, 256, 2 * channels), BF16),
            dma((devices,)),
            dma((devices,)),
            dma((devices,)),
            dma((devices,)),
            dma((2,)),
        ],
        compiler_params=pltpu.CompilerParams(
            vmem_limit_bytes=VMEM_LIMIT, collective_id=LAYERS + 1, has_side_effects=True
        ),
        name="route",
    )(sources, offsets, facts, features)


def find_third(third_ref, lines_of, out_ref, columns):
    kinds, parts, lines = out_ref.shape[:3]
    both = third_ref.shape[0]
    span = both // (2 * kinds * parts)
    turns = 16 // (2 * span)

    def some(turn, carry):
        found = [
            jnp.dot(third_ref[...], lines_of(turn * turns + way), preferred_element_type=F32)
            for way in range(turns)
        ]
        row = pl.multiple_of(turn * 16, 16)
        for slab in range(kinds * parts):
            piece = [one[slab * 2 * span : (slab + 1) * 2 * span, :] for one in found]
            piece = piece[0] if turns == 1 else jnp.concatenate(piece, axis=0)
            out_ref[slab // parts, slab % parts, pl.ds(row, 16), columns] = piece.astype(BF16)
        return carry

    lax.fori_loop(0, lines // 16, some, 0, unroll=True)


def gather_body(
    group, steps, lift, capacity, base_ref, me_ref, tile_ref, third_ref, out_ref, modes_ref, total_ref
):
    step = pl.program_id(0)
    lanes = out_ref.shape[1]
    depth = third_ref.shape[2] // 2
    tiles = lanes // 128

    @pl.when(step == 0)
    def _():
        total_ref[...] = jnp.zeros_like(total_ref)

    def some(turn, carry):
        for way in range(WAYS):
            member = turn * WAYS + way
            slot = step * group + member
            room = base_ref.shape[1] * capacity // (steps * group)
            spot = slot if room == capacity else slot // capacity * room + slot % capacity
            bases = [base_ref[brick, spot] for brick in range(4)]
            places = [base + cy * lift for base in bases for cy in range(4)]
            sums = [
                total_ref[place] + tile_ref[member, 16 * at : 16 * at + 16, :].astype(F32)
                for at, place in enumerate(places)
            ]
            for place, value in zip(places, sums):
                total_ref[place] = value
        return carry

    lax.fori_loop(0, group // WAYS, some, 0)

    @pl.when(step == steps - 1)
    def _():
        width = math.gcd(lanes, 256)
        pieces = width // 128

        def tile(turn, carry):
            columns = pl.ds(pl.multiple_of(turn * width, width), width)

            def lines_of(pair):
                place = pl.ds(pl.multiple_of(pair * 2 * depth, 2 * depth), 2 * depth)
                rows = []
                for at in range(2 * depth // 16):
                    here = (pair * (2 * depth // 16) + at) * tiles + turn * pieces
                    rows.append(
                        jnp.concatenate([total_ref[here + to] for to in range(pieces)], axis=1)
                    )
                value = jnp.concatenate(rows, axis=0).astype(BF16)
                out_ref[place, columns] = value
                return value

            find_third(third_ref.at[0], lines_of, modes_ref, columns)
            return carry

        lax.fori_loop(0, lanes // width, tile, 0)


def gather_grid(bases, me, tiles, third_pair, rows, lanes, kinds, parts, lift, capacity):
    slots = tiles.shape[0]
    group = math.gcd(slots, 32)
    depth = third_pair.shape[2] // 2
    lines = rows // depth * third_pair.shape[1] // (2 * kinds * parts)
    return pl.pallas_call(
        functools.partial(gather_body, group, slots // group, lift, capacity),
        grid_spec=pltpu.PrefetchScalarGridSpec(
            num_scalar_prefetch=2,
            grid=(slots // group,),
            in_specs=[
                pl.BlockSpec((group,) + tiles.shape[1:], lambda i, base, me: (i, 0, 0)),
                pl.BlockSpec((1,) + third_pair.shape[1:], lambda i, base, me: (me[0], 0, 0)),
            ],
            out_specs=[
                pl.BlockSpec((rows, lanes), lambda i, base, me: (0, 0)),
                pl.BlockSpec((kinds, parts, lines, lanes), lambda i, base, me: (0, 0, 0, 0)),
            ],
            scratch_shapes=[pltpu.VMEM((rows * lanes // 2048, 16, 128), F32)],
        ),
        out_shape=[
            jax.ShapeDtypeStruct((rows, lanes), BF16),
            jax.ShapeDtypeStruct((kinds, parts, lines, lanes), BF16),
        ],
        compiler_params=pltpu.CompilerParams(vmem_limit_bytes=46 * 1024 * 1024),
        name="gather_grid",
    )(bases, me, tiles, third_pair)


def decode_body(size_x, size_y, lift, base_ref, held_ref, note_ref, got_ref, reply_ref, ssem, rsem, own_sem):
    slots, channels, points = got_ref.shape
    devices = size_x * size_y
    capacity = slots // devices
    ways = math.gcd(WAYS, capacity)
    me_x, me_y = lax.axis_index("px"), lax.axis_index("py")
    me = me_x * size_y + me_y
    barrier = pltpu.get_barrier_semaphore()

    def greet(mask, carry):
        other = crossed(me, mask, devices)
        pl.semaphore_signal(
            barrier,
            inc=1,
            device_id={"px": other // size_y, "py": other % size_y},
            device_id_type=pl.DeviceIdType.MESH,
        )
        return carry

    lax.fori_loop(1, devices, greet, 0)

    def transfer(mask):
        other = crossed(me, mask, devices)
        return pltpu.make_async_remote_copy(
            src_ref=reply_ref.at[pl.ds(other * capacity, capacity)],
            dst_ref=got_ref.at[pl.ds(me * capacity, capacity)],
            send_sem=ssem.at[mask],
            recv_sem=rsem.at[mask],
            device_id={"px": other // size_y, "py": other % size_y},
            device_id_type=pl.DeviceIdType.MESH,
        )

    room = base_ref.shape[1] // devices

    def fill(other):
        notes = note_ref[other].astype(F32)
        for start in range(0, capacity, ways):
            results = []
            for slot in range(start, start + ways):
                values = note_values(notes, slot, points)
                bases = [base_ref[brick, other * room + slot] for brick in range(4)]
                cells = jnp.concatenate(
                    [held_ref[base + cy * lift] for base in bases for cy in range(4)], axis=0
                )
                both = lax.dot_general(
                    cells, values, (((0,), (0,)), ((), ())), preferred_element_type=F32
                )
                summed = both[:channels, :points] + both[channels:, points:]
                results.append((DECODE_SCALE * summed).astype(BF16))
            for way in range(ways):
                reply_ref[other * capacity + start + way] = results[way]

    first = mask_at(1, devices)
    fill(crossed(me, first, devices))
    pl.semaphore_wait(barrier, devices - 1)
    transfer(first).start()

    def step(turn, carry):
        mask = mask_at(turn, devices)
        fill(crossed(me, mask, devices))
        transfer(mask).start()
        return carry

    lax.fori_loop(2, devices, step, 0)
    fill(me)
    mine = pl.ds(me * capacity, capacity)
    own = pltpu.make_async_copy(reply_ref.at[mine], got_ref.at[mine], own_sem)
    own.start()
    own.wait()

    def finish(mask, carry):
        transfer(mask).wait_recv()
        return carry

    lax.fori_loop(1, devices, finish, 0)

    def leave(mask, carry):
        transfer(mask).wait_send()
        return carry

    lax.fori_loop(1, devices, leave, 0)


def decode(bases, grid, notes, slots, channels, lift):
    points = notes.shape[2]
    size_x, size_y = lax.axis_size("px"), lax.axis_size("py")
    devices = size_x * size_y
    vmem = pl.BlockSpec(memory_space=pltpu.VMEM)
    return pl.pallas_call(
        functools.partial(decode_body, size_x, size_y, lift),
        in_specs=[pl.BlockSpec(memory_space=pltpu.SMEM), vmem, vmem],
        out_specs=vmem,
        out_shape=jax.ShapeDtypeStruct((slots, channels, points), BF16),
        scratch_shapes=[
            pltpu.VMEM((slots, channels, points), BF16),
            pltpu.SemaphoreType.DMA((devices,)),
            pltpu.SemaphoreType.DMA((devices,)),
            pltpu.SemaphoreType.DMA,
        ],
        compiler_params=pltpu.CompilerParams(
            vmem_limit_bytes=24 * 1024 * 1024, collective_id=LAYERS, has_side_effects=True
        ),
        name="decode",
    )(bases, grid, notes)


def partner(me, distance):
    return me + distance - 2 * distance * ((me // distance) % 2)


def spectral_body(
    layer,
    second_ref,
    forward_ref,
    backward_ref,
    third_ref,
    weight_ref,
    modes_ref,
    held_ref,
    sums_send,
    sums_recv,
    lines_send,
    lines_recv,
    back_send,
    weight_held,
    wide_in,
    wide_out,
    sums_ssem,
    sums_rsem,
    lines_ssem,
    lines_rsem,
    back_ssem,
    back_rsem,
    modes_ssem,
    modes_rsem,
    weight_sem,
):
    kinds, parts, rows, lanes = modes_ref.shape
    devices_x, slab_rows = lines_send.shape[1:3]
    pairs_x = lanes // 128
    channels = weight_held.shape[4]
    kz_part = weight_held.shape[3]
    kx_all = weight_held.shape[1]
    me_x, me_y = lax.axis_index("px"), lax.axis_index("py")
    steps = kinds.bit_length() - 1
    tile = math.gcd(lanes, 256)
    lane_tiles = lanes // tile
    batch = 8
    weight_copies = []
    for part in range(parts):
        copy = pltpu.make_async_copy(
            weight_ref.at[layer, :, :, pl.ds(part * kz_part, kz_part)],
            weight_held.at[part],
            weight_sem.at[part],
        )
        copy.start()
        weight_copies.append(copy)

    def at_x(device):
        return {"px": device}

    def at_y(distance):
        return {"py": partner(me_y, distance)}

    barrier = pltpu.get_barrier_semaphore()
    for hop in range(1, devices_x):
        pl.semaphore_signal(
            barrier,
            inc=1,
            device_id=at_x((me_x + hop) % devices_x),
            device_id_type=pl.DeviceIdType.MESH,
        )
    for step in range(steps):
        pl.semaphore_signal(
            barrier, inc=1, device_id=at_y(1 << step), device_id_type=pl.DeviceIdType.MESH
        )

    started = []

    def send(source, target, ssem, rsem, device):
        copy = pltpu.make_async_remote_copy(
            src_ref=source,
            dst_ref=target,
            send_sem=ssem,
            recv_sem=rsem,
            device_id=device,
            device_id_type=pl.DeviceIdType.MESH,
        )
        copy.start()
        started.append(copy)
        return copy

    bases = [kinds - (kinds >> step) for step in range(steps)]
    sums_copies, lines_copies, back_copies, modes_copies = {}, {}, {}, {}

    def send_sums(part, step):
        count = kinds >> (step + 1)
        at = pl.ds(bases[step], count)
        sums_copies[part, step] = send(
            sums_send.at[part, at],
            sums_recv.at[part, at],
            sums_ssem.at[part, step],
            sums_rsem.at[part, step],
            at_y(1 << step),
        )

    def second_stage(part):
        def one(turn, carry):
            columns = pl.ds(pl.multiple_of(turn * tile, tile), tile)
            for kind in range(kinds - 1, -1, -1):
                value = jnp.dot(
                    second_ref[me_y], third_ref[kind, part, :, columns], preferred_element_type=F32
                )
                if kind % 2:
                    sums_send[part, kind // 2, :, columns] = value.astype(BF16)
                else:
                    held_ref[part, kind // 2, :, columns] = value
            return carry

        lax.fori_loop(0, lane_tiles, one, 0)
        send_sums(part, 0)

    def sum_stage(part, step):
        sums_copies[part, step].wait_recv()

        def one(turn, carry):
            columns = pl.ds(pl.multiple_of(turn * tile, tile), tile)
            for index in range(kinds >> (step + 1)):
                kind = index << (step + 1)
                value = held_ref[part, kind // 2, :, columns] + sums_recv[
                    part, bases[step] + index, :, columns
                ].astype(F32)
                if index % 2:
                    sums_send[part, bases[step + 1] + index // 2, :, columns] = value.astype(BF16)
                elif step + 1 < steps:
                    held_ref[part, kind // 2, :, columns] = value
                else:
                    lines_send[part, :, :, columns] = value.astype(BF16).reshape(
                        devices_x, slab_rows, tile
                    )
            return carry

        lax.fori_loop(0, lane_tiles, one, 0)
        if step + 1 < steps:
            send_sums(part, step + 1)
            return
        for hop in range(1, devices_x):
            target = (me_x + hop) % devices_x
            lines_copies[part, hop] = send(
                lines_send.at[part, target],
                lines_recv.at[part, me_x],
                lines_ssem.at[part, hop],
                lines_rsem.at[part, hop],
                at_x(target),
            )
        lines_recv[part, me_x] = lines_send[part, me_x]

    half_lane = lax.broadcasted_iota(jnp.int32, (1, 128), 1) < channels

    def mix_stage(part):
        for hop in range(1, devices_x):
            lines_copies[part, hop].wait_recv()
        weight_copies[part].wait()

        def widen(source, carry):
            for pair in range(pairs_x):
                row = pl.multiple_of((source * pairs_x + pair) * slab_rows, slab_rows)
                wide_in[pl.ds(row, slab_rows), :] = lines_recv[
                    part, source, :, pair * 128 : (pair + 1) * 128
                ].astype(F32)
            return carry

        lax.fori_loop(0, devices_x, widen, 0)
        count = devices_x * pairs_x
        modes_rows = 2 * kx_all
        row_at = lax.broadcasted_iota(jnp.int32, (modes_rows, batch * channels), 0)
        lane_at = lax.broadcasted_iota(jnp.int32, (modes_rows, batch * channels), 1)
        own = (row_at // 2) % batch == lane_at // channels

        def one(pick, carry):
            ky, kz = pick // kz_part, pick % kz_part
            line = jnp.concatenate(
                [
                    wide_in[pl.ds(2 * pick, count, stride=slab_rows), :],
                    wide_in[pl.ds(2 * pick + 1, count, stride=slab_rows), :],
                ],
                axis=0,
            ).astype(BF16)
            first = jnp.dot(forward_ref[...], line, preferred_element_type=F32)
            first = jnp.where(half_lane, first[:modes_rows], first[modes_rows:])
            first = first + pltpu.roll(first, channels, 1)
            spread = jnp.where(own, jnp.concatenate([first] * (batch // 2), axis=1), 0.0)
            spread = spread.astype(BF16)
            mixed = []
            for at in range(kx_all // batch):
                weight = weight_held[part, at * batch : (at + 1) * batch, ky, kz]
                mixed.append(
                    jnp.dot(
                        spread[2 * at * batch : 2 * (at + 1) * batch],
                        weight.reshape(batch * channels, 2 * channels),
                        preferred_element_type=F32,
                    )
                )
            mixed = jnp.concatenate(mixed, axis=0).astype(BF16)
            back = jnp.dot(backward_ref[...], mixed, preferred_element_type=F32)
            size = 2 * count
            part_at = [back[at * size : (at + 1) * size] for at in range(4)]
            final = jnp.where(half_lane, part_at[0], part_at[3]) + pltpu.roll(
                jnp.where(half_lane, part_at[2], part_at[1]), channels, 1
            )
            wide_out[pl.ds(2 * pick, count, stride=slab_rows), :] = final[:count]
            wide_out[pl.ds(2 * pick + 1, count, stride=slab_rows), :] = final[count:]
            return carry

        lax.fori_loop(0, slab_rows // 2, one, 0)

        def narrow(target, carry):
            for pair in range(pairs_x):
                row = pl.multiple_of((target * pairs_x + pair) * slab_rows, slab_rows)
                back_send[part, target, :, pair * 128 : (pair + 1) * 128] = wide_out[
                    pl.ds(row, slab_rows), :
                ].astype(BF16)
            return carry

        lax.fori_loop(0, devices_x, narrow, 0)
        mine = pl.ds(pl.multiple_of(me_x * slab_rows, slab_rows), slab_rows)
        for hop in range(1, devices_x):
            target = (me_x + hop) % devices_x
            back_copies[part, hop] = send(
                back_send.at[part, target],
                modes_ref.at[0, part, mine],
                back_ssem.at[part, hop],
                back_rsem.at[part, hop],
                at_x(target),
            )
        modes_ref[0, part, mine, :] = back_send[part, me_x]

    def spread_stage(part, kind):
        if kind == 0:
            for hop in range(1, devices_x):
                back_copies[part, hop].wait_recv()
            limit = kinds
        else:
            modes_copies[part, kind].wait_recv()
            limit = kind & -kind
        distance = limit // 2
        while distance >= 1:
            modes_copies[part, kind + distance] = send(
                modes_ref.at[kind, part],
                modes_ref.at[kind + distance, part],
                modes_ssem.at[part, kind + distance],
                modes_rsem.at[part, kind + distance],
                at_y(distance),
            )
            distance //= 2

    order = []
    for part in range(parts):
        order.append((1.5 * part, second_stage, (part,)))
        for step in range(steps):
            order.append((1.5 * part + 6.0 if step == 0 else 12.0 * step + 5.0 * part, sum_stage, (part, step)))
        base = 12.0 * (steps - 1) + 5.0 * part
        order.append((base + 7.1, mix_stage, (part,)))
        order.append((base + 13.0, spread_stage, (part, 0)))
        level = kinds // 2
        while level >= 1:
            for kind in range(level, kinds, 2 * level):
                late = 6.0 * (kinds // level).bit_length()
                order.append((base + 13.1 + late, spread_stage, (part, kind)))
            level //= 2
    order.sort(key=lambda entry: entry[0])
    waited = False
    for _, stage, given in order:
        stage_first = stage is second_stage and given == (0,)
        if stage_first and not waited:
            pl.semaphore_wait(barrier, devices_x - 1 + steps)
            waited = True
        stage(*given)
    for copy in started:
        copy.wait_send()


def spectral(layer, second, first_forward, first_back, third, weights, parts):
    kinds, _, lines, lanes = third.shape
    rows = second.shape[1]
    devices_x = lax.axis_size("px")
    slab_rows = rows // devices_x
    _, kx_all, ky_dev, kz_dev, channels, wide = weights.shape
    steps = kinds.bit_length() - 1
    count = devices_x * lanes // 128 * slab_rows
    dma = pltpu.SemaphoreType.DMA
    return pl.pallas_call(
        functools.partial(spectral_body, layer),
        in_specs=[pl.BlockSpec(memory_space=pltpu.VMEM)] * 4 + [pl.BlockSpec(memory_space=pl.ANY)],
        out_specs=pl.BlockSpec(memory_space=pltpu.VMEM),
        out_shape=jax.ShapeDtypeStruct((kinds, parts, rows, lanes), BF16),
        scratch_shapes=[
            pltpu.VMEM((parts, kinds // 2, rows, lanes), F32),
            pltpu.VMEM((parts, kinds - 1, rows, lanes), BF16),
            pltpu.VMEM((parts, kinds - 1, rows, lanes), BF16),
            pltpu.VMEM((parts, devices_x, slab_rows, lanes), BF16),
            pltpu.VMEM((parts, devices_x, slab_rows, lanes), BF16),
            pltpu.VMEM((parts, devices_x, slab_rows, lanes), BF16),
            pltpu.VMEM((parts, kx_all, ky_dev, kz_dev // parts, channels, wide), BF16),
            pltpu.VMEM((count, 128), F32),
            pltpu.VMEM((count, 128), F32),
            dma((parts, steps)),
            dma((parts, steps)),
            dma((parts, devices_x)),
            dma((parts, devices_x)),
            dma((parts, devices_x)),
            dma((parts, devices_x)),
            dma((parts, kinds)),
            dma((parts, kinds)),
            dma((parts,)),
        ],
        compiler_params=pltpu.CompilerParams(
            vmem_limit_bytes=35 * 1024 * 1024, collective_id=layer, has_side_effects=True
        ),
        name="spectral",
    )(second, first_forward, first_back, third, weights)


def layer_body(
    layer,
    me_ref,
    second_ref,
    third_ref,
    pair_ref,
    modes_ref,
    grid_ref,
    skip_ref,
    bias_ref,
    out_ref,
    *refs,
):
    held_ref, wide_ref = refs[-2:]
    tiled = len(out_ref.shape) == 4
    kinds, parts = modes_ref.shape[:2]
    slabs = kinds * parts
    lines = second_ref.shape[1]
    block = third_ref.shape[1]
    copies = wide_ref.shape[0] // skip_ref.shape[1]
    bias = jnp.concatenate([bias_ref[layer : layer + 1, :]] * copies, axis=1)

    @pl.when(pl.program_id(0) == 0)
    def _():
        skip = jnp.concatenate([skip_ref[layer].astype(F32)] * copies, axis=1)
        skip = jnp.concatenate([skip] * copies, axis=0)
        at_row = lax.broadcasted_iota(jnp.int32, wide_ref.shape, 0) // skip_ref.shape[1]
        at_lane = lax.broadcasted_iota(jnp.int32, wide_ref.shape, 1) // skip_ref.shape[1]
        wide_ref[...] = jnp.where(at_row == at_lane, skip, 0.0).astype(BF16)

    for slab in range(slabs):
        held_ref[slab] = jnp.dot(
            second_ref[0],
            modes_ref[slab // parts, slab % parts],
            preferred_element_type=F32,
        ).astype(BF16)

    def some(turn, carry):
        row = pl.ds(pl.multiple_of(turn * 16, 16), 16)
        line = jnp.concatenate([held_ref[slab, row, :] for slab in range(slabs)], axis=0)
        for way in range(block // 128):
            place = pl.ds(pl.multiple_of(turn * block + way * 128, 128), 128)
            spectral_part = jnp.dot(
                third_ref[0, way * 128 : (way + 1) * 128, :], line, preferred_element_type=F32
            )
            skipped = jnp.dot(grid_ref[place, :], wide_ref[...], preferred_element_type=F32)
            value = gelu(spectral_part + skipped + bias).astype(BF16)
            if tiled:
                row_tiles = pl.ds(turn * (block // 16) + way * 8, 8)
                for at in range(out_ref.shape[1]):
                    piece = value[:, at * 128 : (at + 1) * 128]
                    out_ref[row_tiles, at] = piece.reshape(8, 16, 128)
            else:
                out_ref[place, :] = value
        return carry

    lax.fori_loop(0, lines // 16, some, 0, unroll=4)
    if not tiled:
        pair = pair_ref.shape[2]

        def lines_of(at):
            return out_ref[pl.ds(pl.multiple_of(at * pair, pair), pair), :]

        find_third(pair_ref.at[0], lines_of, refs[0], slice(None))


def layer_back(layer, me, second, third, third_pair, modes, grid, skips, biases):
    rows, lanes = grid.shape
    kinds, parts, mode_rows = modes.shape[:3]
    width = math.gcd(lanes, 4 * skips.shape[1])
    lines = second.shape[1]

    def mine(table):
        return pl.BlockSpec((1,) + table.shape[1:], lambda i, me: (me[0], 0, 0))

    if layer == LAYERS - 1:
        out_specs = [
            pl.BlockSpec((rows // 16, width // 128, 16, 128), lambda i, me: (0, i, 0, 0)),
        ]
        out_shape = [jax.ShapeDtypeStruct((rows // 16, lanes // 128, 16, 128), BF16)]
    else:
        out_specs = [
            pl.BlockSpec((rows, width), lambda i, me: (0, i)),
            pl.BlockSpec((kinds, parts, lines, width), lambda i, me: (0, 0, 0, i)),
        ]
        out_shape = [
            jax.ShapeDtypeStruct((rows, lanes), BF16),
            jax.ShapeDtypeStruct((kinds, parts, lines, lanes), BF16),
        ]
    return pl.pallas_call(
        functools.partial(layer_body, layer),
        grid_spec=pltpu.PrefetchScalarGridSpec(
            num_scalar_prefetch=1,
            grid=(lanes // width,),
            in_specs=[
                mine(second),
                mine(third),
                mine(third_pair),
                pl.BlockSpec((kinds, parts, mode_rows, width), lambda i, me: (0, 0, 0, i)),
                pl.BlockSpec((rows, width), lambda i, me: (0, i)),
                pl.BlockSpec(skips.shape, lambda i, me: (0, 0, 0)),
                pl.BlockSpec(biases.shape, lambda i, me: (0, 0)),
            ],
            out_specs=out_specs,
            scratch_shapes=[
                pltpu.VMEM((kinds * parts, lines, width), BF16),
                pltpu.VMEM((width, width), BF16),
            ],
        ),
        out_shape=out_shape,
        compiler_params=pltpu.CompilerParams(vmem_limit_bytes=32 * 1024 * 1024),
        name="layer_back",
    )(me, second, third, third_pair, modes, grid, skips, biases)


def unpack_body(places_ref, reply_ref, out_ref):
    def some(turn, carry):
        for way in range(WAYS):
            block = turn * WAYS + way
            out_ref[block] = reply_ref[places_ref[0, block]]
        return carry

    lax.fori_loop(0, out_ref.shape[0] // WAYS, some, 0)


def unpack_slots(places, reply):
    vmem = pl.BlockSpec(memory_space=pltpu.VMEM)
    return pl.pallas_call(
        unpack_body,
        grid_spec=pltpu.PrefetchScalarGridSpec(
            num_scalar_prefetch=1, grid=(1,), in_specs=[vmem], out_specs=vmem
        ),
        out_shape=jax.ShapeDtypeStruct(places.shape[1:] + reply.shape[1:], reply.dtype),
        compiler_params=pltpu.CompilerParams(vmem_limit_bytes=40 * 1024 * 1024),
        name="unpack_slots",
    )(places, reply)


def per_device(
    point_channel_values,
    point_offsets,
    point_counts,
    block_bricks,
    spectral_weights,
    skip_weights,
    skip_bias,
):
    mesh_rows = lax.axis_size("px")
    mesh_columns = lax.axis_size("py")
    device_total = mesh_rows * mesh_columns
    capacity = max(2, 2 * point_channel_values.shape[0] // device_total)
    channels, points = point_channel_values.shape[1:]
    x_dev, y_dev = NX // mesh_rows, NY // mesh_columns
    bricks_y = y_dev // 4
    bricks_z = NZ // 16
    bricks_device = x_dev // 2 * bricks_y * bricks_z
    slot_total = device_total * capacity
    wanted, places, facts = make_plan(
        block_bricks, point_counts, bricks_device, bricks_y, bricks_z, capacity, slot_total, points
    )
    tiles, got_notes = route(wanted, point_offsets, facts, point_channel_values)
    lanes = x_dev * channels
    tiles_x, tiles_z = lanes // 128, NZ // 16
    lift = tiles_z * tiles_x
    bases = find_spots(got_notes, tiles_x, tiles_z)

    kz_dev = MODES // mesh_columns
    ky_dev = MODES // mesh_rows
    parts = 1
    while ky_dev * kz_dev * 2 // (2 * parts) % 16 == 0 and kz_dev % (2 * parts) == 0 and parts < MOST_PARTS:
        parts *= 2
    third_pair, third_back, second, second_back, first_forward, first_back = all_tables(
        mesh_columns, parts
    )
    me = lax.axis_index("py").astype(jnp.int32).reshape(1)
    grid, third_found = gather_grid(
        bases, me, tiles, third_pair, y_dev * NZ, lanes, mesh_columns, parts, lift, capacity
    )
    for layer in range(LAYERS):
        modes = spectral(
            layer, second, first_forward, first_back, third_found, spectral_weights, parts
        )
        found = layer_back(
            layer,
            me,
            second_back,
            third_back,
            third_pair,
            modes,
            grid,
            skip_weights,
            skip_bias,
        )
        grid, third_found = found[0], found[-1]
    grid = grid.reshape(-1, 16, 128)
    reply = decode(bases, grid, got_notes, slot_total, channels, lift)
    return unpack_slots(places, reply)


def solution(mesh):
    return jax.shard_map(
        per_device,
        mesh=mesh,
        in_specs=(
            P(("px", "py"), None, None),
            P(("px", "py"), None, None),
            P(("px", "py")),
            P(("px", "py"), None),
            P(None, None, "px", "py", None, None),
            P(),
            P(),
        ),
        out_specs=P(("px", "py"), None, None),
        check_vma=False,
    )
```

```python
import functools
import math

import jax
import jax.numpy as jnp
import ml_dtypes
import numpy as np
from jax import lax
from jax.experimental import pallas as pl
from jax.experimental.pallas import tpu as pltpu
from jax.sharding import PartitionSpec as P

MODES = 32
NX = 128
NY = 128
NZ = 128
LAYERS = 2

AMPLITUDE = 0.25
SPREAD = 4.5
DECODE_SCALE = 0.1
CHUNKS = 2
MOST_PARTS = 4
WAYS = 4
VMEM_LIMIT = 60 * 1024 * 1024
F32 = jnp.float32
BF16 = jnp.bfloat16


def wave_numbers(kept_modes):
    position = np.arange(kept_modes)
    return np.where(position < kept_modes // 2, position, position - kept_modes)


def forward_matrix(length, frequency):
    angles = 2.0 * math.pi / length * (np.arange(length)[:, None] * frequency[None, :] % length)
    cosine = np.cos(angles) / math.sqrt(length)
    sine_part = np.sin(angles) / math.sqrt(length)
    from_real = np.stack([cosine, -sine_part], axis=-1)
    from_imag = np.stack([sine_part, cosine], axis=-1)
    return np.stack([from_real, from_imag], axis=1)


def unit_angles(products, length):
    return 2.0 * math.pi / length * (products % length)


def repeat_lines(table, slabs, copies):
    rows, depth = table.shape
    span = rows // slabs
    same = np.eye(copies, dtype=bool)[None, :, None, :, None]
    wide = np.where(same, table.reshape(slabs, 1, span, 1, depth), 0.0)
    return wide.reshape(rows * copies, copies * depth)


def constant(table):
    return jnp.asarray(np.asarray(table).astype(ml_dtypes.bfloat16))


def third_tables(kinds, parts, me_y):
    kz_dev = MODES // kinds
    index = np.arange(2 * MODES)
    kz = index // 2 % kz_dev + kz_dev * (index // (2 * kz_dev) ^ me_y)
    angle = unit_angles(kz[:, None] * np.arange(NZ)[None, :], NZ)
    third = np.where((index % 2 == 0)[:, None], np.cos(angle), -np.sin(angle)) / math.sqrt(NZ)
    fold = np.where(kz == 0, 1.0, 2.0)[:, None]
    span = 2 * kz_dev // parts
    return (
        repeat_lines(third, kinds * parts, 2),
        repeat_lines(third * fold, kinds * parts, 16 // span).T,
    )


def second_table(kinds, parts, me_y):
    span = 2 * MODES // kinds // parts
    y_dev = NY // kinds
    row = np.arange(MODES * span)[:, None]
    column = np.arange(y_dev * span)[None, :]
    ky = wave_numbers(MODES)[row // span]
    angle = unit_angles(ky * (me_y * y_dev + column // span), NY)
    sine = np.where(row % 2 == 0, np.sin(angle), -np.sin(angle))
    second = np.where(row % 2 == column % 2, np.cos(angle), sine) / math.sqrt(NY)
    return np.where(row % span // 2 == column % span // 2, second, 0.0)


def all_tables(kinds, parts):
    third = [third_tables(kinds, parts, me_y) for me_y in range(kinds)]
    second = np.stack([second_table(kinds, parts, me_y) for me_y in range(kinds)])
    by_pair = forward_matrix(NX, wave_numbers(MODES)).reshape(NX // 2, 2, 2, MODES, 2)
    first_forward = by_pair.transpose(1, 3, 4, 2, 0).reshape(4 * MODES, NX)
    turned = np.stack([by_pair[..., 1], -by_pair[..., 0]], axis=-1)
    first_back = np.stack([by_pair, turned], axis=0).transpose(2, 0, 3, 1, 4, 5)
    return [
        constant(table)
        for table in (
            np.stack([one[0] for one in third]),
            np.stack([one[1] for one in third]),
            second,
            second.transpose(0, 2, 1),
            first_forward,
            first_back.reshape(4 * NX, 2 * MODES),
        )
    ]


def gelu(value):
    return 0.5 * value * (1.0 + lax.erf(value * math.sqrt(0.5)))


def block_values(offsets, shift_of, count, points):
    lanes = lax.broadcasted_iota(jnp.int32, (1, points), 1).astype(F32)
    amplitude = jnp.where(lanes < count, AMPLITUDE, 0.0).astype(F32)

    def part(dim, brick, cells, scale):
        center = lax.broadcasted_iota(jnp.int32, (cells, points), 0).astype(F32) + 0.5
        apart = (offsets[dim : dim + 1, :] - shift_of(dim, brick) * scale) - center
        return jnp.exp(apart * apart * (-1.0 / SPREAD))

    rows = []
    for brick in range(4):
        along_x = part(0, brick, 2, 2.0) * amplitude
        along_y = part(1, brick, 4, 4.0)
        along_z = part(2, brick, 16, 16.0)
        for cy in range(4):
            plane = along_z * along_y[cy : cy + 1, :]
            rows.append(
                jnp.concatenate(
                    [plane * along_x[0:1, :], plane * along_x[1:2, :]], axis=1
                ).astype(BF16)
            )
    return jnp.concatenate(rows, axis=0)


def note_values(notes, slot, points):
    facts = notes[4 * slot + 3 : 4 * slot + 4, :]
    return block_values(
        notes[4 * slot : 4 * slot + 3, :],
        lambda dim, brick: facts[:, 3 * brick + dim : 3 * brick + dim + 1]
        - facts[:, dim : dim + 1],
        facts[:, 12:13],
        points,
    )


def bits(size):
    return size.bit_length() - 1


def plan_body(bricks_y, bricks_z, capacity, brick_ref, count_ref, wanted_ref, place_ref, fact_ref):
    blocks = brick_ref.shape[0]
    slots = wanted_ref.shape[1]
    bricks_device = bricks_y[1]
    bricks_y = bricks_y[0]
    brick = brick_ref[...]
    down = lax.broadcasted_iota(jnp.int32, (blocks, blocks), 0)
    across = lax.broadcasted_iota(jnp.int32, (blocks, blocks), 1)
    owner_column = lax.shift_right_logical(brick[:, 0:1], jnp.int32(bits(bricks_device)))
    diagonal = down == across
    owner_row = jnp.sum(jnp.where(diagonal, owner_column, 0), axis=0, keepdims=True)
    same = owner_column == owner_row
    rank_row = jnp.sum(jnp.where(same & (down < across), 1, 0), axis=0, keepdims=True)
    rank_column = jnp.sum(jnp.where(same & (across < down), 1, 0), axis=1, keepdims=True)
    place_ref[...] = owner_row * capacity + rank_row
    slot = owner_column * capacity + rank_column
    slot_at = lax.broadcasted_iota(jnp.int32, (blocks, slots), 1)
    block_at = lax.broadcasted_iota(jnp.int32, (blocks, slots), 0) + 1
    wanted_ref[...] = jnp.sum(jnp.where(slot == slot_at, block_at, 0), axis=0, keepdims=True) - 1
    local = brick & (bricks_device - 1)
    parts = (
        lax.shift_right_logical(local, jnp.int32(bits(bricks_y * bricks_z))),
        lax.shift_right_logical(local, jnp.int32(bits(bricks_z))) & (bricks_y - 1),
        local & (bricks_z - 1),
    )
    count = jnp.sum(jnp.where(diagonal, count_ref[...], 0), axis=1, keepdims=True)
    lane = lax.broadcasted_iota(jnp.int32, (blocks, fact_ref.shape[2]), 1)
    facts = jnp.where(lane == 12, count, 0)
    for at in range(4):
        for dim in range(3):
            facts = jnp.where(lane == 3 * at + dim, parts[dim][:, at : at + 1], facts)
    fact_ref[...] = facts.astype(F32).reshape(fact_ref.shape)


def make_plan(bricks, counts, bricks_device, bricks_y, bricks_z, capacity, slots, points):
    blocks = bricks.shape[0]
    vmem = pl.BlockSpec(memory_space=pltpu.VMEM)
    return pl.pallas_call(
        functools.partial(plan_body, (bricks_y, bricks_device), bricks_z, capacity),
        in_specs=[vmem] * 2,
        out_specs=[vmem] * 3,
        out_shape=[
            jax.ShapeDtypeStruct((1, slots), jnp.int32),
            jax.ShapeDtypeStruct((1, blocks), jnp.int32),
            jax.ShapeDtypeStruct((blocks, 1, points), F32),
        ],
        name="make_plan",
    )(bricks, counts.reshape(1, blocks))


def spot_body(tiles_x, tiles_z, note_ref, base_ref, wide_ref):
    wide_ref[...] = note_ref[...].reshape(wide_ref.shape).astype(F32)
    facts = wide_ref[pl.ds(3, wide_ref.shape[0] // 4, stride=4), :].T
    rows = []
    for at in range(4):
        cell_x, cell_y, cell_z = (facts[3 * at + dim : 3 * at + dim + 1, :] for dim in range(3))
        rows.append((cell_y * (4 * tiles_z) + cell_z) * tiles_x + cell_x)
    base_ref[...] = jnp.concatenate(rows, axis=0).astype(jnp.int32)


def find_spots(notes, tiles_x, tiles_z):
    rows = notes.shape[0] * notes.shape[1]
    vmem = pl.BlockSpec(memory_space=pltpu.VMEM)
    return pl.pallas_call(
        functools.partial(spot_body, tiles_x, tiles_z),
        in_specs=[vmem],
        out_specs=vmem,
        out_shape=jax.ShapeDtypeStruct((4, rows // 4), jnp.int32),
        scratch_shapes=[pltpu.VMEM((rows, notes.shape[2]), F32)],
        name="find_spots",
    )(notes)


def near_at(index, devices):
    return (7 * index) % (devices // 2)


def far_at(index, devices):
    return devices // 2 + (7 * index + devices // 3) % (devices // 2)


def mask_at(turn, devices):
    index, far = turn // 2, turn % 2
    return far * far_at(index, devices) + (1 - far) * near_at(index, devices)


def crossed(value, mask, size):
    result, bit = 0, 1
    while bit < size:
        result = result + bit * ((value // bit + mask // bit) % 2)
        bit *= 2
    return result


def route_body(
    size_x,
    size_y,
    source_ref,
    offset_ref,
    fact_ref,
    feature_ref,
    tile_ref,
    got_note_ref,
    feature_send,
    feature_got,
    note_send,
    tile_held,
    feature_ssem,
    feature_rsem,
    note_ssem,
    note_rsem,
    tile_sem,
):
    slots, channels, points = feature_send.shape
    devices = size_x * size_y
    capacity = slots // devices
    ways = math.gcd(WAYS, capacity)
    note_rows = note_send.shape[1]
    me = lax.axis_index("px") * size_y + lax.axis_index("py")
    barrier = pltpu.get_barrier_semaphore()

    def greet(mask, carry):
        other = crossed(me, mask, devices)
        pl.semaphore_signal(
            barrier,
            inc=1,
            device_id={"px": other // size_y, "py": other % size_y},
            device_id_type=pl.DeviceIdType.MESH,
        )
        return carry

    lax.fori_loop(1, devices, greet, 0)

    def transfers(mask):
        other = crossed(me, mask, devices)
        there = {"px": other // size_y, "py": other % size_y}
        return (
            pltpu.make_async_remote_copy(
                src_ref=note_send.at[other],
                dst_ref=got_note_ref.at[me],
                send_sem=note_ssem.at[mask],
                recv_sem=note_rsem.at[mask],
                device_id=there,
                device_id_type=pl.DeviceIdType.MESH,
            ),
            pltpu.make_async_remote_copy(
                src_ref=feature_send.at[pl.ds(other * capacity, capacity)],
                dst_ref=feature_got.at[pl.ds(me * capacity, capacity)],
                send_sem=feature_ssem.at[mask],
                recv_sem=feature_rsem.at[mask],
                device_id=there,
                device_id_type=pl.DeviceIdType.MESH,
            ),
        )

    def pack(other, notes_to, features_to):
        notes = []
        for slot in range(capacity):
            source = source_ref[0, other * capacity + slot]
            present = source >= 0
            source = jnp.maximum(source, 0)
            feature = feature_ref[source]
            features_to[other * capacity + slot] = jnp.where(
                present, feature, jnp.zeros_like(feature)
            )
            note = jnp.concatenate([offset_ref[source].astype(F32), fact_ref[source]], axis=0)
            notes.append(jnp.where(present, note, 0.0))
        if note_rows > 4 * capacity:
            notes.append(jnp.zeros((note_rows - 4 * capacity, points), F32))
        notes_to[other] = jnp.concatenate(notes, axis=0).astype(BF16)

    first = mask_at(1, devices)
    pack(crossed(me, first, devices), note_send, feature_send)
    pl.semaphore_wait(barrier, devices - 1)
    for copy in transfers(first):
        copy.start()

    def launch(turn, carry):
        mask = mask_at(turn, devices)
        pack(crossed(me, mask, devices), note_send, feature_send)
        for copy in transfers(mask):
            copy.start()
        return carry

    lax.fori_loop(2, devices, launch, 0)
    pack(me, got_note_ref, feature_got)

    def tile_copy(turn, other):
        return pltpu.make_async_copy(
            tile_held.at[turn % 2],
            tile_ref.at[pl.ds(other * capacity, capacity)],
            tile_sem.at[turn % 2],
        )

    def work(turn, other):
        notes = got_note_ref[other].astype(F32)
        for start in range(0, capacity, ways):
            tiles = []
            for slot in range(start, start + ways):
                values = note_values(notes, slot, points)
                feature = feature_got[other * capacity + slot]
                empty = jnp.zeros_like(feature)
                pair = jnp.concatenate(
                    [
                        jnp.concatenate([feature, empty], axis=1),
                        jnp.concatenate([empty, feature], axis=1),
                    ],
                    axis=0,
                )
                tiles.append(
                    lax.dot_general(
                        values, pair, (((1,), (1,)), ((), ())), preferred_element_type=F32
                    ).astype(BF16)
                )
            for way in range(ways):
                tile_held[turn % 2, start + way] = tiles[way]
        tile_copy(turn, other).start()

    work(0, me)

    def step(mask_of, turn, carry):
        mask = mask_of(turn % (devices // 2), devices)
        for copy in transfers(mask):
            copy.wait_recv()

        @pl.when(turn >= 2)
        def _():
            tile_copy(turn, me).wait()

        work(turn, crossed(me, mask, devices))
        return carry

    lax.fori_loop(1, devices // 2, functools.partial(step, near_at), 0)
    lax.fori_loop(devices // 2, devices, functools.partial(step, far_at), 0)
    for turn in range(devices - 2, devices):
        tile_copy(turn, me).wait()

    def leave(mask, carry):
        for copy in transfers(mask):
            copy.wait_send()
        return carry

    lax.fori_loop(1, devices, leave, 0)


def route(sources, offsets, facts, features):
    slots = sources.shape[1]
    channels, points = features.shape[1:]
    size_x, size_y = lax.axis_size("px"), lax.axis_size("py")
    devices = size_x * size_y
    capacity = slots // devices
    note_rows = (4 * capacity + 15) // 16 * 16
    vmem = pl.BlockSpec(memory_space=pltpu.VMEM)
    dma = pltpu.SemaphoreType.DMA
    return pl.pallas_call(
        functools.partial(route_body, size_x, size_y),
        in_specs=[pl.BlockSpec(memory_space=pltpu.SMEM), vmem, vmem, vmem],
        out_specs=[pl.BlockSpec(memory_space=pl.ANY), vmem],
        out_shape=[
            jax.ShapeDtypeStruct((slots, 256, 2 * channels), BF16),
            jax.ShapeDtypeStruct((devices, note_rows, points), BF16),
        ],
        scratch_shapes=[
            pltpu.VMEM((slots, channels, points), BF16),
            pltpu.VMEM((slots, channels, points), BF16),
            pltpu.VMEM((devices, note_rows, points), BF16),
            pltpu.VMEM((2, capacity, 256, 2 * channels), BF16),
            dma((devices,)),
            dma((devices,)),
            dma((devices,)),
            dma((devices,)),
            dma((2,)),
        ],
        compiler_params=pltpu.CompilerParams(
            vmem_limit_bytes=VMEM_LIMIT, collective_id=LAYERS + 1, has_side_effects=True
        ),
        name="route",
    )(sources, offsets, facts, features)


def find_third(third_ref, lines_of, out_ref, columns):
    kinds, parts, lines = out_ref.shape[:3]
    both = third_ref.shape[0]
    span = both // (2 * kinds * parts)
    turns = 16 // (2 * span)

    def some(turn, carry):
        found = [
            jnp.dot(third_ref[...], lines_of(turn * turns + way), preferred_element_type=F32)
            for way in range(turns)
        ]
        row = pl.multiple_of(turn * 16, 16)
        for slab in range(kinds * parts):
            piece = [one[slab * 2 * span : (slab + 1) * 2 * span, :] for one in found]
            piece = piece[0] if turns == 1 else jnp.concatenate(piece, axis=0)
            out_ref[slab // parts, slab % parts, pl.ds(row, 16), columns] = piece.astype(BF16)
        return carry

    lax.fori_loop(0, lines // 16, some, 0, unroll=True)


def gather_body(
    group, steps, lift, capacity, base_ref, me_ref, tile_ref, third_ref, out_ref, modes_ref, total_ref
):
    step = pl.program_id(0)
    lanes = out_ref.shape[1]
    depth = third_ref.shape[2] // 2
    tiles = lanes // 128

    @pl.when(step == 0)
    def _():
        total_ref[...] = jnp.zeros_like(total_ref)

    def some(turn, carry):
        for way in range(WAYS):
            member = turn * WAYS + way
            slot = step * group + member
            room = base_ref.shape[1] * capacity // (steps * group)
            spot = slot if room == capacity else slot // capacity * room + slot % capacity
            bases = [base_ref[brick, spot] for brick in range(4)]
            places = [base + cy * lift for base in bases for cy in range(4)]
            sums = [
                total_ref[place] + tile_ref[member, 16 * at : 16 * at + 16, :].astype(F32)
                for at, place in enumerate(places)
            ]
            for place, value in zip(places, sums):
                total_ref[place] = value
        return carry

    lax.fori_loop(0, group // WAYS, some, 0, unroll=2)

    @pl.when(step == steps - 1)
    def _():
        width = math.gcd(lanes, 256)
        pieces = width // 128

        def tile(turn, carry):
            columns = pl.ds(pl.multiple_of(turn * width, width), width)

            def lines_of(pair):
                place = pl.ds(pl.multiple_of(pair * 2 * depth, 2 * depth), 2 * depth)
                rows = []
                for at in range(2 * depth // 16):
                    here = (pair * (2 * depth // 16) + at) * tiles + turn * pieces
                    rows.append(
                        jnp.concatenate([total_ref[here + to] for to in range(pieces)], axis=1)
                    )
                value = jnp.concatenate(rows, axis=0).astype(BF16)
                out_ref[place, columns] = value
                return value

            find_third(third_ref.at[0], lines_of, modes_ref, columns)
            return carry

        lax.fori_loop(0, lanes // width, tile, 0)


def gather_grid(bases, me, tiles, third_pair, rows, lanes, kinds, parts, lift, capacity):
    slots = tiles.shape[0]
    group = math.gcd(slots, 32)
    depth = third_pair.shape[2] // 2
    lines = rows // depth * third_pair.shape[1] // (2 * kinds * parts)
    return pl.pallas_call(
        functools.partial(gather_body, group, slots // group, lift, capacity),
        grid_spec=pltpu.PrefetchScalarGridSpec(
            num_scalar_prefetch=2,
            grid=(slots // group,),
            in_specs=[
                pl.BlockSpec((group,) + tiles.shape[1:], lambda i, base, me: (i, 0, 0)),
                pl.BlockSpec((1,) + third_pair.shape[1:], lambda i, base, me: (me[0], 0, 0)),
            ],
            out_specs=[
                pl.BlockSpec((rows, lanes), lambda i, base, me: (0, 0)),
                pl.BlockSpec((kinds, parts, lines, lanes), lambda i, base, me: (0, 0, 0, 0)),
            ],
            scratch_shapes=[pltpu.VMEM((rows * lanes // 2048, 16, 128), F32)],
        ),
        out_shape=[
            jax.ShapeDtypeStruct((rows, lanes), BF16),
            jax.ShapeDtypeStruct((kinds, parts, lines, lanes), BF16),
        ],
        compiler_params=pltpu.CompilerParams(vmem_limit_bytes=46 * 1024 * 1024),
        name="gather_grid",
    )(bases, me, tiles, third_pair)


def decode_body(size_x, size_y, lift, base_ref, held_ref, note_ref, got_ref, reply_ref, ssem, rsem, own_sem):
    slots, channels, points = got_ref.shape
    devices = size_x * size_y
    capacity = slots // devices
    ways = math.gcd(WAYS, capacity)
    me_x, me_y = lax.axis_index("px"), lax.axis_index("py")
    me = me_x * size_y + me_y
    barrier = pltpu.get_barrier_semaphore()

    def greet(mask, carry):
        other = crossed(me, mask, devices)
        pl.semaphore_signal(
            barrier,
            inc=1,
            device_id={"px": other // size_y, "py": other % size_y},
            device_id_type=pl.DeviceIdType.MESH,
        )
        return carry

    lax.fori_loop(1, devices, greet, 0)

    def transfer(mask):
        other = crossed(me, mask, devices)
        return pltpu.make_async_remote_copy(
            src_ref=reply_ref.at[pl.ds(other * capacity, capacity)],
            dst_ref=got_ref.at[pl.ds(me * capacity, capacity)],
            send_sem=ssem.at[mask],
            recv_sem=rsem.at[mask],
            device_id={"px": other // size_y, "py": other % size_y},
            device_id_type=pl.DeviceIdType.MESH,
        )

    room = base_ref.shape[1] // devices

    def fill(other):
        notes = note_ref[other].astype(F32)
        for start in range(0, capacity, ways):
            results = []
            for slot in range(start, start + ways):
                values = note_values(notes, slot, points)
                bases = [base_ref[brick, other * room + slot] for brick in range(4)]
                cells = jnp.concatenate(
                    [held_ref[base + cy * lift] for base in bases for cy in range(4)], axis=0
                )
                both = lax.dot_general(
                    cells, values, (((0,), (0,)), ((), ())), preferred_element_type=F32
                )
                summed = both[:channels, :points] + both[channels:, points:]
                results.append((DECODE_SCALE * summed).astype(BF16))
            for way in range(ways):
                reply_ref[other * capacity + start + way] = results[way]

    first = mask_at(1, devices)
    fill(crossed(me, first, devices))
    pl.semaphore_wait(barrier, devices - 1)
    transfer(first).start()

    def step(turn, carry):
        mask = mask_at(turn, devices)
        fill(crossed(me, mask, devices))
        transfer(mask).start()
        return carry

    lax.fori_loop(2, devices, step, 0)
    fill(me)
    mine = pl.ds(me * capacity, capacity)
    own = pltpu.make_async_copy(reply_ref.at[mine], got_ref.at[mine], own_sem)
    own.start()
    own.wait()

    def finish(mask, carry):
        transfer(mask).wait_recv()
        return carry

    lax.fori_loop(1, devices, finish, 0)

    def leave(mask, carry):
        transfer(mask).wait_send()
        return carry

    lax.fori_loop(1, devices, leave, 0)


def decode(bases, grid, notes, slots, channels, lift):
    points = notes.shape[2]
    size_x, size_y = lax.axis_size("px"), lax.axis_size("py")
    devices = size_x * size_y
    vmem = pl.BlockSpec(memory_space=pltpu.VMEM)
    return pl.pallas_call(
        functools.partial(decode_body, size_x, size_y, lift),
        in_specs=[pl.BlockSpec(memory_space=pltpu.SMEM), vmem, vmem],
        out_specs=vmem,
        out_shape=jax.ShapeDtypeStruct((slots, channels, points), BF16),
        scratch_shapes=[
            pltpu.VMEM((slots, channels, points), BF16),
            pltpu.SemaphoreType.DMA((devices,)),
            pltpu.SemaphoreType.DMA((devices,)),
            pltpu.SemaphoreType.DMA,
        ],
        compiler_params=pltpu.CompilerParams(
            vmem_limit_bytes=24 * 1024 * 1024, collective_id=LAYERS, has_side_effects=True
        ),
        name="decode",
    )(bases, grid, notes)


def partner(me, distance):
    return me + distance - 2 * distance * ((me // distance) % 2)


def spectral_body(
    layer,
    second_ref,
    forward_ref,
    backward_ref,
    third_ref,
    weight_ref,
    modes_ref,
    held_ref,
    sums_send,
    sums_recv,
    lines_send,
    lines_recv,
    back_send,
    weight_held,
    wide_in,
    wide_out,
    sums_ssem,
    sums_rsem,
    lines_ssem,
    lines_rsem,
    back_ssem,
    back_rsem,
    modes_ssem,
    modes_rsem,
    weight_sem,
):
    kinds, parts, rows, lanes = modes_ref.shape
    devices_x, slab_rows = lines_send.shape[1:3]
    pairs_x = lanes // 128
    channels = weight_held.shape[4]
    kz_part = weight_held.shape[3]
    kx_all = weight_held.shape[1]
    me_x, me_y = lax.axis_index("px"), lax.axis_index("py")
    steps = kinds.bit_length() - 1
    tile = math.gcd(lanes, 256)
    lane_tiles = lanes // tile
    batch = 8
    weight_copies = []
    for part in range(parts):
        copy = pltpu.make_async_copy(
            weight_ref.at[layer, :, :, pl.ds(part * kz_part, kz_part)],
            weight_held.at[part],
            weight_sem.at[part],
        )
        copy.start()
        weight_copies.append(copy)

    def at_x(device):
        return {"px": device}

    def at_y(distance):
        return {"py": partner(me_y, distance)}

    barrier = pltpu.get_barrier_semaphore()
    for hop in range(1, devices_x):
        pl.semaphore_signal(
            barrier,
            inc=1,
            device_id=at_x((me_x + hop) % devices_x),
            device_id_type=pl.DeviceIdType.MESH,
        )
    for step in range(steps):
        pl.semaphore_signal(
            barrier, inc=1, device_id=at_y(1 << step), device_id_type=pl.DeviceIdType.MESH
        )

    started = []

    def send(source, target, ssem, rsem, device):
        copy = pltpu.make_async_remote_copy(
            src_ref=source,
            dst_ref=target,
            send_sem=ssem,
            recv_sem=rsem,
            device_id=device,
            device_id_type=pl.DeviceIdType.MESH,
        )
        copy.start()
        started.append(copy)
        return copy

    bases = [kinds - (kinds >> step) for step in range(steps)]
    sums_copies, lines_copies, back_copies, modes_copies = {}, {}, {}, {}

    def send_sums(part, step):
        count = kinds >> (step + 1)
        at = pl.ds(bases[step], count)
        sums_copies[part, step] = send(
            sums_send.at[part, at],
            sums_recv.at[part, at],
            sums_ssem.at[part, step],
            sums_rsem.at[part, step],
            at_y(1 << step),
        )

    def second_stage(part):
        def one(turn, carry):
            columns = pl.ds(pl.multiple_of(turn * tile, tile), tile)
            for kind in range(kinds - 1, -1, -1):
                value = jnp.dot(
                    second_ref[me_y], third_ref[kind, part, :, columns], preferred_element_type=F32
                )
                if kind % 2:
                    sums_send[part, kind // 2, :, columns] = value.astype(BF16)
                else:
                    held_ref[part, kind // 2, :, columns] = value
            return carry

        lax.fori_loop(0, lane_tiles, one, 0)
        send_sums(part, 0)

    def sum_stage(part, step):
        sums_copies[part, step].wait_recv()

        def one(turn, carry):
            columns = pl.ds(pl.multiple_of(turn * tile, tile), tile)
            for index in range(kinds >> (step + 1)):
                kind = index << (step + 1)
                value = held_ref[part, kind // 2, :, columns] + sums_recv[
                    part, bases[step] + index, :, columns
                ].astype(F32)
                if index % 2:
                    sums_send[part, bases[step + 1] + index // 2, :, columns] = value.astype(BF16)
                elif step + 1 < steps:
                    held_ref[part, kind // 2, :, columns] = value
                else:
                    lines_send[part, :, :, columns] = value.astype(BF16).reshape(
                        devices_x, slab_rows, tile
                    )
            return carry

        lax.fori_loop(0, lane_tiles, one, 0)
        if step + 1 < steps:
            send_sums(part, step + 1)
            return
        for hop in range(1, devices_x):
            target = (me_x + hop) % devices_x
            lines_copies[part, hop] = send(
                lines_send.at[part, target],
                lines_recv.at[part, me_x],
                lines_ssem.at[part, hop],
                lines_rsem.at[part, hop],
                at_x(target),
            )
        lines_recv[part, me_x] = lines_send[part, me_x]

    half_lane = lax.broadcasted_iota(jnp.int32, (1, 128), 1) < channels

    def mix_stage(part):
        for hop in range(1, devices_x):
            lines_copies[part, hop].wait_recv()
        weight_copies[part].wait()

        def widen(source, carry):
            for pair in range(pairs_x):
                row = pl.multiple_of((source * pairs_x + pair) * slab_rows, slab_rows)
                wide_in[pl.ds(row, slab_rows), :] = lines_recv[
                    part, source, :, pair * 128 : (pair + 1) * 128
                ].astype(F32)
            return carry

        lax.fori_loop(0, devices_x, widen, 0)
        count = devices_x * pairs_x
        modes_rows = 2 * kx_all
        row_at = lax.broadcasted_iota(jnp.int32, (modes_rows, batch * channels), 0)
        lane_at = lax.broadcasted_iota(jnp.int32, (modes_rows, batch * channels), 1)
        own = (row_at // 2) % batch == lane_at // channels

        def one(pick, carry):
            ky, kz = pick // kz_part, pick % kz_part
            line = jnp.concatenate(
                [
                    wide_in[pl.ds(2 * pick, count, stride=slab_rows), :],
                    wide_in[pl.ds(2 * pick + 1, count, stride=slab_rows), :],
                ],
                axis=0,
            ).astype(BF16)
            first = jnp.dot(forward_ref[...], line, preferred_element_type=F32)
            first = jnp.where(half_lane, first[:modes_rows], first[modes_rows:])
            first = first + pltpu.roll(first, channels, 1)
            spread = jnp.where(own, jnp.concatenate([first] * (batch // 2), axis=1), 0.0)
            spread = spread.astype(BF16)
            mixed = []
            for at in range(kx_all // batch):
                weight = weight_held[part, at * batch : (at + 1) * batch, ky, kz]
                mixed.append(
                    jnp.dot(
                        spread[2 * at * batch : 2 * (at + 1) * batch],
                        weight.reshape(batch * channels, 2 * channels),
                        preferred_element_type=F32,
                    )
                )
            mixed = jnp.concatenate(mixed, axis=0).astype(BF16)
            back = jnp.dot(backward_ref[...], mixed, preferred_element_type=F32)
            size = 2 * count
            part_at = [back[at * size : (at + 1) * size] for at in range(4)]
            final = jnp.where(half_lane, part_at[0], part_at[3]) + pltpu.roll(
                jnp.where(half_lane, part_at[2], part_at[1]), channels, 1
            )
            wide_out[pl.ds(2 * pick, count, stride=slab_rows), :] = final[:count]
            wide_out[pl.ds(2 * pick + 1, count, stride=slab_rows), :] = final[count:]
            return carry

        lax.fori_loop(0, slab_rows // 2, one, 0, unroll=2)

        def narrow(target, carry):
            for pair in range(pairs_x):
                row = pl.multiple_of((target * pairs_x + pair) * slab_rows, slab_rows)
                back_send[part, target, :, pair * 128 : (pair + 1) * 128] = wide_out[
                    pl.ds(row, slab_rows), :
                ].astype(BF16)
            return carry

        lax.fori_loop(0, devices_x, narrow, 0)
        mine = pl.ds(pl.multiple_of(me_x * slab_rows, slab_rows), slab_rows)
        for hop in range(1, devices_x):
            target = (me_x + hop) % devices_x
            back_copies[part, hop] = send(
                back_send.at[part, target],
                modes_ref.at[0, part, mine],
                back_ssem.at[part, hop],
                back_rsem.at[part, hop],
                at_x(target),
            )
        modes_ref[0, part, mine, :] = back_send[part, me_x]

    def spread_stage(part, kind):
        if kind == 0:
            for hop in range(1, devices_x):
                back_copies[part, hop].wait_recv()
            limit = kinds
        else:
            modes_copies[part, kind].wait_recv()
            limit = kind & -kind
        distance = limit // 2
        while distance >= 1:
            modes_copies[part, kind + distance] = send(
                modes_ref.at[kind, part],
                modes_ref.at[kind + distance, part],
                modes_ssem.at[part, kind + distance],
                modes_rsem.at[part, kind + distance],
                at_y(distance),
            )
            distance //= 2

    order = []
    for part in range(parts):
        order.append((1.5 * part, second_stage, (part,)))
        for step in range(steps):
            order.append((1.5 * part + 6.0 if step == 0 else 12.0 * step + 5.0 * part, sum_stage, (part, step)))
        base = 12.0 * (steps - 1) + 5.0 * part
        order.append((base + 7.1, mix_stage, (part,)))
        order.append((base + 13.0, spread_stage, (part, 0)))
        level = kinds // 2
        while level >= 1:
            for kind in range(level, kinds, 2 * level):
                late = 6.0 * (kinds // level).bit_length()
                order.append((base + 13.1 + late, spread_stage, (part, kind)))
            level //= 2
    order.sort(key=lambda entry: entry[0])
    waited = False
    for _, stage, given in order:
        stage_first = stage is second_stage and given == (0,)
        if stage_first and not waited:
            pl.semaphore_wait(barrier, devices_x - 1 + steps)
            waited = True
        stage(*given)
    for copy in started:
        copy.wait_send()


def spectral(layer, second, first_forward, first_back, third, weights, parts):
    kinds, _, lines, lanes = third.shape
    rows = second.shape[1]
    devices_x = lax.axis_size("px")
    slab_rows = rows // devices_x
    _, kx_all, ky_dev, kz_dev, channels, wide = weights.shape
    steps = kinds.bit_length() - 1
    count = devices_x * lanes // 128 * slab_rows
    dma = pltpu.SemaphoreType.DMA
    return pl.pallas_call(
        functools.partial(spectral_body, layer),
        in_specs=[pl.BlockSpec(memory_space=pltpu.VMEM)] * 4 + [pl.BlockSpec(memory_space=pl.ANY)],
        out_specs=pl.BlockSpec(memory_space=pltpu.VMEM),
        out_shape=jax.ShapeDtypeStruct((kinds, parts, rows, lanes), BF16),
        scratch_shapes=[
            pltpu.VMEM((parts, kinds // 2, rows, lanes), F32),
            pltpu.VMEM((parts, kinds - 1, rows, lanes), BF16),
            pltpu.VMEM((parts, kinds - 1, rows, lanes), BF16),
            pltpu.VMEM((parts, devices_x, slab_rows, lanes), BF16),
            pltpu.VMEM((parts, devices_x, slab_rows, lanes), BF16),
            pltpu.VMEM((parts, devices_x, slab_rows, lanes), BF16),
            pltpu.VMEM((parts, kx_all, ky_dev, kz_dev // parts, channels, wide), BF16),
            pltpu.VMEM((count, 128), F32),
            pltpu.VMEM((count, 128), F32),
            dma((parts, steps)),
            dma((parts, steps)),
            dma((parts, devices_x)),
            dma((parts, devices_x)),
            dma((parts, devices_x)),
            dma((parts, devices_x)),
            dma((parts, kinds)),
            dma((parts, kinds)),
            dma((parts,)),
        ],
        compiler_params=pltpu.CompilerParams(
            vmem_limit_bytes=35 * 1024 * 1024, collective_id=layer, has_side_effects=True
        ),
        name="spectral",
    )(second, first_forward, first_back, third, weights)


def layer_body(
    layer,
    me_ref,
    second_ref,
    third_ref,
    pair_ref,
    modes_ref,
    grid_ref,
    skip_ref,
    bias_ref,
    out_ref,
    *refs,
):
    held_ref, wide_ref = refs[-2:]
    tiled = len(out_ref.shape) == 4
    kinds, parts = modes_ref.shape[:2]
    slabs = kinds * parts
    lines = second_ref.shape[1]
    block = third_ref.shape[1]
    copies = wide_ref.shape[0] // skip_ref.shape[1]
    bias = jnp.concatenate([bias_ref[layer : layer + 1, :]] * copies, axis=1)

    @pl.when(pl.program_id(0) == 0)
    def _():
        skip = jnp.concatenate([skip_ref[layer].astype(F32)] * copies, axis=1)
        skip = jnp.concatenate([skip] * copies, axis=0)
        at_row = lax.broadcasted_iota(jnp.int32, wide_ref.shape, 0) // skip_ref.shape[1]
        at_lane = lax.broadcasted_iota(jnp.int32, wide_ref.shape, 1) // skip_ref.shape[1]
        wide_ref[...] = jnp.where(at_row == at_lane, skip, 0.0).astype(BF16)

    for slab in range(slabs):
        held_ref[slab] = jnp.dot(
            second_ref[0],
            modes_ref[slab // parts, slab % parts],
            preferred_element_type=F32,
        ).astype(BF16)

    def some(turn, carry):
        row = pl.ds(pl.multiple_of(turn * 16, 16), 16)
        line = jnp.concatenate([held_ref[slab, row, :] for slab in range(slabs)], axis=0)
        for way in range(block // 128):
            place = pl.ds(pl.multiple_of(turn * block + way * 128, 128), 128)
            spectral_part = jnp.dot(
                third_ref[0, way * 128 : (way + 1) * 128, :], line, preferred_element_type=F32
            )
            skipped = jnp.dot(grid_ref[place, :], wide_ref[...], preferred_element_type=F32)
            value = gelu(spectral_part + skipped + bias).astype(BF16)
            if tiled:
                row_tiles = pl.ds(turn * (block // 16) + way * 8, 8)
                for at in range(out_ref.shape[1]):
                    piece = value[:, at * 128 : (at + 1) * 128]
                    out_ref[row_tiles, at] = piece.reshape(8, 16, 128)
            else:
                out_ref[place, :] = value
        return carry

    lax.fori_loop(0, lines // 16, some, 0, unroll=True)
    if not tiled:
        pair = pair_ref.shape[2]

        def lines_of(at):
            return out_ref[pl.ds(pl.multiple_of(at * pair, pair), pair), :]

        find_third(pair_ref.at[0], lines_of, refs[0], slice(None))


def layer_back(layer, me, second, third, third_pair, modes, grid, skips, biases):
    rows, lanes = grid.shape
    kinds, parts, mode_rows = modes.shape[:3]
    width = math.gcd(lanes, 4 * skips.shape[1])
    lines = second.shape[1]

    def mine(table):
        return pl.BlockSpec((1,) + table.shape[1:], lambda i, me: (me[0], 0, 0))

    if layer == LAYERS - 1:
        out_specs = [
            pl.BlockSpec((rows // 16, width // 128, 16, 128), lambda i, me: (0, i, 0, 0)),
        ]
        out_shape = [jax.ShapeDtypeStruct((rows // 16, lanes // 128, 16, 128), BF16)]
    else:
        out_specs = [
            pl.BlockSpec((rows, width), lambda i, me: (0, i)),
            pl.BlockSpec((kinds, parts, lines, width), lambda i, me: (0, 0, 0, i)),
        ]
        out_shape = [
            jax.ShapeDtypeStruct((rows, lanes), BF16),
            jax.ShapeDtypeStruct((kinds, parts, lines, lanes), BF16),
        ]
    return pl.pallas_call(
        functools.partial(layer_body, layer),
        grid_spec=pltpu.PrefetchScalarGridSpec(
            num_scalar_prefetch=1,
            grid=(lanes // width,),
            in_specs=[
                mine(second),
                mine(third),
                mine(third_pair),
                pl.BlockSpec((kinds, parts, mode_rows, width), lambda i, me: (0, 0, 0, i)),
                pl.BlockSpec((rows, width), lambda i, me: (0, i)),
                pl.BlockSpec(skips.shape, lambda i, me: (0, 0, 0)),
                pl.BlockSpec(biases.shape, lambda i, me: (0, 0)),
            ],
            out_specs=out_specs,
            scratch_shapes=[
                pltpu.VMEM((kinds * parts, lines, width), BF16),
                pltpu.VMEM((width, width), BF16),
            ],
        ),
        out_shape=out_shape,
        compiler_params=pltpu.CompilerParams(vmem_limit_bytes=32 * 1024 * 1024),
        name="layer_back",
    )(me, second, third, third_pair, modes, grid, skips, biases)


def unpack_body(places_ref, reply_ref, out_ref):
    def some(turn, carry):
        for way in range(WAYS):
            block = turn * WAYS + way
            out_ref[block] = reply_ref[places_ref[0, block]]
        return carry

    lax.fori_loop(0, out_ref.shape[0] // WAYS, some, 0)


def unpack_slots(places, reply):
    vmem = pl.BlockSpec(memory_space=pltpu.VMEM)
    return pl.pallas_call(
        unpack_body,
        grid_spec=pltpu.PrefetchScalarGridSpec(
            num_scalar_prefetch=1, grid=(1,), in_specs=[vmem], out_specs=vmem
        ),
        out_shape=jax.ShapeDtypeStruct(places.shape[1:] + reply.shape[1:], reply.dtype),
        compiler_params=pltpu.CompilerParams(vmem_limit_bytes=40 * 1024 * 1024),
        name="unpack_slots",
    )(places, reply)


def per_device(
    point_channel_values,
    point_offsets,
    point_counts,
    block_bricks,
    spectral_weights,
    skip_weights,
    skip_bias,
):
    mesh_rows = lax.axis_size("px")
    mesh_columns = lax.axis_size("py")
    device_total = mesh_rows * mesh_columns
    capacity = max(2, 2 * point_channel_values.shape[0] // device_total)
    channels, points = point_channel_values.shape[1:]
    x_dev, y_dev = NX // mesh_rows, NY // mesh_columns
    bricks_y = y_dev // 4
    bricks_z = NZ // 16
    bricks_device = x_dev // 2 * bricks_y * bricks_z
    slot_total = device_total * capacity
    wanted, places, facts = make_plan(
        block_bricks, point_counts, bricks_device, bricks_y, bricks_z, capacity, slot_total, points
    )
    tiles, got_notes = route(wanted, point_offsets, facts, point_channel_values)
    lanes = x_dev * channels
    tiles_x, tiles_z = lanes // 128, NZ // 16
    lift = tiles_z * tiles_x
    bases = find_spots(got_notes, tiles_x, tiles_z)

    kz_dev = MODES // mesh_columns
    ky_dev = MODES // mesh_rows
    parts = 1
    while ky_dev * kz_dev * 2 // (2 * parts) % 16 == 0 and kz_dev % (2 * parts) == 0 and parts < MOST_PARTS:
        parts *= 2
    third_pair, third_back, second, second_back, first_forward, first_back = all_tables(
        mesh_columns, parts
    )
    me = lax.axis_index("py").astype(jnp.int32).reshape(1)
    grid, third_found = gather_grid(
        bases, me, tiles, third_pair, y_dev * NZ, lanes, mesh_columns, parts, lift, capacity
    )
    for layer in range(LAYERS):
        modes = spectral(
            layer, second, first_forward, first_back, third_found, spectral_weights, parts
        )
        found = layer_back(
            layer,
            me,
            second_back,
            third_back,
            third_pair,
            modes,
            grid,
            skip_weights,
            skip_bias,
        )
        grid, third_found = found[0], found[-1]
    grid = grid.reshape(-1, 16, 128)
    reply = decode(bases, grid, got_notes, slot_total, channels, lift)
    return unpack_slots(places, reply)


def solution(mesh):
    return jax.shard_map(
        per_device,
        mesh=mesh,
        in_specs=(
            P(("px", "py"), None, None),
            P(("px", "py"), None, None),
            P(("px", "py")),
            P(("px", "py"), None),
            P(None, None, "px", "py", None, None),
            P(),
            P(),
        ),
        out_specs=P(("px", "py"), None, None),
        check_vma=False,
    )
```

```python
import functools
import math

import jax
import jax.numpy as jnp
import ml_dtypes
import numpy as np
from jax import lax
from jax.experimental import pallas as pl
from jax.experimental.pallas import tpu as pltpu
from jax.sharding import PartitionSpec as P

MODES = 32
NX = 128
NY = 128
NZ = 128
LAYERS = 2

AMPLITUDE = 0.25
SPREAD = 4.5
DECODE_SCALE = 0.1
CHUNKS = 2
MOST_PARTS = 4
WAYS = 4
VMEM_LIMIT = 60 * 1024 * 1024
F32 = jnp.float32
BF16 = jnp.bfloat16


def wave_numbers(kept_modes):
    position = np.arange(kept_modes)
    return np.where(position < kept_modes // 2, position, position - kept_modes)


def forward_matrix(length, frequency):
    angles = 2.0 * math.pi / length * (np.arange(length)[:, None] * frequency[None, :] % length)
    cosine = np.cos(angles) / math.sqrt(length)
    sine_part = np.sin(angles) / math.sqrt(length)
    from_real = np.stack([cosine, -sine_part], axis=-1)
    from_imag = np.stack([sine_part, cosine], axis=-1)
    return np.stack([from_real, from_imag], axis=1)


def unit_angles(products, length):
    return 2.0 * math.pi / length * (products % length)


def repeat_lines(table, slabs, copies):
    rows, depth = table.shape
    span = rows // slabs
    same = np.eye(copies, dtype=bool)[None, :, None, :, None]
    wide = np.where(same, table.reshape(slabs, 1, span, 1, depth), 0.0)
    return wide.reshape(rows * copies, copies * depth)


def constant(table):
    return jnp.asarray(np.asarray(table).astype(ml_dtypes.bfloat16))


def third_tables(kinds, parts, me_y):
    kz_dev = MODES // kinds
    index = np.arange(2 * MODES)
    kz = index // 2 % kz_dev + kz_dev * (index // (2 * kz_dev) ^ me_y)
    angle = unit_angles(kz[:, None] * np.arange(NZ)[None, :], NZ)
    third = np.where((index % 2 == 0)[:, None], np.cos(angle), -np.sin(angle)) / math.sqrt(NZ)
    fold = np.where(kz == 0, 1.0, 2.0)[:, None]
    span = 2 * kz_dev // parts
    return (
        repeat_lines(third, kinds * parts, 2),
        repeat_lines(third * fold, kinds * parts, 16 // span).T,
    )


def second_table(kinds, parts, me_y):
    span = 2 * MODES // kinds // parts
    y_dev = NY // kinds
    row = np.arange(MODES * span)[:, None]
    column = np.arange(y_dev * span)[None, :]
    ky = wave_numbers(MODES)[row // span]
    angle = unit_angles(ky * (me_y * y_dev + column // span), NY)
    sine = np.where(row % 2 == 0, np.sin(angle), -np.sin(angle))
    second = np.where(row % 2 == column % 2, np.cos(angle), sine) / math.sqrt(NY)
    return np.where(row % span // 2 == column % span // 2, second, 0.0)


def all_tables(kinds, parts):
    third = [third_tables(kinds, parts, me_y) for me_y in range(kinds)]
    second = np.stack([second_table(kinds, parts, me_y) for me_y in range(kinds)])
    by_pair = forward_matrix(NX, wave_numbers(MODES)).reshape(NX // 2, 2, 2, MODES, 2)
    first_forward = by_pair.transpose(1, 3, 4, 2, 0).reshape(4 * MODES, NX)
    turned = np.stack([by_pair[..., 1], -by_pair[..., 0]], axis=-1)
    first_back = np.stack([by_pair, turned], axis=0).transpose(2, 0, 3, 1, 4, 5)
    return [
        constant(table)
        for table in (
            np.stack([one[0] for one in third]),
            np.stack([one[1] for one in third]),
            second,
            second.transpose(0, 2, 1),
            first_forward,
            first_back.reshape(4 * NX, 2 * MODES),
        )
    ]


def gelu(value):
    return 0.5 * value * (1.0 + lax.erf(value * math.sqrt(0.5)))


def block_values(offsets, shift_of, count, points):
    lanes = lax.broadcasted_iota(jnp.int32, (1, points), 1).astype(F32)
    amplitude = jnp.where(lanes < count, AMPLITUDE, 0.0).astype(F32)

    def part(dim, brick, cells, scale):
        center = lax.broadcasted_iota(jnp.int32, (cells, points), 0).astype(F32) + 0.5
        apart = (offsets[dim : dim + 1, :] - shift_of(dim, brick) * scale) - center
        return jnp.exp(apart * apart * (-1.0 / SPREAD))

    rows = []
    for brick in range(4):
        along_x = part(0, brick, 2, 2.0) * amplitude
        along_y = part(1, brick, 4, 4.0)
        along_z = part(2, brick, 16, 16.0)
        for cy in range(4):
            plane = along_z * along_y[cy : cy + 1, :]
            rows.append(
                jnp.concatenate(
                    [plane * along_x[0:1, :], plane * along_x[1:2, :]], axis=1
                ).astype(BF16)
            )
    return jnp.concatenate(rows, axis=0)


def note_values(notes, slot, points):
    facts = notes[4 * slot + 3 : 4 * slot + 4, :]
    return block_values(
        notes[4 * slot : 4 * slot + 3, :],
        lambda dim, brick: facts[:, 3 * brick + dim : 3 * brick + dim + 1]
        - facts[:, dim : dim + 1],
        facts[:, 12:13],
        points,
    )


def bits(size):
    return size.bit_length() - 1


def plan_body(bricks_y, bricks_z, capacity, brick_ref, count_ref, wanted_ref, place_ref, fact_ref):
    blocks = brick_ref.shape[0]
    slots = wanted_ref.shape[1]
    bricks_device = bricks_y[1]
    bricks_y = bricks_y[0]
    brick = brick_ref[...]
    down = lax.broadcasted_iota(jnp.int32, (blocks, blocks), 0)
    across = lax.broadcasted_iota(jnp.int32, (blocks, blocks), 1)
    owner_column = lax.shift_right_logical(brick[:, 0:1], jnp.int32(bits(bricks_device)))
    diagonal = down == across
    owner_row = jnp.sum(jnp.where(diagonal, owner_column, 0), axis=0, keepdims=True)
    same = owner_column == owner_row
    rank_row = jnp.sum(jnp.where(same & (down < across), 1, 0), axis=0, keepdims=True)
    rank_column = jnp.sum(jnp.where(same & (across < down), 1, 0), axis=1, keepdims=True)
    place_ref[...] = owner_row * capacity + rank_row
    slot = owner_column * capacity + rank_column
    slot_at = lax.broadcasted_iota(jnp.int32, (blocks, slots), 1)
    block_at = lax.broadcasted_iota(jnp.int32, (blocks, slots), 0) + 1
    wanted_ref[...] = jnp.sum(jnp.where(slot == slot_at, block_at, 0), axis=0, keepdims=True) - 1
    local = brick & (bricks_device - 1)
    parts = (
        lax.shift_right_logical(local, jnp.int32(bits(bricks_y * bricks_z))),
        lax.shift_right_logical(local, jnp.int32(bits(bricks_z))) & (bricks_y - 1),
        local & (bricks_z - 1),
    )
    count = jnp.sum(jnp.where(diagonal, count_ref[...], 0), axis=1, keepdims=True)
    lane = lax.broadcasted_iota(jnp.int32, (blocks, fact_ref.shape[2]), 1)
    facts = jnp.where(lane == 12, count, 0)
    for at in range(4):
        for dim in range(3):
            facts = jnp.where(lane == 3 * at + dim, parts[dim][:, at : at + 1], facts)
    fact_ref[...] = facts.astype(F32).reshape(fact_ref.shape)


def make_plan(bricks, counts, bricks_device, bricks_y, bricks_z, capacity, slots, points):
    blocks = bricks.shape[0]
    vmem = pl.BlockSpec(memory_space=pltpu.VMEM)
    return pl.pallas_call(
        functools.partial(plan_body, (bricks_y, bricks_device), bricks_z, capacity),
        in_specs=[vmem] * 2,
        out_specs=[vmem] * 3,
        out_shape=[
            jax.ShapeDtypeStruct((1, slots), jnp.int32),
            jax.ShapeDtypeStruct((1, blocks), jnp.int32),
            jax.ShapeDtypeStruct((blocks, 1, points), F32),
        ],
        name="make_plan",
    )(bricks, counts.reshape(1, blocks))


def spot_body(tiles_x, tiles_z, note_ref, base_ref, wide_ref):
    wide_ref[...] = note_ref[...].reshape(wide_ref.shape).astype(F32)
    facts = wide_ref[pl.ds(3, wide_ref.shape[0] // 4, stride=4), :].T
    rows = []
    for at in range(4):
        cell_x, cell_y, cell_z = (facts[3 * at + dim : 3 * at + dim + 1, :] for dim in range(3))
        rows.append((cell_y * (4 * tiles_z) + cell_z) * tiles_x + cell_x)
    base_ref[...] = jnp.concatenate(rows, axis=0).astype(jnp.int32)


def find_spots(notes, tiles_x, tiles_z):
    rows = notes.shape[0] * notes.shape[1]
    vmem = pl.BlockSpec(memory_space=pltpu.VMEM)
    return pl.pallas_call(
        functools.partial(spot_body, tiles_x, tiles_z),
        in_specs=[vmem],
        out_specs=vmem,
        out_shape=jax.ShapeDtypeStruct((4, rows // 4), jnp.int32),
        scratch_shapes=[pltpu.VMEM((rows, notes.shape[2]), F32)],
        name="find_spots",
    )(notes)


def near_at(index, devices):
    return (7 * index) % (devices // 2)


def far_at(index, devices):
    return devices // 2 + (7 * index + devices // 3) % (devices // 2)


def mask_at(turn, devices):
    index, far = turn // 2, turn % 2
    return far * far_at(index, devices) + (1 - far) * near_at(index, devices)


def crossed(value, mask, size):
    result, bit = 0, 1
    while bit < size:
        result = result + bit * ((value // bit + mask // bit) % 2)
        bit *= 2
    return result


def route_body(
    size_x,
    size_y,
    source_ref,
    offset_ref,
    fact_ref,
    feature_ref,
    tile_ref,
    got_note_ref,
    feature_send,
    feature_got,
    note_send,
    tile_held,
    feature_ssem,
    feature_rsem,
    note_ssem,
    note_rsem,
    tile_sem,
):
    slots, channels, points = feature_send.shape
    devices = size_x * size_y
    capacity = slots // devices
    ways = math.gcd(WAYS, capacity)
    note_rows = note_send.shape[1]
    me = lax.axis_index("px") * size_y + lax.axis_index("py")
    barrier = pltpu.get_barrier_semaphore()

    def greet(mask, carry):
        other = crossed(me, mask, devices)
        pl.semaphore_signal(
            barrier,
            inc=1,
            device_id={"px": other // size_y, "py": other % size_y},
            device_id_type=pl.DeviceIdType.MESH,
        )
        return carry

    lax.fori_loop(1, devices, greet, 0)

    def transfers(mask):
        other = crossed(me, mask, devices)
        there = {"px": other // size_y, "py": other % size_y}
        return (
            pltpu.make_async_remote_copy(
                src_ref=note_send.at[other],
                dst_ref=got_note_ref.at[me],
                send_sem=note_ssem.at[mask],
                recv_sem=note_rsem.at[mask],
                device_id=there,
                device_id_type=pl.DeviceIdType.MESH,
            ),
            pltpu.make_async_remote_copy(
                src_ref=feature_send.at[pl.ds(other * capacity, capacity)],
                dst_ref=feature_got.at[pl.ds(me * capacity, capacity)],
                send_sem=feature_ssem.at[mask],
                recv_sem=feature_rsem.at[mask],
                device_id=there,
                device_id_type=pl.DeviceIdType.MESH,
            ),
        )

    def pack(other, notes_to, features_to):
        notes = []
        for slot in range(capacity):
            source = source_ref[0, other * capacity + slot]
            present = source >= 0
            source = jnp.maximum(source, 0)
            feature = feature_ref[source]
            features_to[other * capacity + slot] = jnp.where(
                present, feature, jnp.zeros_like(feature)
            )
            note = jnp.concatenate([offset_ref[source].astype(F32), fact_ref[source]], axis=0)
            notes.append(jnp.where(present, note, 0.0))
        if note_rows > 4 * capacity:
            notes.append(jnp.zeros((note_rows - 4 * capacity, points), F32))
        notes_to[other] = jnp.concatenate(notes, axis=0).astype(BF16)

    first = mask_at(1, devices)
    pack(crossed(me, first, devices), note_send, feature_send)
    pl.semaphore_wait(barrier, devices - 1)
    for copy in transfers(first):
        copy.start()

    def launch(turn, carry):
        mask = mask_at(turn, devices)
        pack(crossed(me, mask, devices), note_send, feature_send)
        for copy in transfers(mask):
            copy.start()
        return carry

    lax.fori_loop(2, devices, launch, 0)
    pack(me, got_note_ref, feature_got)

    def tile_copy(turn, other):
        return pltpu.make_async_copy(
            tile_held.at[turn % 2],
            tile_ref.at[pl.ds(other * capacity, capacity)],
            tile_sem.at[turn % 2],
        )

    def work(turn, other):
        notes = got_note_ref[other].astype(F32)
        for start in range(0, capacity, ways):
            tiles = []
            for slot in range(start, start + ways):
                values = note_values(notes, slot, points)
                feature = feature_got[other * capacity + slot]
                empty = jnp.zeros_like(feature)
                pair = jnp.concatenate(
                    [
                        jnp.concatenate([feature, empty], axis=1),
                        jnp.concatenate([empty, feature], axis=1),
                    ],
                    axis=0,
                )
                tiles.append(
                    lax.dot_general(
                        values, pair, (((1,), (1,)), ((), ())), preferred_element_type=F32
                    ).astype(BF16)
                )
            for way in range(ways):
                tile_held[turn % 2, start + way] = tiles[way]
        tile_copy(turn, other).start()

    work(0, me)

    def step(mask_of, turn, carry):
        mask = mask_of(turn % (devices // 2), devices)
        for copy in transfers(mask):
            copy.wait_recv()

        @pl.when(turn >= 2)
        def _():
            tile_copy(turn, me).wait()

        work(turn, crossed(me, mask, devices))
        return carry

    lax.fori_loop(1, devices // 2, functools.partial(step, near_at), 0)
    lax.fori_loop(devices // 2, devices, functools.partial(step, far_at), 0)
    for turn in range(devices - 2, devices):
        tile_copy(turn, me).wait()

    def leave(mask, carry):
        for copy in transfers(mask):
            copy.wait_send()
        return carry

    lax.fori_loop(1, devices, leave, 0)


def route(sources, offsets, facts, features):
    slots = sources.shape[1]
    channels, points = features.shape[1:]
    size_x, size_y = lax.axis_size("px"), lax.axis_size("py")
    devices = size_x * size_y
    capacity = slots // devices
    note_rows = (4 * capacity + 15) // 16 * 16
    vmem = pl.BlockSpec(memory_space=pltpu.VMEM)
    dma = pltpu.SemaphoreType.DMA
    return pl.pallas_call(
        functools.partial(route_body, size_x, size_y),
        in_specs=[pl.BlockSpec(memory_space=pltpu.SMEM), vmem, vmem, vmem],
        out_specs=[pl.BlockSpec(memory_space=pl.ANY), vmem],
        out_shape=[
            jax.ShapeDtypeStruct((slots, 256, 2 * channels), BF16),
            jax.ShapeDtypeStruct((devices, note_rows, points), BF16),
        ],
        scratch_shapes=[
            pltpu.VMEM((slots, channels, points), BF16),
            pltpu.VMEM((slots, channels, points), BF16),
            pltpu.VMEM((devices, note_rows, points), BF16),
            pltpu.VMEM((2, capacity, 256, 2 * channels), BF16),
            dma((devices,)),
            dma((devices,)),
            dma((devices,)),
            dma((devices,)),
            dma((2,)),
        ],
        compiler_params=pltpu.CompilerParams(
            vmem_limit_bytes=VMEM_LIMIT, collective_id=LAYERS + 1, has_side_effects=True
        ),
        name="route",
    )(sources, offsets, facts, features)


def find_third(third_ref, lines_of, out_ref, columns):
    kinds, parts, lines = out_ref.shape[:3]
    both = third_ref.shape[0]
    span = both // (2 * kinds * parts)
    turns = 16 // (2 * span)

    def some(turn, carry):
        found = [
            jnp.dot(third_ref[...], lines_of(turn * turns + way), preferred_element_type=F32)
            for way in range(turns)
        ]
        row = pl.multiple_of(turn * 16, 16)
        for slab in range(kinds * parts):
            piece = [one[slab * 2 * span : (slab + 1) * 2 * span, :] for one in found]
            piece = piece[0] if turns == 1 else jnp.concatenate(piece, axis=0)
            out_ref[slab // parts, slab % parts, pl.ds(row, 16), columns] = piece.astype(BF16)
        return carry

    lax.fori_loop(0, lines // 16, some, 0, unroll=True)


def gather_body(
    group, steps, lift, capacity, base_ref, me_ref, tile_ref, third_ref, out_ref, modes_ref, total_ref
):
    step = pl.program_id(0)
    lanes = out_ref.shape[1]
    depth = third_ref.shape[2] // 2
    tiles = lanes // 128

    @pl.when(step == 0)
    def _():
        total_ref[...] = jnp.zeros_like(total_ref)

    def some(turn, carry):
        for way in range(WAYS):
            member = turn * WAYS + way
            slot = step * group + member
            room = base_ref.shape[1] * capacity // (steps * group)
            spot = slot if room == capacity else slot // capacity * room + slot % capacity
            bases = [base_ref[brick, spot] for brick in range(4)]
            places = [base + cy * lift for base in bases for cy in range(4)]
            sums = [
                total_ref[place] + tile_ref[member, 16 * at : 16 * at + 16, :].astype(F32)
                for at, place in enumerate(places)
            ]
            for place, value in zip(places, sums):
                total_ref[place] = value
        return carry

    lax.fori_loop(0, group // WAYS, some, 0, unroll=4)

    @pl.when(step == steps - 1)
    def _():
        width = math.gcd(lanes, 256)
        pieces = width // 128

        def tile(turn, carry):
            columns = pl.ds(pl.multiple_of(turn * width, width), width)

            def lines_of(pair):
                place = pl.ds(pl.multiple_of(pair * 2 * depth, 2 * depth), 2 * depth)
                rows = []
                for at in range(2 * depth // 16):
                    here = (pair * (2 * depth // 16) + at) * tiles + turn * pieces
                    rows.append(
                        jnp.concatenate([total_ref[here + to] for to in range(pieces)], axis=1)
                    )
                value = jnp.concatenate(rows, axis=0).astype(BF16)
                out_ref[place, columns] = value
                return value

            find_third(third_ref.at[0], lines_of, modes_ref, columns)
            return carry

        lax.fori_loop(0, lanes // width, tile, 0)


def gather_grid(bases, me, tiles, third_pair, rows, lanes, kinds, parts, lift, capacity):
    slots = tiles.shape[0]
    group = math.gcd(slots, 32)
    depth = third_pair.shape[2] // 2
    lines = rows // depth * third_pair.shape[1] // (2 * kinds * parts)
    return pl.pallas_call(
        functools.partial(gather_body, group, slots // group, lift, capacity),
        grid_spec=pltpu.PrefetchScalarGridSpec(
            num_scalar_prefetch=2,
            grid=(slots // group,),
            in_specs=[
                pl.BlockSpec((group,) + tiles.shape[1:], lambda i, base, me: (i, 0, 0)),
                pl.BlockSpec((1,) + third_pair.shape[1:], lambda i, base, me: (me[0], 0, 0)),
            ],
            out_specs=[
                pl.BlockSpec((rows, lanes), lambda i, base, me: (0, 0)),
                pl.BlockSpec((kinds, parts, lines, lanes), lambda i, base, me: (0, 0, 0, 0)),
            ],
            scratch_shapes=[pltpu.VMEM((rows * lanes // 2048, 16, 128), F32)],
        ),
        out_shape=[
            jax.ShapeDtypeStruct((rows, lanes), BF16),
            jax.ShapeDtypeStruct((kinds, parts, lines, lanes), BF16),
        ],
        compiler_params=pltpu.CompilerParams(vmem_limit_bytes=46 * 1024 * 1024),
        name="gather_grid",
    )(bases, me, tiles, third_pair)


def decode_body(size_x, size_y, lift, base_ref, held_ref, note_ref, got_ref, reply_ref, ssem, rsem, own_sem):
    slots, channels, points = got_ref.shape
    devices = size_x * size_y
    capacity = slots // devices
    ways = math.gcd(WAYS, capacity)
    me_x, me_y = lax.axis_index("px"), lax.axis_index("py")
    me = me_x * size_y + me_y
    barrier = pltpu.get_barrier_semaphore()

    def greet(mask, carry):
        other = crossed(me, mask, devices)
        pl.semaphore_signal(
            barrier,
            inc=1,
            device_id={"px": other // size_y, "py": other % size_y},
            device_id_type=pl.DeviceIdType.MESH,
        )
        return carry

    lax.fori_loop(1, devices, greet, 0)

    def transfer(mask):
        other = crossed(me, mask, devices)
        return pltpu.make_async_remote_copy(
            src_ref=reply_ref.at[pl.ds(other * capacity, capacity)],
            dst_ref=got_ref.at[pl.ds(me * capacity, capacity)],
            send_sem=ssem.at[mask],
            recv_sem=rsem.at[mask],
            device_id={"px": other // size_y, "py": other % size_y},
            device_id_type=pl.DeviceIdType.MESH,
        )

    room = base_ref.shape[1] // devices

    def fill(other):
        notes = note_ref[other].astype(F32)
        for start in range(0, capacity, ways):
            results = []
            for slot in range(start, start + ways):
                values = note_values(notes, slot, points)
                bases = [base_ref[brick, other * room + slot] for brick in range(4)]
                cells = jnp.concatenate(
                    [held_ref[base + cy * lift] for base in bases for cy in range(4)], axis=0
                )
                both = lax.dot_general(
                    cells, values, (((0,), (0,)), ((), ())), preferred_element_type=F32
                )
                summed = both[:channels, :points] + both[channels:, points:]
                results.append((DECODE_SCALE * summed).astype(BF16))
            for way in range(ways):
                reply_ref[other * capacity + start + way] = results[way]

    first = mask_at(1, devices)
    fill(crossed(me, first, devices))
    pl.semaphore_wait(barrier, devices - 1)
    transfer(first).start()

    def step(turn, carry):
        mask = mask_at(turn, devices)
        fill(crossed(me, mask, devices))
        transfer(mask).start()
        return carry

    lax.fori_loop(2, devices, step, 0)
    fill(me)
    mine = pl.ds(me * capacity, capacity)
    own = pltpu.make_async_copy(reply_ref.at[mine], got_ref.at[mine], own_sem)
    own.start()
    own.wait()

    def finish(mask, carry):
        transfer(mask).wait_recv()
        return carry

    lax.fori_loop(1, devices, finish, 0)

    def leave(mask, carry):
        transfer(mask).wait_send()
        return carry

    lax.fori_loop(1, devices, leave, 0)


def decode(bases, grid, notes, slots, channels, lift):
    points = notes.shape[2]
    size_x, size_y = lax.axis_size("px"), lax.axis_size("py")
    devices = size_x * size_y
    vmem = pl.BlockSpec(memory_space=pltpu.VMEM)
    return pl.pallas_call(
        functools.partial(decode_body, size_x, size_y, lift),
        in_specs=[pl.BlockSpec(memory_space=pltpu.SMEM), vmem, vmem],
        out_specs=vmem,
        out_shape=jax.ShapeDtypeStruct((slots, channels, points), BF16),
        scratch_shapes=[
            pltpu.VMEM((slots, channels, points), BF16),
            pltpu.SemaphoreType.DMA((devices,)),
            pltpu.SemaphoreType.DMA((devices,)),
            pltpu.SemaphoreType.DMA,
        ],
        compiler_params=pltpu.CompilerParams(
            vmem_limit_bytes=24 * 1024 * 1024, collective_id=LAYERS, has_side_effects=True
        ),
        name="decode",
    )(bases, grid, notes)


def partner(me, distance):
    return me + distance - 2 * distance * ((me // distance) % 2)


def spectral_body(
    layer,
    second_ref,
    forward_ref,
    backward_ref,
    third_ref,
    weight_ref,
    modes_ref,
    held_ref,
    sums_send,
    sums_recv,
    lines_send,
    lines_recv,
    back_send,
    weight_held,
    wide_in,
    wide_out,
    sums_ssem,
    sums_rsem,
    lines_ssem,
    lines_rsem,
    back_ssem,
    back_rsem,
    modes_ssem,
    modes_rsem,
    weight_sem,
):
    kinds, parts, rows, lanes = modes_ref.shape
    devices_x, slab_rows = lines_send.shape[1:3]
    pairs_x = lanes // 128
    channels = weight_held.shape[4]
    kz_part = weight_held.shape[3]
    kx_all = weight_held.shape[1]
    me_x, me_y = lax.axis_index("px"), lax.axis_index("py")
    steps = kinds.bit_length() - 1
    tile = math.gcd(lanes, 256)
    lane_tiles = lanes // tile
    batch = 8
    weight_copies = []
    for part in range(parts):
        copy = pltpu.make_async_copy(
            weight_ref.at[layer, :, :, pl.ds(part * kz_part, kz_part)],
            weight_held.at[part],
            weight_sem.at[part],
        )
        copy.start()
        weight_copies.append(copy)

    def at_x(device):
        return {"px": device}

    def at_y(distance):
        return {"py": partner(me_y, distance)}

    barrier = pltpu.get_barrier_semaphore()
    for hop in range(1, devices_x):
        pl.semaphore_signal(
            barrier,
            inc=1,
            device_id=at_x((me_x + hop) % devices_x),
            device_id_type=pl.DeviceIdType.MESH,
        )
    for step in range(steps):
        pl.semaphore_signal(
            barrier, inc=1, device_id=at_y(1 << step), device_id_type=pl.DeviceIdType.MESH
        )

    started = []

    def send(source, target, ssem, rsem, device):
        copy = pltpu.make_async_remote_copy(
            src_ref=source,
            dst_ref=target,
            send_sem=ssem,
            recv_sem=rsem,
            device_id=device,
            device_id_type=pl.DeviceIdType.MESH,
        )
        copy.start()
        started.append(copy)
        return copy

    bases = [kinds - (kinds >> step) for step in range(steps)]
    sums_copies, lines_copies, back_copies, modes_copies = {}, {}, {}, {}

    def send_sums(part, step):
        count = kinds >> (step + 1)
        at = pl.ds(bases[step], count)
        sums_copies[part, step] = send(
            sums_send.at[part, at],
            sums_recv.at[part, at],
            sums_ssem.at[part, step],
            sums_rsem.at[part, step],
            at_y(1 << step),
        )

    def second_stage(part):
        def one(turn, carry):
            columns = pl.ds(pl.multiple_of(turn * tile, tile), tile)
            for kind in range(kinds - 1, -1, -1):
                value = jnp.dot(
                    second_ref[me_y], third_ref[kind, part, :, columns], preferred_element_type=F32
                )
                if kind % 2:
                    sums_send[part, kind // 2, :, columns] = value.astype(BF16)
                else:
                    held_ref[part, kind // 2, :, columns] = value
            return carry

        lax.fori_loop(0, lane_tiles, one, 0)
        send_sums(part, 0)

    def sum_stage(part, step):
        sums_copies[part, step].wait_recv()

        def one(turn, carry):
            columns = pl.ds(pl.multiple_of(turn * tile, tile), tile)
            for index in range(kinds >> (step + 1)):
                kind = index << (step + 1)
                value = held_ref[part, kind // 2, :, columns] + sums_recv[
                    part, bases[step] + index, :, columns
                ].astype(F32)
                if index % 2:
                    sums_send[part, bases[step + 1] + index // 2, :, columns] = value.astype(BF16)
                elif step + 1 < steps:
                    held_ref[part, kind // 2, :, columns] = value
                else:
                    lines_send[part, :, :, columns] = value.astype(BF16).reshape(
                        devices_x, slab_rows, tile
                    )
            return carry

        lax.fori_loop(0, lane_tiles, one, 0)
        if step + 1 < steps:
            send_sums(part, step + 1)
            return
        for hop in range(1, devices_x):
            target = (me_x + hop) % devices_x
            lines_copies[part, hop] = send(
                lines_send.at[part, target],
                lines_recv.at[part, me_x],
                lines_ssem.at[part, hop],
                lines_rsem.at[part, hop],
                at_x(target),
            )
        lines_recv[part, me_x] = lines_send[part, me_x]

    half_lane = lax.broadcasted_iota(jnp.int32, (1, 128), 1) < channels

    def mix_stage(part):
        for hop in range(1, devices_x):
            lines_copies[part, hop].wait_recv()
        weight_copies[part].wait()

        def widen(source, carry):
            for pair in range(pairs_x):
                row = pl.multiple_of((source * pairs_x + pair) * slab_rows, slab_rows)
                wide_in[pl.ds(row, slab_rows), :] = lines_recv[
                    part, source, :, pair * 128 : (pair + 1) * 128
                ].astype(F32)
            return carry

        lax.fori_loop(0, devices_x, widen, 0)
        count = devices_x * pairs_x
        modes_rows = 2 * kx_all
        row_at = lax.broadcasted_iota(jnp.int32, (modes_rows, batch * channels), 0)
        lane_at = lax.broadcasted_iota(jnp.int32, (modes_rows, batch * channels), 1)
        own = (row_at // 2) % batch == lane_at // channels

        def one(pick, carry):
            ky, kz = pick // kz_part, pick % kz_part
            line = jnp.concatenate(
                [
                    wide_in[pl.ds(2 * pick, count, stride=slab_rows), :],
                    wide_in[pl.ds(2 * pick + 1, count, stride=slab_rows), :],
                ],
                axis=0,
            ).astype(BF16)
            first = jnp.dot(forward_ref[...], line, preferred_element_type=F32)
            first = jnp.where(half_lane, first[:modes_rows], first[modes_rows:])
            first = first + pltpu.roll(first, channels, 1)
            spread = jnp.where(own, jnp.concatenate([first] * (batch // 2), axis=1), 0.0)
            spread = spread.astype(BF16)
            mixed = []
            for at in range(kx_all // batch):
                weight = weight_held[part, at * batch : (at + 1) * batch, ky, kz]
                mixed.append(
                    jnp.dot(
                        spread[2 * at * batch : 2 * (at + 1) * batch],
                        weight.reshape(batch * channels, 2 * channels),
                        preferred_element_type=F32,
                    )
                )
            mixed = jnp.concatenate(mixed, axis=0).astype(BF16)
            back = jnp.dot(backward_ref[...], mixed, preferred_element_type=F32)
            size = 2 * count
            part_at = [back[at * size : (at + 1) * size] for at in range(4)]
            final = jnp.where(half_lane, part_at[0], part_at[3]) + pltpu.roll(
                jnp.where(half_lane, part_at[2], part_at[1]), channels, 1
            )
            wide_out[pl.ds(2 * pick, count, stride=slab_rows), :] = final[:count]
            wide_out[pl.ds(2 * pick + 1, count, stride=slab_rows), :] = final[count:]
            return carry

        lax.fori_loop(0, slab_rows // 2, one, 0, unroll=4)

        def narrow(target, carry):
            for pair in range(pairs_x):
                row = pl.multiple_of((target * pairs_x + pair) * slab_rows, slab_rows)
                back_send[part, target, :, pair * 128 : (pair + 1) * 128] = wide_out[
                    pl.ds(row, slab_rows), :
                ].astype(BF16)
            return carry

        lax.fori_loop(0, devices_x, narrow, 0)
        mine = pl.ds(pl.multiple_of(me_x * slab_rows, slab_rows), slab_rows)
        for hop in range(1, devices_x):
            target = (me_x + hop) % devices_x
            back_copies[part, hop] = send(
                back_send.at[part, target],
                modes_ref.at[0, part, mine],
                back_ssem.at[part, hop],
                back_rsem.at[part, hop],
                at_x(target),
            )
        modes_ref[0, part, mine, :] = back_send[part, me_x]

    def spread_stage(part, kind):
        if kind == 0:
            for hop in range(1, devices_x):
                back_copies[part, hop].wait_recv()
            limit = kinds
        else:
            modes_copies[part, kind].wait_recv()
            limit = kind & -kind
        distance = limit // 2
        while distance >= 1:
            modes_copies[part, kind + distance] = send(
                modes_ref.at[kind, part],
                modes_ref.at[kind + distance, part],
                modes_ssem.at[part, kind + distance],
                modes_rsem.at[part, kind + distance],
                at_y(distance),
            )
            distance //= 2

    order = []
    for part in range(parts):
        order.append((1.5 * part, second_stage, (part,)))
        for step in range(steps):
            order.append((1.5 * part + 6.0 if step == 0 else 12.0 * step + 5.0 * part, sum_stage, (part, step)))
        base = 12.0 * (steps - 1) + 5.0 * part
        order.append((base + 7.1, mix_stage, (part,)))
        order.append((base + 13.0, spread_stage, (part, 0)))
        level = kinds // 2
        while level >= 1:
            for kind in range(level, kinds, 2 * level):
                late = 6.0 * (kinds // level).bit_length()
                order.append((base + 13.1 + late, spread_stage, (part, kind)))
            level //= 2
    order.sort(key=lambda entry: entry[0])
    waited = False
    for _, stage, given in order:
        stage_first = stage is second_stage and given == (0,)
        if stage_first and not waited:
            pl.semaphore_wait(barrier, devices_x - 1 + steps)
            waited = True
        stage(*given)
    for copy in started:
        copy.wait_send()


def spectral(layer, second, first_forward, first_back, third, weights, parts):
    kinds, _, lines, lanes = third.shape
    rows = second.shape[1]
    devices_x = lax.axis_size("px")
    slab_rows = rows // devices_x
    _, kx_all, ky_dev, kz_dev, channels, wide = weights.shape
    steps = kinds.bit_length() - 1
    count = devices_x * lanes // 128 * slab_rows
    dma = pltpu.SemaphoreType.DMA
    return pl.pallas_call(
        functools.partial(spectral_body, layer),
        in_specs=[pl.BlockSpec(memory_space=pltpu.VMEM)] * 4 + [pl.BlockSpec(memory_space=pl.ANY)],
        out_specs=pl.BlockSpec(memory_space=pltpu.VMEM),
        out_shape=jax.ShapeDtypeStruct((kinds, parts, rows, lanes), BF16),
        scratch_shapes=[
            pltpu.VMEM((parts, kinds // 2, rows, lanes), F32),
            pltpu.VMEM((parts, kinds - 1, rows, lanes), BF16),
            pltpu.VMEM((parts, kinds - 1, rows, lanes), BF16),
            pltpu.VMEM((parts, devices_x, slab_rows, lanes), BF16),
            pltpu.VMEM((parts, devices_x, slab_rows, lanes), BF16),
            pltpu.VMEM((parts, devices_x, slab_rows, lanes), BF16),
            pltpu.VMEM((parts, kx_all, ky_dev, kz_dev // parts, channels, wide), BF16),
            pltpu.VMEM((count, 128), F32),
            pltpu.VMEM((count, 128), F32),
            dma((parts, steps)),
            dma((parts, steps)),
            dma((parts, devices_x)),
            dma((parts, devices_x)),
            dma((parts, devices_x)),
            dma((parts, devices_x)),
            dma((parts, kinds)),
            dma((parts, kinds)),
            dma((parts,)),
        ],
        compiler_params=pltpu.CompilerParams(
            vmem_limit_bytes=35 * 1024 * 1024, collective_id=layer, has_side_effects=True
        ),
        name="spectral",
    )(second, first_forward, first_back, third, weights)


def layer_body(
    layer,
    me_ref,
    second_ref,
    third_ref,
    pair_ref,
    modes_ref,
    grid_ref,
    skip_ref,
    bias_ref,
    out_ref,
    *refs,
):
    held_ref, wide_ref = refs[-2:]
    tiled = len(out_ref.shape) == 4
    kinds, parts = modes_ref.shape[:2]
    slabs = kinds * parts
    lines = second_ref.shape[1]
    block = third_ref.shape[1]
    copies = wide_ref.shape[0] // skip_ref.shape[1]
    bias = jnp.concatenate([bias_ref[layer : layer + 1, :]] * copies, axis=1)

    @pl.when(pl.program_id(0) == 0)
    def _():
        skip = jnp.concatenate([skip_ref[layer].astype(F32)] * copies, axis=1)
        skip = jnp.concatenate([skip] * copies, axis=0)
        at_row = lax.broadcasted_iota(jnp.int32, wide_ref.shape, 0) // skip_ref.shape[1]
        at_lane = lax.broadcasted_iota(jnp.int32, wide_ref.shape, 1) // skip_ref.shape[1]
        wide_ref[...] = jnp.where(at_row == at_lane, skip, 0.0).astype(BF16)

    for slab in range(slabs):
        held_ref[slab] = jnp.dot(
            second_ref[0],
            modes_ref[slab // parts, slab % parts],
            preferred_element_type=F32,
        ).astype(BF16)

    def some(turn, carry):
        row = pl.ds(pl.multiple_of(turn * 16, 16), 16)
        line = jnp.concatenate([held_ref[slab, row, :] for slab in range(slabs)], axis=0)
        for way in range(block // 128):
            place = pl.ds(pl.multiple_of(turn * block + way * 128, 128), 128)
            spectral_part = jnp.dot(
                third_ref[0, way * 128 : (way + 1) * 128, :], line, preferred_element_type=F32
            )
            skipped = jnp.dot(grid_ref[place, :], wide_ref[...], preferred_element_type=F32)
            value = gelu(spectral_part + skipped + bias).astype(BF16)
            if tiled:
                row_tiles = pl.ds(turn * (block // 16) + way * 8, 8)
                for at in range(out_ref.shape[1]):
                    piece = value[:, at * 128 : (at + 1) * 128]
                    out_ref[row_tiles, at] = piece.reshape(8, 16, 128)
            else:
                out_ref[place, :] = value
        return carry

    lax.fori_loop(0, lines // 16, some, 0, unroll=True)
    if not tiled:
        pair = pair_ref.shape[2]

        def lines_of(at):
            return out_ref[pl.ds(pl.multiple_of(at * pair, pair), pair), :]

        find_third(pair_ref.at[0], lines_of, refs[0], slice(None))


def layer_back(layer, me, second, third, third_pair, modes, grid, skips, biases):
    rows, lanes = grid.shape
    kinds, parts, mode_rows = modes.shape[:3]
    width = math.gcd(lanes, 4 * skips.shape[1])
    lines = second.shape[1]

    def mine(table):
        return pl.BlockSpec((1,) + table.shape[1:], lambda i, me: (me[0], 0, 0))

    if layer == LAYERS - 1:
        out_specs = [
            pl.BlockSpec((rows // 16, width // 128, 16, 128), lambda i, me: (0, i, 0, 0)),
        ]
        out_shape = [jax.ShapeDtypeStruct((rows // 16, lanes // 128, 16, 128), BF16)]
    else:
        out_specs = [
            pl.BlockSpec((rows, width), lambda i, me: (0, i)),
            pl.BlockSpec((kinds, parts, lines, width), lambda i, me: (0, 0, 0, i)),
        ]
        out_shape = [
            jax.ShapeDtypeStruct((rows, lanes), BF16),
            jax.ShapeDtypeStruct((kinds, parts, lines, lanes), BF16),
        ]
    return pl.pallas_call(
        functools.partial(layer_body, layer),
        grid_spec=pltpu.PrefetchScalarGridSpec(
            num_scalar_prefetch=1,
            grid=(lanes // width,),
            in_specs=[
                mine(second),
                mine(third),
                mine(third_pair),
                pl.BlockSpec((kinds, parts, mode_rows, width), lambda i, me: (0, 0, 0, i)),
                pl.BlockSpec((rows, width), lambda i, me: (0, i)),
                pl.BlockSpec(skips.shape, lambda i, me: (0, 0, 0)),
                pl.BlockSpec(biases.shape, lambda i, me: (0, 0)),
            ],
            out_specs=out_specs,
            scratch_shapes=[
                pltpu.VMEM((kinds * parts, lines, width), BF16),
                pltpu.VMEM((width, width), BF16),
            ],
        ),
        out_shape=out_shape,
        compiler_params=pltpu.CompilerParams(vmem_limit_bytes=32 * 1024 * 1024),
        name="layer_back",
    )(me, second, third, third_pair, modes, grid, skips, biases)


def unpack_body(places_ref, reply_ref, out_ref):
    def some(turn, carry):
        for way in range(WAYS):
            block = turn * WAYS + way
            out_ref[block] = reply_ref[places_ref[0, block]]
        return carry

    lax.fori_loop(0, out_ref.shape[0] // WAYS, some, 0)


def unpack_slots(places, reply):
    vmem = pl.BlockSpec(memory_space=pltpu.VMEM)
    return pl.pallas_call(
        unpack_body,
        grid_spec=pltpu.PrefetchScalarGridSpec(
            num_scalar_prefetch=1, grid=(1,), in_specs=[vmem], out_specs=vmem
        ),
        out_shape=jax.ShapeDtypeStruct(places.shape[1:] + reply.shape[1:], reply.dtype),
        compiler_params=pltpu.CompilerParams(vmem_limit_bytes=40 * 1024 * 1024),
        name="unpack_slots",
    )(places, reply)


def per_device(
    point_channel_values,
    point_offsets,
    point_counts,
    block_bricks,
    spectral_weights,
    skip_weights,
    skip_bias,
):
    mesh_rows = lax.axis_size("px")
    mesh_columns = lax.axis_size("py")
    device_total = mesh_rows * mesh_columns
    capacity = max(2, 2 * point_channel_values.shape[0] // device_total)
    channels, points = point_channel_values.shape[1:]
    x_dev, y_dev = NX // mesh_rows, NY // mesh_columns
    bricks_y = y_dev // 4
    bricks_z = NZ // 16
    bricks_device = x_dev // 2 * bricks_y * bricks_z
    slot_total = device_total * capacity
    wanted, places, facts = make_plan(
        block_bricks, point_counts, bricks_device, bricks_y, bricks_z, capacity, slot_total, points
    )
    tiles, got_notes = route(wanted, point_offsets, facts, point_channel_values)
    lanes = x_dev * channels
    tiles_x, tiles_z = lanes // 128, NZ // 16
    lift = tiles_z * tiles_x
    bases = find_spots(got_notes, tiles_x, tiles_z)

    kz_dev = MODES // mesh_columns
    ky_dev = MODES // mesh_rows
    parts = 1
    while ky_dev * kz_dev * 2 // (2 * parts) % 16 == 0 and kz_dev % (2 * parts) == 0 and parts < MOST_PARTS:
        parts *= 2
    third_pair, third_back, second, second_back, first_forward, first_back = all_tables(
        mesh_columns, parts
    )
    me = lax.axis_index("py").astype(jnp.int32).reshape(1)
    grid, third_found = gather_grid(
        bases, me, tiles, third_pair, y_dev * NZ, lanes, mesh_columns, parts, lift, capacity
    )
    for layer in range(LAYERS):
        modes = spectral(
            layer, second, first_forward, first_back, third_found, spectral_weights, parts
        )
        found = layer_back(
            layer,
            me,
            second_back,
            third_back,
            third_pair,
            modes,
            grid,
            skip_weights,
            skip_bias,
        )
        grid, third_found = found[0], found[-1]
    grid = grid.reshape(-1, 16, 128)
    reply = decode(bases, grid, got_notes, slot_total, channels, lift)
    return unpack_slots(places, reply)


def solution(mesh):
    return jax.shard_map(
        per_device,
        mesh=mesh,
        in_specs=(
            P(("px", "py"), None, None),
            P(("px", "py"), None, None),
            P(("px", "py")),
            P(("px", "py"), None),
            P(None, None, "px", "py", None, None),
            P(),
            P(),
        ),
        out_specs=P(("px", "py"), None, None),
        check_vma=False,
    )
```
